32 devices in a mesh: tile: 8 (over z, x), row: 4 (over y, core).
Axes of the slice: x: 2, y: 2, z: 4, core: 2. Of those that a mesh axis runs over, the one named last changes fastest.
Arguments:
- point_feats: bfloat16 [11, 262144], P(None, ('tile', 'row')), may hold values from -6 to 6
- point_tile: int32 [262144, 1], P(('tile', 'row')), may hold values from 0 to 7; in each aligned block of 8192 rows (0 to 8191, 8192 to 16383, ...) at most 2048 rows name the same one
- point_cell: int32 [262144], P(('tile', 'row')), may hold values from 0 to 4607
- point_valid: int32 [262144], P(('tile', 'row')), may hold values 0 or 1
- pillar_frame: int32 [192, 768], P('tile', 'row'), may hold values from 0 to 2
- cotangent: bfloat16 [192, 768, 128], P('tile', 'row'), may hold values from -6 to 6
- params: float32 [273792], replicated, as said below
- first_moment: float32 [273792], replicated, as said below
- second_moment: float32 [273792], replicated, as said below
Outputs:
- grad_norm: float32 [], replicated
- new_params: float32 [273792], replicated
- new_first_moment: float32 [273792], replicated
- new_second_moment: float32 [273792], replicated
- params_bf16: bfloat16 [273792], replicated
- sublayer_rms: float32 [6], replicated
The draws below stay inside these ranges and needn't reach their ends.
Inputs may be any that keep to these rules, and one draw needn't show every extreme that they name: `point_tile`: in the 8192 rows of one device no tile is named by more than 2048 rows, a bound that some block reaches. `params`: matrices of order one over the square root of their fan-in, norm gains near 1, other vectors of order a few tenths. `first_moment`: entries of both signs. `second_moment`: every entry is positive.
All inputs are finite; a program needn't handle non-finite values. No bound on the sum of `point_valid` on one device may be relied on, other than what follows from the above.
Results may differ from the reference program's by a relative error of at most 0.0075.
The reference program's roundings to bfloat16 on the way count: a program that leaves them out, or rounds other values in their place, can miss the bound.
Values may be sent and summed in bfloat16 or wider, within the bound.
No kernel may reach another device: no remote copies, remote signals or barrier semaphores. Data moves between devices by JAX's collectives and lax.ppermute only.
A program may use at most 320 MiB of HBM per device.

```python
import math
import jax
import jax.numpy as jnp
import numpy as np
from jax import lax

D = 128
HEADS = 8
HD = 16
FF = 256
H1 = 64
WIN = 12
C_IN = 11
FRAMES = 3
LAYERS = 2
TX = 24
TY = 192
P_DEV = 8192
NXG = 192
NYG = 768
CELLS = 4608
CAP = 2048
POINTS = 262144
NPARAM = 273792
N_TILE = 8
N_ROW = 4


clip_norm = 0.01


beta_one = 0.9


beta_two = 0.999


def layout_drawn():
    entries = [('point_in_weight', (C_IN, H1)), ('point_in_bias', (H1,)), ('point_out_weight', (H1, D)), ('point_out_bias', (D,))]
    for layer_idx in range(LAYERS):
        entries = entries + [('qkv_weight', (D, 3 * D)), ('out_weight', (D, D)), ('ffn_in_weight', (D, FF)), ('ffn_out_weight', (FF, D)), ('query_bias', (D,)), ('value_bias', (D,)), ('out_bias', (D,)), ('norm1_gain', (D,)), ('norm1_bias', (D,)), ('ffn_in_bias', (FF,)), ('ffn_out_bias', (D,)), ('norm2_gain', (D,)), ('norm2_bias', (D,))]
    return entries


def entry_law(entry_name, extents):
    if entry_name in ('norm1_gain', 'norm2_gain'):
        return (1.0, 0.2)
    if len(extents) == 1:
        return (0.0, 0.4)
    factors = {'point_in_weight': 1.0, 'point_out_weight': 2.5, 'qkv_weight': 1.2, 'out_weight': 4.0, 'ffn_in_weight': 1.0, 'ffn_out_weight': 1.5}
    return (0.0, factors[entry_name] / math.sqrt(extents[0]))


def grad_guess(extents):
    scale_base = clip_norm / math.sqrt(NPARAM)
    if len(extents) == 1:
        return 4.0 * scale_base
    return scale_base


def draw_params(key, part):
    pieces = []
    for position, entry in enumerate(layout_drawn()):
        center, spread = entry_law(entry[0], entry[1])
        sub_key = jax.random.fold_in(key, 100 + position)
        unit_draw = jax.random.truncated_normal(sub_key, -3.0, 3.0, entry[1], jnp.float32)
        pieces.append((center + spread * unit_draw).reshape(-1))
    return jnp.concatenate(pieces)


def draw_first_moment(key, part):
    pieces = []
    for position, entry in enumerate(layout_drawn()):
        sub_key = jax.random.fold_in(key, 300 + position)
        unit_draw = jax.random.uniform(sub_key, entry[1], jnp.float32, -1.5, 1.5)
        pieces.append(((1.0 - beta_one) / beta_one * grad_guess(entry[1]) * unit_draw).reshape(-1))
    return jnp.concatenate(pieces)


def draw_second_moment(key, part):
    pieces = []
    for position, entry in enumerate(layout_drawn()):
        sub_key = jax.random.fold_in(key, 500 + position)
        log_factor = jax.random.uniform(sub_key, entry[1], jnp.float32, math.log(0.5), math.log(2.0))
        guess = grad_guess(entry[1])
        pieces.append(((1.0 - beta_two) / beta_two * guess * guess * 2.0 * jnp.exp(log_factor)).reshape(-1))
    return jnp.concatenate(pieces)


def place_ends(result, stream_key, smallest, largest):
    spot = [jax.random.randint(jax.random.fold_in(stream_key, axis), (), 0, length) for axis, length in enumerate(result.shape)]
    widest = result.shape.index(max(result.shape))
    next_to = spot[:widest] + [(spot[widest] + 1) % result.shape[widest]] + spot[widest + 1:]
    return result.at[tuple(spot)].set(smallest).at[tuple(next_to)].set(largest)


def levels(stream_key, shape, split, smallest, high):
    loudness, own = 1.0, jax.random.fold_in(stream_key, 6)
    for axis_at, parts in split:
        draws = jnp.exp(jax.random.uniform(jax.random.fold_in(own, axis_at), (parts,), jnp.float32, smallest / len(split), high / len(split)))
        loudness = loudness * jnp.repeat(draws, shape[axis_at] // parts).reshape([-1 if axis == axis_at else 1 for axis in range(len(shape))])
    return loudness


def deal_out(rng, own, number, rows, number_of, top, bound, skew):
    order = jax.random.permutation(rng, number_of)
    heavy_load, ordinary = load_shares(number_of, rows * top, bound, skew, True), load_shares(number_of, rows * top, bound, skew, False)
    places = jnp.arange(number_of)

    def named(lengths, rotation):
        used = int((lengths > 0).sum())
        fixed = max(1, used // 4)
        shifted = fixed + (places - fixed + rotation * (used - fixed)) % max(1, number_of - fixed)
        return jnp.zeros((number_of,), jnp.int32).at[order[jnp.where(places < fixed, places, shifted)]].set(jnp.asarray(lengths, jnp.int32))

    lengths = jnp.where(number % 4 == 0, named(heavy_load, number // 4), named(ordinary, number - number // 4 - 1))
    mixed = jax.random.permutation(jax.random.fold_in(own, 3), number_of)
    source_of, receiver = mixed[0:number_of // 2 * 2:2], mixed[1:number_of // 2 * 2:2]
    slack = jnp.minimum(lengths[source_of] - 1, bound - lengths[receiver]) // 2
    slack = jnp.where((source_of == order[0]) | (receiver == order[0]) | (lengths[receiver] == 0), 0, jnp.maximum(slack, 0))
    shifted = jax.random.randint(jax.random.fold_in(own, 4), (number_of // 2,), 0, 1 << 20) % (slack + 1)
    lengths = lengths.at[source_of].add(-shifted).at[receiver].add(shifted)
    members = jnp.searchsorted(jnp.cumsum(lengths), jnp.arange(rows * top), side="right").astype(jnp.int32)
    table = members.reshape(top, rows).T
    table = table[jax.random.permutation(jax.random.fold_in(own, 1), rows)]
    rotation = jax.random.randint(jax.random.fold_in(own, 2), (rows, 1), 0, top)
    return jnp.take_along_axis(table, (jnp.arange(top)[None, :] + rotation) % top, axis=1)


def load_shares(number_of, total, limit, lean, full):
    portions = [(1 << 20) // math.isqrt(standing ** lean) + 1 for standing in range(1, number_of + 1)]
    largest = limit if full else min(limit, max(-(-total // number_of), total * portions[0] // sum(portions)))
    least = 1 if total - largest >= number_of - 1 else 0
    given, rest = [largest] + [least] * (number_of - 1), total - largest - least * (number_of - 1)
    while rest > 0:
        candidates = [i for i in range(1, number_of) if given[i] < largest] or [i for i in range(1, number_of) if given[i] < limit]
        mass, budget = sum([portions[i] for i in candidates]), rest
        for i in candidates:
            addition = min(limit - given[i], max(1, budget * portions[i] // mass), rest)
            given[i] = given[i] + addition
            rest = rest - addition
    return np.array(given)


def scatter_about(rng, shape, width, bound, cuts=(), kind=jnp.bfloat16):
    level = levels(rng, shape, cuts, -0.22, 0.18) if cuts else 1.0
    result = jax.random.normal(rng, shape, jnp.float32) * width * level
    return jnp.minimum(jnp.maximum(result, -bound), bound).astype(kind)


def setup_inputs(seed: int = 0) -> dict:
    splits = jax.random.split(jax.random.key(seed), 10)
    point_feats = scatter_about(splits[0], (C_IN, POINTS), 1.0, 6.0, ((1, 32),))
    point_tile_keys = jax.random.split(jax.random.fold_in(splits[1], 1), POINTS // P_DEV)
    point_tile_turns = jax.random.permutation(jax.random.fold_in(splits[1], 3), POINTS // P_DEV)
    point_tile = jax.vmap(lambda own, number: deal_out(jax.random.fold_in(splits[1], 2), own, number, P_DEV, N_TILE, 1, CAP, 1))(point_tile_keys, point_tile_turns).reshape((POINTS, 1))
    point_cell = place_ends(jax.random.randint(splits[2], (POINTS,), 0, CELLS), jax.random.fold_in(splits[2], 1), 0, CELLS - 1).astype(jnp.int32)
    point_valid = place_ends((jax.random.randint(splits[3], (POINTS,), 0, 8) < 7).astype(jnp.int32), jax.random.fold_in(splits[3], 1), 0, 1)
    pillar_frame = place_ends(jax.random.randint(splits[4], (NXG, NYG), 0, FRAMES), jax.random.fold_in(splits[4], 1), 0, FRAMES - 1).astype(jnp.int32)
    cotangent = scatter_about(splits[5], (NXG, NYG, D), 1.0, 6.0, ((0, 8), (1, 4)))
    params = draw_params(jax.random.fold_in(splits[9], 71), 0)
    first_moment = draw_first_moment(jax.random.fold_in(splits[9], 71), 0)
    second_moment = draw_second_moment(jax.random.fold_in(splits[9], 71), 0)
    return dict(point_feats=point_feats, point_tile=point_tile, point_cell=point_cell, point_valid=point_valid, pillar_frame=pillar_frame, cotangent=cotangent, params=params, first_moment=first_moment, second_moment=second_moment)


@jax.custom_vjp
def low(v):
    return lax.optimization_barrier(v.astype(jnp.bfloat16)).astype(jnp.float32)

@jax.custom_vjp
def low_back(v):
    return v

def low_keep(v):
    return (low(v), None)

def low_pass(kept, grad):
    return (grad,)

def back_keep(v):
    return (v, None)

def back_low(kept, grad):
    return (low(grad),)
low.defvjp(low_keep, low_pass)
low_back.defvjp(back_keep, back_low)
highest = lax.Precision.HIGHEST
clip_norm = 0.01
beta_one = 0.9
beta_two = 0.999
step_count = 10
learn_rate = 0.1
decay_rate = 0.05
adam_eps = 1e-08

def layout():
    entries = [('point_in_weight', (C_IN, H1)), ('point_in_bias', (H1,)), ('point_out_weight', (H1, D)), ('point_out_bias', (D,))]
    for layer_idx in range(LAYERS):
        entries = entries + [('qkv_weight', (D, 3 * D)), ('out_weight', (D, D)), ('ffn_in_weight', (D, FF)), ('ffn_out_weight', (FF, D)), ('query_bias', (D,)), ('value_bias', (D,)), ('out_bias', (D,)), ('norm1_gain', (D,)), ('norm1_bias', (D,)), ('ffn_in_bias', (FF,)), ('ffn_out_bias', (D,)), ('norm2_gain', (D,)), ('norm2_bias', (D,))]
    return entries

def unpack(flat_vec):
    pieces = []
    offset = 0
    for entry_name, extents in layout():
        length = math.prod(extents)
        pieces.append(flat_vec[offset:offset + length].reshape(extents))
        offset = offset + length
    return pieces

def layer_norm(values, gain, shift_bias):
    center = values - lax.optimization_barrier(jnp.mean(values, axis=-1, keepdims=True))
    spread = lax.optimization_barrier(jnp.mean(center * center, axis=-1, keepdims=True))
    return center * lax.rsqrt(spread + 1e-05) * gain + shift_bias

def to_windows(grid):
    across = grid.shape[0] // WIN
    along = grid.shape[1] // WIN
    trailing = grid.shape[2:]
    parted = grid.reshape((across, WIN, along, WIN) + trailing)
    parted = jnp.swapaxes(parted, 1, 2)
    return parted.reshape((across * along, WIN * WIN) + trailing)

def from_windows(parted, extent_x, extent_y):
    across = extent_x // WIN
    along = extent_y // WIN
    trailing = parted.shape[2:]
    grid = parted.reshape((across, along, WIN, WIN) + trailing)
    grid = jnp.swapaxes(grid, 1, 2)
    return grid.reshape((extent_x, extent_y) + trailing)

def attention_mask(win_tags, win_regions):
    slot_count = win_tags.shape[1]
    same_group = (win_tags[:, :, None] == win_tags[:, None, :]) & (win_tags[:, None, :] > 0) & (win_regions[:, :, None] == win_regions[:, None, :])
    return same_group | jnp.eye(slot_count, dtype=bool)[None]

def sublayers(windows, win_tags, win_regions, weights):
    qkv_weight, out_weight, ffn_in_weight, ffn_out_weight, query_bias, value_bias, out_bias, norm1_gain, norm1_bias, ffn_in_bias, ffn_out_bias, norm2_gain, norm2_bias = weights
    win_count = windows.shape[0]
    slot_count = windows.shape[1]
    live_mask = (win_tags > 0).astype(jnp.float32)[..., None]
    allowed = attention_mask(win_tags, win_regions)
    qkv_bias = jnp.concatenate([query_bias, jnp.zeros_like(query_bias), value_bias])
    packed = jnp.einsum('wsd,de->wse', low(windows), low(qkv_weight), precision=highest) + qkv_bias
    packed = low(low_back(packed)).reshape(win_count, slot_count, 3, HEADS, HD)
    scores = jnp.einsum('wqhd,wkhd->whqk', packed[:, :, 0], packed[:, :, 1], precision=highest) * HD ** (-0.5)
    scores = jnp.where(allowed[:, None], low_back(scores), -1000000000.0)
    attn_probs = low(jax.nn.softmax(scores, axis=-1))
    mixture = jnp.einsum('whqk,wkhd->wqhd', attn_probs, packed[:, :, 2], precision=highest).reshape(win_count, slot_count, D)
    mixture = low(low_back(mixture))
    attn_out = low_back(jnp.einsum('wsd,de->wse', mixture, low(out_weight), precision=highest) + out_bias)
    normed = layer_norm(windows + attn_out, norm1_gain, norm1_bias) * live_mask
    hidden = low_back(jnp.einsum('wsd,df->wsf', low(normed), low(ffn_in_weight), precision=highest) + ffn_in_bias)
    hidden = low(jax.nn.gelu(hidden))
    ffn_result = low_back(jnp.einsum('wsf,fd->wsd', hidden, low(ffn_out_weight), precision=highest) + ffn_out_bias)
    layer_out = layer_norm(normed + ffn_result, norm2_gain, norm2_bias) * live_mask
    square_sums = jnp.stack([jnp.sum(attn_out * attn_out * live_mask), jnp.sum(ffn_result * ffn_result * live_mask), jnp.sum(layer_out * layer_out)])
    return (layer_out, square_sums)

def run_layer(grid_field, cell_tags, regions, weights):
    extent_x, extent_y = cell_tags.shape
    per_group = TX // WIN * (TY // WIN)
    slot_total = WIN * WIN
    field_groups = to_windows(grid_field).reshape(-1, per_group, slot_total, D)
    tag_groups = to_windows(cell_tags).reshape(-1, per_group, slot_total)
    region_groups = to_windows(regions).reshape(-1, per_group, slot_total)
    checked = jax.checkpoint(sublayers)

    def one_group(group_items):
        return checked(group_items[0], group_items[1], group_items[2], weights)
    results, square_sums = lax.map(one_group, (field_groups, tag_groups, region_groups))
    return (from_windows(results.reshape(-1, slot_total, D), extent_x, extent_y), lax.optimization_barrier(jnp.sum(square_sums, axis=0)))

def reference(point_feats, point_tile, point_cell, point_valid, pillar_frame, cotangent, params, first_moment, second_moment):
    extent_x, extent_y = pillar_frame.shape
    half_win = WIN // 2
    features = point_feats.astype(jnp.float32).T
    point_band = (jnp.arange(point_cell.shape[0]) // P_DEV % N_ROW).astype(jnp.int32)
    cell_x = point_tile[:, 0] * TX + point_cell // TY
    cell_y = point_band * TY + point_cell % TY
    cell_index = (cell_x * extent_y + cell_y).astype(jnp.int32)
    point_live = point_valid.astype(jnp.float32)
    counts = jax.ops.segment_sum(point_live, cell_index, num_segments=extent_x * extent_y)
    live_cells = (counts > 0).reshape(extent_x, extent_y)
    cell_tags = jnp.where(live_cells, pillar_frame + 1, 0).astype(jnp.int32)
    rolled_tags = jnp.roll(cell_tags, (-half_win, -half_win), axis=(0, 1))
    wrap_x = (jnp.arange(extent_x) + half_win >= extent_x).astype(jnp.int32)
    wrap_y = (jnp.arange(extent_y) + half_win >= extent_y).astype(jnp.int32)
    regions = wrap_x[:, None] * 2 + wrap_y[None, :]
    flat_regions = jnp.zeros_like(cell_tags)

    def forward(flat_params):
        pieces = unpack(flat_params)
        point_in_weight, point_in_bias, point_out_weight, point_out_bias = pieces[:4]
        pre_act = low_back(jnp.dot(features, low(point_in_weight), precision=highest) + point_in_bias)
        activity = low(jax.nn.gelu(pre_act))
        point_out = low(jnp.dot(activity, low(point_out_weight), precision=highest) + point_out_bias) * point_live[:, None]
        pillar_sum = low_back(jax.ops.segment_sum(point_out, cell_index, num_segments=extent_x * extent_y))
        grid_field = (pillar_sum / jnp.maximum(counts, 1.0)[:, None]).reshape(extent_x, extent_y, D)
        grid_field, first_sums = run_layer(grid_field, cell_tags, flat_regions, pieces[4:17])
        grid_field = jnp.roll(grid_field, (-half_win, -half_win), axis=(0, 1))
        grid_field, second_sums = run_layer(grid_field, rolled_tags, regions, pieces[17:30])
        return (grid_field, jnp.concatenate([first_sums, second_sums]))
    final_field, pullback, square_sums = jax.vjp(forward, params, has_aux=True)
    rolled_cot = jnp.roll(cotangent.astype(jnp.float32), (-half_win, -half_win), axis=(0, 1)) / (extent_x * extent_y)
    gradient = pullback(rolled_cot)[0]
    grad_norm = jnp.sqrt(jnp.sum(gradient * gradient))
    clipped = gradient * jnp.minimum(1.0, clip_norm / (grad_norm + 1e-06))
    new_first = beta_one * first_moment + (1.0 - beta_one) * clipped
    new_second = beta_two * second_moment + (1.0 - beta_two) * clipped * clipped
    first_hat = new_first / (1.0 - beta_one ** step_count)
    second_hat = new_second / (1.0 - beta_two ** step_count)
    new_params = params - learn_rate * (first_hat / (jnp.sqrt(second_hat) + adam_eps) + decay_rate * params)
    live_total = jnp.maximum(jnp.sum(live_cells.astype(jnp.float32)), 1.0)
    sublayer_rms = jnp.sqrt(square_sums / (live_total * D))
    return (grad_norm, new_params, new_first, new_second, new_params.astype(jnp.bfloat16), sublayer_rms)
```

```python
import jax
import jax.numpy as jnp
from jax import lax
from jax.experimental import pallas as pl
from jax.experimental.pallas import tpu as pltpu
from jax.sharding import PartitionSpec as P

D = 128
HEADS = 8
HD = 16
FF = 256
H1 = 64
WIN = 12
C_IN = 11
QS = 6
QC = 36
QP = 40
SLOTS = 144
KEYS = HEADS * SLOTS
LAYER_ROWS = 1034
POINT_ROWS = 71
GRAD_ROWS = 1040
BLOCK = 256
CHUNK = 512
LO = 512
NW = 2

clip_norm = 0.01
beta_one = 0.9
beta_two = 0.999
step_count = 10
learn_rate = 0.1
decay_rate = 0.05
adam_eps = 1e-08

F32 = jnp.float32
BF16 = jnp.bfloat16
GELU_C = 0.7978845608028654
GELU_A = 0.044715


def mm(a, b):
    return lax.dot_general(a, b, (((1,), (0,)), ((), ())), preferred_element_type=F32)


def mm_nt(a, b):
    return lax.dot_general(a, b, (((1,), (1,)), ((), ())), preferred_element_type=F32)


def mm_tn(a, b):
    return lax.dot_general(a, b, (((0,), (0,)), ((), ())), preferred_element_type=F32)


def lane_iota(rows=1):
    return lax.broadcasted_iota(jnp.int32, (rows, D), 1)


def part8(v):
    return jnp.sum(v.reshape(v.shape[0] // 8, 8, v.shape[1]), axis=0)


def gelu_parts(v):
    sq = v * v
    t = jnp.tanh(v * (GELU_C + (GELU_C * GELU_A) * sq))
    half = 0.5 + 0.5 * t
    slope = half + (0.5 * v) * (1.0 - t * t) * (GELU_C + (3.0 * GELU_C * GELU_A) * sq)
    return v * half, slope


def gelu_only(v):
    t = jnp.tanh(v * (GELU_C + (GELU_C * GELU_A) * (v * v)))
    return v * (0.5 + 0.5 * t)


def normalize(y):
    center = y - jnp.mean(y, axis=-1, keepdims=True)
    rs = lax.rsqrt(jnp.mean(center * center, axis=-1, keepdims=True) + 1e-05)
    return center * rs, rs


def norm_pull(gx, xhat, rs):
    return rs * (
        gx
        - jnp.mean(gx, axis=-1, keepdims=True)
        - xhat * jnp.mean(gx * xhat, axis=-1, keepdims=True)
    )


def load_layer(par, base, w):
    for part in range(3):
        m = par[pl.ds(base + part, D, stride=3), :]
        w["qkv"][:, part * D : (part + 1) * D] = m.astype(BF16)
        if "qkv_t" in w:
            w["qkv_t"][part * D : (part + 1) * D, :] = m.T.astype(BF16)
    m = par[pl.ds(base + 384, D), :]
    w["out"][...] = m.astype(BF16)
    if "out_t" in w:
        w["out_t"][...] = m.T.astype(BF16)
    for part in range(2):
        m = par[pl.ds(base + 512 + part, D, stride=2), :]
        w["fin"][:, part * D : (part + 1) * D] = m.astype(BF16)
        if "fin_t" in w:
            w["fin_t"][part * D : (part + 1) * D, :] = m.T.astype(BF16)
        m = par[pl.ds(base + 768 + part * D, D), :]
        w["fout"][part * D : (part + 1) * D, :] = m.astype(BF16)
        if "fout_t" in w:
            w["fout_t"][:, part * D : (part + 1) * D] = m.T.astype(BF16)


WEIGHT_SHAPES = {
    "qkv": (D, 3 * D),
    "qkv_t": (3 * D, D),
    "out": (D, D),
    "out_t": (D, D),
    "fin": (D, FF),
    "fin_t": (FF, D),
    "fout": (FF, D),
    "fout_t": (D, FF),
}


def vec(par, base, row):
    return par[base + 1024 + row : base + 1025 + row, :]


def vec2(par, base, row):
    return jnp.concatenate([vec(par, base, row), vec(par, base, row + 1)], axis=1)


def head_lanes():
    return lane_iota() // HD


def head_rows(m):
    lanes = head_lanes()
    keep = [jnp.where(lanes == h, 1.0, 0.0).astype(BF16) for h in range(HEADS)]
    top = m[:D]
    rest = m[D:]
    return jnp.concatenate([top * k for k in keep] + [rest * k for k in keep], axis=0)


def window_bias(groups):
    keys = jnp.concatenate(
        [groups[:D]] + [groups[D:]] * HEADS + [jnp.ones((D, D), BF16)], axis=0
    )
    same = mm_nt(groups, keys)
    rows = lax.broadcasted_iota(jnp.int32, (SLOTS, D), 0)
    lanes = lane_iota(SLOTS)
    first = (same[:, :D] > 0.5) | (rows == lanes)
    last = (same[:, D : 2 * D] > 0.5) | (rows == lanes % HD + D)
    return (
        jnp.where(first, 0.0, -1000000000.0),
        jnp.where(last, 0.0, -1000000000.0),
        same[:, 2 * D :],
    )


def attend(qs, key, val, bias_first, bias_last):
    scores = mm_nt(key, head_rows(qs))
    probs = []
    for h in range(HEADS + 1):
        part = scores[:, h * D : (h + 1) * D] + (bias_first if h < HEADS else bias_last)
        expo = jnp.exp(part - jnp.max(part, axis=0, keepdims=True))
        probs.append((expo * (1.0 / jnp.sum(expo, axis=0, keepdims=True))).astype(BF16))
    probs = jnp.concatenate(probs, axis=1)
    return probs, query_pull(val, probs)


def attend_pull(probs, qs, key, val, gmix):
    rows = head_rows(gmix)
    pulled = mm_nt(val, rows)
    gs = []
    for h in range(HEADS + 1):
        cols = slice(h * D, (h + 1) * D)
        p = probs[:, cols].astype(F32)
        both = p * pulled[:, cols]
        gs.append((both - p * jnp.sum(both, axis=0, keepdims=True)).astype(BF16))
    gs = jnp.concatenate(gs, axis=1)
    return query_pull(key * 0.25, gs), mm(gs, head_rows(qs)).astype(BF16), mm(probs, rows).astype(BF16)


def query_pull(rows, cols):
    full = mm_tn(rows, cols)
    top = jnp.concatenate(
        [full[h * HD : (h + 1) * HD, h * D : (h + 1) * D] for h in range(HEADS)], axis=0
    )
    chan = lax.broadcasted_iota(jnp.int32, (D, D), 0)
    lanes = lane_iota(D)
    rest = jnp.where(chan // HD == lanes // HD, full[:, HEADS * D :], 0.0).astype(BF16)
    fold = jnp.where(
        lax.broadcasted_iota(jnp.int32, (HD, D), 0) == lane_iota(HD) % HD, 1.0, 0.0
    ).astype(BF16)
    return jnp.concatenate([top.T.astype(BF16), mm_nt(fold, rest).astype(BF16)], axis=0)


def split_qkv(packed, w):
    rows = slice(w * SLOTS, (w + 1) * SLOTS)
    return packed[rows, :D] * 0.25, packed[rows, D : 2 * D], packed[rows, 2 * D :]


def layer_forward(x, groups, par, base, w, sums):
    count = x.shape[0] // SLOTS
    low = x.astype(BF16)
    qkv_bias = jnp.concatenate(
        [vec(par, base, 0), jnp.zeros((1, D), F32), vec(par, base, 1)], axis=1
    )
    packed = (mm(low, w["qkv"][...]) + qkv_bias).astype(BF16)
    probs, mixes, lives = [], [], []
    for i in range(count):
        bias_first, bias_last, live = window_bias(groups[i])
        qs, key, val = split_qkv(packed, i)
        prob, mix = attend(qs, key, val, bias_first, bias_last)
        probs.append(prob)
        mixes.append(mix)
        lives.append(live)
    mix = jnp.concatenate(mixes, axis=0)
    live = jnp.concatenate(lives, axis=0)
    attn_out = mm(mix, w["out"][...]) + vec(par, base, 2)
    first = x + attn_out
    xhat1, rs1 = normalize(first)
    normed = (xhat1 * vec(par, base, 3) + vec(par, base, 4)) * live
    normed_low = normed.astype(BF16)
    pre = mm(normed_low, w["fin"][...]) + vec2(par, base, 5)
    act, slope = gelu_parts(pre)
    hidden = act.astype(BF16)
    ffn = mm(hidden, w["fout"][...]) + vec(par, base, 7)
    second = normed + ffn
    xhat2, rs2 = normalize(second)
    result = (xhat2 * vec(par, base, 8) + vec(par, base, 9)) * live
    sums[0] += part8(attn_out * attn_out * live)
    sums[1] += part8(ffn * ffn * live)
    sums[2] += part8(result * result)
    sums[3] += part8(live)
    return dict(
        low=low,
        packed=packed,
        probs=probs,
        mix=mix,
        live=live,
        first=first,
        second=second,
        xhat1=xhat1,
        rs1=rs1,
        xhat2=xhat2,
        rs2=rs2,
        normed_low=normed_low,
        slope=slope,
        hidden=hidden,
        result=result,
    )


def layer_backward(grad, k, par, base, w, acc):
    live = k["live"]
    gl = grad * live
    acc["vec"][8] += part8(gl * k["xhat2"])
    acc["vec"][9] += part8(gl)
    g2 = norm_pull(gl * vec(par, base, 8), k["xhat2"], k["rs2"])
    g_ffn = g2.astype(BF16)
    acc["fout"][...] += mm_tn(k["hidden"], g_ffn)
    acc["vec"][7] += part8(g_ffn.astype(F32))
    g_pre = (mm(g_ffn, w["fout_t"][...]) * k["slope"]).astype(BF16)
    acc["fin"][...] += mm_tn(k["normed_low"], g_pre)
    for part in range(2):
        acc["vec"][5 + part] += part8(g_pre[:, part * D : (part + 1) * D].astype(F32))
    g_norm = (g2 + mm(g_pre, w["fin_t"][...])) * live
    acc["vec"][3] += part8(g_norm * k["xhat1"])
    acc["vec"][4] += part8(g_norm)
    g1 = norm_pull(g_norm * vec(par, base, 3), k["xhat1"], k["rs1"])
    g_attn = g1.astype(BF16)
    acc["out"][...] += mm_tn(k["mix"], g_attn)
    acc["vec"][2] += part8(g_attn.astype(F32))
    g_mix = mm(g_attn, w["out_t"][...]).astype(BF16)
    pieces = []
    for i in range(grad.shape[0] // SLOTS):
        rows = slice(i * SLOTS, (i + 1) * SLOTS)
        qs, key, val = split_qkv(k["packed"], i)
        pieces.append(
            jnp.concatenate(
                attend_pull(k["probs"][i], qs, key, val, g_mix[rows]), axis=1
            )
        )
    g_packed = jnp.concatenate(pieces, axis=0)
    acc["qkv"][...] += mm_tn(k["low"], g_packed)
    acc["vec"][0] += part8(g_packed[:, :D].astype(F32))
    acc["vec"][1] += part8(g_packed[:, 2 * D :].astype(F32))
    return g1 + mm(g_packed, w["qkv_t"][...])


ACC_SHAPES = {
    "qkv": (D, 3 * D),
    "out": (D, D),
    "fin": (D, FF),
    "fout": (FF, D),
    "vec": (10, 8, D),
}


def clear(acc):
    for ref in acc.values():
        ref[...] = jnp.zeros(ref.shape, ref.dtype)


def store_grads(acc, out):
    for part in range(3):
        out[pl.ds(part, D, stride=3), :] = acc["qkv"][:, part * D : (part + 1) * D]
    out[pl.ds(384, D), :] = acc["out"][...]
    for part in range(2):
        out[pl.ds(512 + part, D, stride=2), :] = acc["fin"][:, part * D : (part + 1) * D]
    out[pl.ds(768, FF), :] = acc["fout"][...]
    out[pl.ds(1024, 16), :] = jnp.concatenate(
        [jnp.sum(acc["vec"][i], axis=0, keepdims=True) for i in range(10)]
        + [jnp.zeros((6, D), F32)],
        axis=0,
    )


def gather_windows(scratch, pick):
    for i in range(NW):
        for r in range(2):
            for c in range(2):
                at = i * SLOTS + (2 * r + c) * QC
                scratch[pl.ds(at, QC), :] = pick(r, 2 * i + c)
    return scratch[...]


def spread_windows(scratch, value, put):
    scratch[...] = value
    for i in range(NW):
        for r in range(2):
            for c in range(2):
                put(r, 2 * i + c, scratch[pl.ds(i * SLOTS + (2 * r + c) * QC, QC), :])


def whole(shape, space=pltpu.VMEM):
    return pl.BlockSpec(shape, lambda *_: (0,) * len(shape), memory_space=space)


def params_for(limit=56):
    return pltpu.CompilerParams(
        dimension_semantics=("arbitrary",), vmem_limit_bytes=limit * 1024 * 1024
    )


def first_layer(pillars, par, quads_x, quads_y):
    across = quads_x // 2
    along = quads_y // (2 * NW)
    windows = quads_x * quads_y // 4
    base = POINT_ROWS

    def kernel(pil, par_ref, *refs):
        outs, scratch = refs[:12], refs[12:]
        (
            field,
            probs_out,
            packed_out,
            mix_out,
            first_out,
            second_out,
            low_out,
            live_out,
            sums_out,
            row_out,
            col_out,
            cor_out,
        ) = outs
        names = ["qkv", "out", "fin", "fout"]
        w = dict(zip(names, scratch[:4]))
        wide, pout, sums = scratch[4:]
        step = pl.program_id(0)
        a = step // along
        b = step % along

        @pl.when(step == 0)
        def _():
            load_layer(par_ref, base, w)
            m = par_ref[pl.ds(6, H1), :].astype(BF16)
            pout[...] = jnp.concatenate([m, m], axis=0)
            sums[...] = jnp.zeros(sums.shape, F32)

        cells = gather_windows(wide, lambda r, c: pil[r, c, :QC, :])
        lanes = lane_iota()
        total = jnp.where(lanes < H1, cells, 0.0)
        count = cells[:, H1 : H1 + 1]
        high = total.astype(BF16).astype(F32)
        both = (high + pltpu.roll(total - high, H1, axis=1)).astype(BF16)
        pillar = mm(both, pout[...]) + count * par_ref[70:71, :]
        x = pillar / jnp.maximum(count, 1.0)
        onehot = jnp.where((lanes > H1) & (lanes < H1 + 4) & (count > 0.0), cells, 0.0).astype(BF16)
        groups = [onehot[i * SLOTS : (i + 1) * SLOTS] for i in range(NW)]
        k = layer_forward(x, groups, par_ref, base, w, sums)
        for i in range(NW):
            rows = slice(i * SLOTS, (i + 1) * SLOTS)
            probs_out[i] = k["probs"][i]
            packed_out[i] = k["packed"][rows]
            mix_out[i] = k["mix"][rows]
            first_out[i] = k["first"][rows]
            second_out[i] = k["second"][rows]
            low_out[i] = k["low"][rows]
            live_out[i] = k["live"][rows]

        def put(r, c, v):
            field[r, c, :QC, :] = v

        spread_windows(wide, k["result"], put)

        @pl.when(a == 0)
        def _():
            for c in range(2 * NW):
                row_out[c] = field[0, c, :QC, :].astype(BF16)

        @pl.when(b == 0)
        def _():
            for r in range(2):
                col_out[r] = field[r, 0, :QC, :].astype(BF16)

        @pl.when(step == 0)
        def _():
            cor_out[0] = field[0, 0, :QC, :].astype(BF16)

        @pl.when(step == pl.num_programs(0) - 1)
        def _():
            sums_out[...] = sums[...]

    def win_spec(width):
        return pl.BlockSpec((NW, SLOTS, width), lambda s: (s, 0, 0))

    quad_spec = pl.BlockSpec((2, 2 * NW, QP, D), lambda s: (s // along, s % along, 0, 0))
    shape = jax.ShapeDtypeStruct
    return pl.pallas_call(
        kernel,
        grid=(across * along,),
        in_specs=[quad_spec, whole(par.shape)],
        out_specs=[
            quad_spec,
            win_spec(KEYS),
            win_spec(3 * D),
            win_spec(D),
            win_spec(D),
            win_spec(D),
            win_spec(D),
            win_spec(D),
            whole((4, 8, D)),
            pl.BlockSpec((2 * NW, QC, D), lambda s: (jnp.minimum(s, along - 1), 0, 0)),
            pl.BlockSpec((2, QC, D), lambda s: (s // along, 0, 0)),
            whole((1, QC, D)),
        ],
        out_shape=[
            shape((quads_x, quads_y, QP, D), F32),
            shape((windows, SLOTS, KEYS), BF16),
            shape((windows, SLOTS, 3 * D), BF16),
            shape((windows, SLOTS, D), BF16),
            shape((windows, SLOTS, D), F32),
            shape((windows, SLOTS, D), F32),
            shape((windows, SLOTS, D), BF16),
            shape((windows, SLOTS, D), F32),
            shape((4, 8, D), F32),
            shape((quads_y, QC, D), BF16),
            shape((quads_x, QC, D), BF16),
            shape((1, QC, D), BF16),
        ],
        scratch_shapes=[pltpu.VMEM(WEIGHT_SHAPES[n], BF16) for n in ["qkv", "out", "fin", "fout"]]
        + [
            pltpu.VMEM((NW * SLOTS, D), F32),
            pltpu.VMEM((D, D), BF16),
            pltpu.VMEM((4, 8, D), F32),
        ],
        compiler_params=params_for(),
        name="first_layer",
    )(pillars, par)


def second_layer(flags, field, halos, tags, tag_halos, cot, cot_halos, par, scale):
    quads_x, quads_y = field.shape[:2]
    across = quads_x // 2
    along = quads_y // (2 * NW)
    base = POINT_ROWS + LAYER_ROWS
    wnames = list(WEIGHT_SHAPES)
    anames = list(ACC_SHAPES)

    def kernel(flag, *refs):
        ins, refs = refs[:13], refs[13:]
        outs, scratch = refs[:6], refs[6:]
        fields, tagss, cots, par_ref = ins[:4], ins[4:8], ins[8:12], ins[12]
        grads, weights, row_out, col_out, cor_out, sums_out = outs
        w = dict(zip(wnames, scratch))
        scratch = scratch[len(wnames) :]
        acc = dict(zip(anames, scratch))
        wide, sums, ext_x, ext_t, ext_g = scratch[len(anames) :]
        step = pl.program_id(0)
        a = step // along
        b = step % along

        @pl.when(step == 0)
        def _():
            load_layer(par_ref, base, w)
            sums[...] = jnp.zeros(sums.shape, F32)
            clear(acc)
            lanes = lane_iota()

            def moved(v, region):
                return pltpu.roll(v, 3 * region, axis=1)

            def fill(ext, srcs, turn_row, turn_col, turn_cor):
                main, row, col, cor = srcs

                def one(i, _):
                    ext[i // quads_y, i % quads_y, :QC, :] = main[
                        i // quads_y, i % quads_y, :QC, :
                    ].astype(F32)
                    return 0

                lax.fori_loop(0, quads_x * quads_y, one, 0, unroll=4)

                def one_row(i, _):
                    ext[quads_x, i, :QC, :] = turn_row(row[i].astype(F32))
                    return 0

                lax.fori_loop(1, quads_y, one_row, 0)
                for i in range(1, quads_x):
                    ext[i, quads_y, :QC, :] = turn_col(col[i].astype(F32))
                ext[quads_x, quads_y, :QC, :] = turn_cor(cor[0].astype(F32))

            def same(v):
                return v

            last_x = flag[0] > 0
            last_y = flag[1] > 0

            def tag_row(v):
                return jnp.where(last_x, moved(v, 2), v)

            def tag_col(v):
                return jnp.where(last_y, moved(v, 1), v)

            fill(ext_x, fields, same, same, same)
            fill(ext_t, tagss, tag_row, tag_col, lambda v: tag_row(tag_col(v)))
            fill(ext_g, cots, same, same, same)

        def picker(ext):
            return lambda r, c: ext[2 * a + 1 + r, 2 * NW * b + 1 + c, :QC, :]

        tag = gather_windows(wide, picker(ext_t)).astype(BF16)
        groups = [tag[i * SLOTS : (i + 1) * SLOTS] for i in range(NW)]
        x = gather_windows(wide, picker(ext_x))
        k = layer_forward(x, groups, par_ref, base, w, sums)
        grad = gather_windows(wide, picker(ext_g)) * scale
        gx = layer_backward(grad, k, par_ref, base, w, acc)

        def put(r, c, v):
            grads[r, c, :QC, :] = v

        spread_windows(wide, gx, put)

        @pl.when(a == across - 1)
        def _():
            for c in range(2 * NW):
                row_out[c] = grads[1, c, :QC, :].astype(BF16)

        @pl.when(b == along - 1)
        def _():
            for r in range(2):
                col_out[r] = grads[r, 2 * NW - 1, :QC, :].astype(BF16)

        @pl.when(step == pl.num_programs(0) - 1)
        def _():
            cor_out[0] = grads[1, 2 * NW - 1, :QC, :].astype(BF16)
            sums_out[...] = sums[...]
            store_grads(acc, weights)

    shape = jax.ShapeDtypeStruct
    quad_spec = pl.BlockSpec((2, 2 * NW, QP, D), lambda s: (s // along, s % along, 0, 0))
    ext = pltpu.VMEM((quads_x + 1, quads_y + 1, QP, D), F32)
    arrays = [field, *halos, tags, *tag_halos, cot, *cot_halos, par]
    return pl.pallas_call(
        kernel,
        grid=(across * along,),
        in_specs=[pl.BlockSpec(memory_space=pltpu.SMEM)] + [whole(v.shape) for v in arrays],
        out_specs=[
            quad_spec,
            whole((GRAD_ROWS, D)),
            pl.BlockSpec(
                (2 * NW, QC, D), lambda s: (jnp.maximum(s - (across - 1) * along, 0), 0, 0)
            ),
            pl.BlockSpec((2, QC, D), lambda s: (s // along, 0, 0)),
            whole((1, QC, D)),
            whole((4, 8, D)),
        ],
        out_shape=[
            shape((quads_x, quads_y, QP, D), F32),
            shape((GRAD_ROWS, D), F32),
            shape((quads_y, QC, D), BF16),
            shape((quads_x, QC, D), BF16),
            shape((1, QC, D), BF16),
            shape((4, 8, D), F32),
        ],
        scratch_shapes=[pltpu.VMEM(WEIGHT_SHAPES[n], BF16) for n in wnames]
        + [pltpu.VMEM(ACC_SHAPES[n], F32) for n in anames]
        + [
            pltpu.VMEM((NW * SLOTS, D), F32),
            pltpu.VMEM((4, 8, D), F32),
            ext,
            ext,
            ext,
        ],
        compiler_params=params_for(),
        name="second_layer",
    )(flags, *arrays)


def first_layer_back(grads, halos, pillars, saved, par):
    quads_x, quads_y = grads.shape[:2]
    across = quads_x // 2
    along = quads_y // (2 * NW)
    base = POINT_ROWS
    wnames = list(WEIGHT_SHAPES)
    anames = list(ACC_SHAPES)

    def kernel(*refs):
        ins, refs = refs[:13], refs[13:]
        outs, scratch = refs[:3], refs[3:]
        main, row, col, cor, pil = ins[:5]
        probs, packed, mix, first, second, low, live = ins[5:12]
        par_ref = ins[12]
        cell_out, weights, point_weights = outs
        w = dict(zip(wnames, scratch))
        scratch = scratch[len(wnames) :]
        acc = dict(zip(anames, scratch))
        wide, ext, pacc = scratch[len(anames) :]
        step = pl.program_id(0)
        a = step // along
        b = step % along

        @pl.when(step == 0)
        def _():
            load_layer(par_ref, base, w)
            clear(acc)
            pacc[...] = jnp.zeros(pacc.shape, F32)
            for r in range(1, quads_x):

                def one(i, _):
                    ext[r, i, :QC, :] = main[r - 1, i - 1, :QC, :]
                    return 0

                lax.fori_loop(1, quads_y, one, 0)
                ext[r, 0, :QC, :] = col[r - 1].astype(F32)

            def one_row(i, _):
                ext[0, i, :QC, :] = row[i - 1].astype(F32)
                return 0

            lax.fori_loop(1, quads_y, one_row, 0)
            ext[0, 0, :QC, :] = cor[0].astype(F32)

        grad = gather_windows(wide, lambda r, c: ext[2 * a + r, 2 * NW * b + c, :QC, :])

        def rows_of(ref):
            return jnp.concatenate([ref[i] for i in range(NW)], axis=0)

        k = dict(
            low=rows_of(low),
            packed=rows_of(packed),
            probs=[probs[i] for i in range(NW)],
            mix=rows_of(mix),
            live=rows_of(live),
        )
        k["xhat1"], k["rs1"] = normalize(rows_of(first))
        k["xhat2"], k["rs2"] = normalize(rows_of(second))
        normed = (k["xhat1"] * vec(par_ref, base, 3) + vec(par_ref, base, 4)) * k["live"]
        k["normed_low"] = normed.astype(BF16)
        act, k["slope"] = gelu_parts(mm(k["normed_low"], w["fin"][...]) + vec2(par_ref, base, 5))
        k["hidden"] = act.astype(BF16)
        gx = layer_backward(grad, k, par_ref, base, w, acc)

        cells = gather_windows(wide, lambda r, c: pil[r, c, :QC, :])
        lanes = lane_iota()
        total = jnp.where(lanes <= H1, cells, 0.0)
        g_pillar = (gx / jnp.maximum(cells[:, H1 : H1 + 1], 1.0)).astype(BF16)
        high = total.astype(BF16)
        rest = (total - high.astype(F32)).astype(BF16)
        pacc[...] += mm_tn(high, g_pillar) + mm_tn(rest, g_pillar)

        def put(r, c, v):
            cell_out[r, c, :QC, :] = v
            cell_out[r, c, QC:, :] = jnp.zeros((QP - QC, D), F32)

        spread_windows(wide, g_pillar.astype(F32), put)

        @pl.when(step == pl.num_programs(0) - 1)
        def _():
            store_grads(acc, weights)
            point_weights[...] = pacc[:72, :]

    def win_spec(width):
        return pl.BlockSpec((NW, SLOTS, width), lambda s: (s, 0, 0))

    shape = jax.ShapeDtypeStruct
    quad_spec = pl.BlockSpec((2, 2 * NW, QP, D), lambda s: (s // along, s % along, 0, 0))
    return pl.pallas_call(
        kernel,
        grid=(across * along,),
        in_specs=[whole(grads.shape)]
        + [whole(v.shape) for v in halos]
        + [quad_spec]
        + [win_spec(v.shape[2]) for v in saved]
        + [whole(par.shape)],
        out_specs=[quad_spec, whole((GRAD_ROWS, D)), whole((72, D))],
        out_shape=[
            shape((quads_x, quads_y, QP, D), F32),
            shape((GRAD_ROWS, D), F32),
            shape((72, D), F32),
        ],
        scratch_shapes=[pltpu.VMEM(WEIGHT_SHAPES[n], BF16) for n in wnames]
        + [pltpu.VMEM(ACC_SHAPES[n], F32) for n in anames]
        + [
            pltpu.VMEM((NW * SLOTS, D), F32),
            pltpu.VMEM((quads_x, quads_y, QP, D), F32),
            pltpu.VMEM((D, D), F32),
        ],
        compiler_params=params_for(),
        name="first_layer_back",
    )(grads, *halos, pillars, *saved, par)


def one_hot(hit):
    return jnp.where(hit, 1.0, 0.0).astype(BF16)


def bin_points(feats, tiles, cells, valid, tile_count, capacity, extent_y, quads_y):
    blocks = tiles.shape[0]
    groups = tile_count * capacity // LO
    lots = 4
    wide = lots * BLOCK

    def kernel(feat_ref, tile_ref, cell_ref, valid_ref, out_ref, slot_ref, code_ref, acc):
        real = valid_ref[...] > 0
        t = jnp.where(real, tile_ref[...], tile_count)
        i0 = lax.broadcasted_iota(jnp.int32, (BLOCK, BLOCK), 0)
        i1 = lax.broadcasted_iota(jnp.int32, (BLOCK, BLOCK), 1)
        upto = one_hot(i0 <= i1)
        j0 = lax.broadcasted_iota(jnp.int32, (blocks, blocks), 0)
        j1 = lax.broadcasted_iota(jnp.int32, (blocks, blocks), 1)
        earlier = one_hot(j1 < j0)
        slot = jnp.full((blocks, BLOCK), -1.0, F32)
        for k in range(tile_count):
            hit = t == k
            run = mm(one_hot(hit), upto)
            total = jnp.broadcast_to(run[:, BLOCK - 1 :], (blocks, D)).astype(BF16)
            at = mm(earlier, total)[:, :1] + (k * capacity - 1.0)
            slot = jnp.where(hit, run + at, slot)
        slot_ref[...] = slot.astype(jnp.int32)

        def part(v, by):
            return ((v.astype(F32) + 0.5) * (1.0 / by)).astype(jnp.int32)

        cell = cell_ref[...]
        cx = part(cell, extent_y)
        cy = cell - cx * extent_y
        qx, qy = part(cx, QS), part(cy, QS)
        row = (qx * quads_y + qy) * QP + (cx - qx * QS) * QS + (cy - qy * QS)
        hi = row // LO
        lo = row - hi * LO
        low_part = lo % 256
        code_ref[0] = jnp.where(real, 1.0, 0.0)
        code_ref[1] = (hi + 1).astype(F32)
        code_ref[2] = (lo - low_part).astype(F32)
        code_ref[3] = low_part.astype(F32)
        acc[...] = jnp.zeros(acc.shape, F32)
        span = lax.broadcasted_iota(jnp.int32, (LO, wide), 0)

        def one(j, _):
            def line(ref, *lead):
                return jnp.concatenate(
                    [ref[(*lead, pl.ds(j * lots + u, 1), slice(None))] for u in range(lots)], axis=1
                )

            at = line(slot_ref)
            feat = feat_ref[:, pl.ds(pl.multiple_of(j * wide, wide), wide)].astype(F32)
            rows = jnp.concatenate(
                [feat] + [line(code_ref, i) for i in range(4)] + [jnp.zeros((1, wide), F32)], axis=0
            ).astype(BF16)
            group = at // LO
            place = one_hot(span == at % LO)
            spread = jnp.concatenate([rows * one_hot(group == g) for g in range(groups)], axis=0)
            acc[...] += mm_nt(spread, place)
            return 0

        lax.fori_loop(0, blocks // lots, one, 0)
        for k in range(tile_count):
            for at in range(0, capacity, LO):
                g, low = (k * capacity + at) // LO, (k * capacity + at) % LO
                size = min(LO, capacity)
                out_ref[k, :, at : at + size] = acc[g * 16 : g * 16 + 16, low : low + size].astype(
                    BF16
                )

    return pl.pallas_call(
        kernel,
        out_shape=jax.ShapeDtypeStruct((tile_count, 16, capacity), BF16),
        scratch_shapes=[
            pltpu.VMEM((blocks, BLOCK), jnp.int32),
            pltpu.VMEM((4, blocks, BLOCK), F32),
            pltpu.VMEM((groups * 16, LO), F32),
        ],
        compiler_params=pltpu.CompilerParams(vmem_limit_bytes=48 * 1024 * 1024),
        name="bin_points",
    )(feats, tiles, cells, valid)


def unpack_point_in(par_ref, win):
    lanes = lane_iota()
    flat = par_ref[0:6, :]
    turned = pltpu.roll(flat, H1, axis=1)
    even = jnp.where(lanes < H1, flat, turned)
    odd = jnp.where(lanes < H1, turned, flat)
    rows = []
    for k in range(C_IN):
        src = even if k % 2 == 0 else odd
        rows.append(src[k // 2 : k // 2 + 1])
    rows.append(jnp.zeros((5, D), F32))
    win[:, :D] = jnp.concatenate(rows, axis=0).astype(BF16)
    at = lax.broadcasted_iota(jnp.int32, (16, D), 0)
    win[:, D : 2 * D] = one_hot(at == 12)
    win[:, 2 * D :] = one_hot((at == 13) | (at == 14))
    return odd[5:6]


def encode_points(recv, held, par, base_rows, quads):
    sources, _, capacity = recv.shape
    chunk = min(CHUNK, capacity)
    groups = -(-quads * QP // LO)
    pairs = -(-groups // 2)

    def kernel(held_ref, recv_ref, par_ref, base_ref, out_ref, tag_ref, win, acc):
        bias = unpack_point_in(par_ref, win)
        acc[...] = jnp.zeros(acc.shape, F32)
        lanes = lane_iota()
        own = jnp.where(lanes < H1, 1.0, 2.0)
        count_of = (lanes + 1).astype(F32)
        span = lax.broadcasted_iota(jnp.int32, (LO, chunk), 0)

        def source(s, _):
            def piece(j, _):
                cols = recv_ref[s, :, pl.ds(pl.multiple_of(j * chunk, chunk), chunk)]
                wide = cols.astype(F32)
                place = one_hot(span == (wide[13:14] + wide[14:15]).astype(jnp.int32))
                both = mm_tn(cols, win[:, : 2 * D])
                act = gelu_only(both[:, :D] + bias)
                group = both[:, D:]
                spread = [
                    jnp.where(group == own + 2.0 * g, act, 0.0).astype(BF16) for g in range(pairs)
                ]
                spread.append(one_hot(group == count_of))
                acc[...] += mm(place, jnp.concatenate(spread, axis=1))
                return 0

            lax.fori_loop(0, (held_ref[s] + chunk - 1) // chunk, piece, 0)
            return 0

        lax.fori_loop(0, sources, source, 0)
        for g in range(groups):
            rows = min(LO, quads * QP - g * LO)
            v = acc[:rows, g // 2 * D : g // 2 * D + D]
            if g % 2 == 1:
                v = pltpu.roll(v, H1, axis=1)
            count = acc[:rows, pairs * D + g : pairs * D + g + 1]
            v = jnp.where(lanes < H1, v, jnp.where(lanes == H1, count, 0.0))
            out_ref[g * LO : g * LO + rows, :] = v + base_ref[g * LO : g * LO + rows, :]

        def finish(i, _):
            total = out_ref[pl.ds(pl.multiple_of(i * QP, 8), QP), :]
            count = total[:, H1 : H1 + 1]
            tag = jnp.where((lanes > H1) & (lanes < H1 + 4) & (count > 0.0), total, 0.0)
            tag_ref[i] = tag[:QC, :].astype(BF16)
            return 0

        lax.fori_loop(0, quads, finish, 0, unroll=4)

    shape = jax.ShapeDtypeStruct
    return pl.pallas_call(
        kernel,
        in_specs=[pl.BlockSpec(memory_space=pltpu.SMEM)]
        + [pl.BlockSpec(memory_space=pltpu.VMEM)] * 3,
        out_shape=[shape((quads * QP, D), F32), shape((quads, QC, D), BF16)],
        scratch_shapes=[pltpu.VMEM((16, 3 * D), BF16), pltpu.VMEM((LO, (pairs + 1) * D), F32)],
        compiler_params=pltpu.CompilerParams(vmem_limit_bytes=56 * 1024 * 1024),
        name="encode_points",
    )(held, recv, par, base_rows)


def points_back(recv, held, par, cell_grads):
    sources, _, capacity = recv.shape
    chunk = min(CHUNK, capacity)
    total_rows = cell_grads.shape[0]
    groups = -(-total_rows // LO)

    def kernel(held_ref, recv_ref, par_ref, grad_ref, out_ref, win, table, pout_t, acc):
        bias = unpack_point_in(par_ref, win)
        for g in range(groups):
            rows = min(LO, total_rows - g * LO)
            table[:rows, g * D : g * D + D] = grad_ref[g * LO : g * LO + rows, :].astype(BF16)
            if rows < LO:
                table[rows:, g * D : g * D + D] = jnp.zeros((LO - rows, D), BF16)
        m = jnp.concatenate([par_ref[pl.ds(6, H1), :], jnp.zeros((D - H1, D), F32)], axis=0)
        pout_t[...] = m.T.astype(BF16)
        acc[...] = jnp.zeros((16, D), F32)
        lanes = lane_iota()

        def source(s, _):
            def piece(j, _):
                cols = recv_ref[s, :, pl.ds(pl.multiple_of(j * chunk, chunk), chunk)]
                made = mm_tn(cols, win[...])
                group = made[:, D : 2 * D]
                at = made[:, 2 * D :].astype(jnp.int32)
                place = jnp.concatenate(
                    [one_hot(at == lanes + k * D) for k in range(LO // D)], axis=1
                )
                got = jnp.zeros((chunk, D), F32)
                for g in range(0, groups, 2):
                    both = mm(place, table[:, g * D : min(g + 2, groups) * D])
                    for u in range(both.shape[1] // D):
                        got = jnp.where(group == g + u + 1.0, both[:, u * D : u * D + D], got)
                slope = gelu_parts(made[:, :D] + bias)[1]
                acc[...] += mm(cols, (mm(got.astype(BF16), pout_t[...]) * slope).astype(BF16))
                return 0

            lax.fori_loop(0, (held_ref[s] + chunk - 1) // chunk, piece, 0)
            return 0

        lax.fori_loop(0, sources, source, 0)
        rows = []
        for k in range(6):
            odd = pltpu.roll(acc[2 * k + 1 : 2 * k + 2, :], H1, axis=1)
            rows.append(jnp.where(lanes < H1, acc[2 * k : 2 * k + 1, :], odd))
        rows.append(jnp.zeros((2, D), F32))
        out_ref[...] = jnp.concatenate(rows, axis=0)

    return pl.pallas_call(
        kernel,
        in_specs=[pl.BlockSpec(memory_space=pltpu.SMEM)]
        + [pl.BlockSpec(memory_space=pltpu.VMEM)] * 3,
        out_shape=jax.ShapeDtypeStruct((8, D), F32),
        scratch_shapes=[
            pltpu.VMEM((16, 3 * D), BF16),
            pltpu.VMEM((LO, groups * D), BF16),
            pltpu.VMEM((D, D), BF16),
            pltpu.VMEM((16, D), F32),
        ],
        compiler_params=pltpu.CompilerParams(vmem_limit_bytes=48 * 1024 * 1024),
        name="points_back",
    )(held, recv, par, cell_grads)


def update(total, params, first_moment, second_moment):
    rows = params.shape[0]
    moves = [
        (2 * GRAD_ROWS + 72, 0, 6),
        (2 * GRAD_ROWS, 6, 65),
        (GRAD_ROWS, POINT_ROWS, LAYER_ROWS),
        (0, POINT_ROWS + LAYER_ROWS, LAYER_ROWS),
    ]

    def kernel(tot, par, mom1, mom2, norm_ref, new_par, new1, new2, low, rms, grad):
        for src, dst, length in moves:
            grad[pl.ds(dst, length), :] = tot[pl.ds(src, length), :].astype(F32)
        g = grad[...]
        norm = jnp.sqrt(jnp.sum(g * g))
        norm_ref[0, 0] = norm
        factor = jnp.minimum(1.0, clip_norm / (norm + 1e-06))
        clipped = g * factor
        first = beta_one * mom1[...] + (1.0 - beta_one) * clipped
        second = beta_two * mom2[...] + (1.0 - beta_two) * clipped * clipped
        new1[...] = first
        new2[...] = second
        first_hat = first / (1.0 - beta_one**step_count)
        second_hat = second / (1.0 - beta_two**step_count)
        p = par[...]
        p = p - learn_rate * (first_hat / (jnp.sqrt(second_hat) + adam_eps) + decay_rate * p)
        new_par[...] = p
        low[...] = p.astype(BF16)
        base = 2 * GRAD_ROWS + 80
        stats = tot[base : base + 8, :].astype(F32)
        sums = jnp.sum(stats, axis=1, keepdims=True)
        live = jnp.maximum(sums[6:7], 1.0)
        rms[...] = jnp.broadcast_to(jnp.sqrt(sums / (live * D)), (8, D))

    shape = jax.ShapeDtypeStruct
    flat = shape((rows, D), F32)
    return pl.pallas_call(
        kernel,
        out_specs=[pl.BlockSpec(memory_space=pltpu.SMEM)]
        + [pl.BlockSpec(memory_space=pltpu.VMEM)] * 5,
        out_shape=[shape((1, 1), F32), flat, flat, flat, shape((rows, D), BF16), shape((8, D), F32)],
        scratch_shapes=[pltpu.VMEM((rows, D), F32)],
        compiler_params=pltpu.CompilerParams(vmem_limit_bytes=48 * 1024 * 1024),
        name="update",
    )(total, params, first_moment, second_moment)


def shifted(x, axes, by):
    if len(axes) == 1:
        count = lax.axis_size(axes[0])
        return lax.ppermute(x, axes[0], [(i, (i + by) % count) for i in range(count)])
    tiles, rows = lax.axis_size(axes[0]), lax.axis_size(axes[1])
    pairs = [
        (i * rows + j, (i + by) % tiles * rows + (j + by) % rows)
        for i in range(tiles)
        for j in range(rows)
    ]
    return lax.ppermute(x, axes, pairs)


def exchange(row, col, cor, by):
    return (
        shifted(row, ("tile",), by),
        shifted(col, ("row",), by),
        shifted(cor, ("tile", "row"), by),
    )


def by_quads(grid, quads_x, quads_y):
    trailing = grid.shape[2:]
    grid = grid.reshape((quads_x, QS, quads_y, QS) + trailing)
    return jnp.swapaxes(grid, 1, 2).reshape((quads_x, quads_y, QC) + trailing)


def reduce_all(x):
    tiles, rows = lax.axis_size("tile"), lax.axis_size("row")
    count = tiles * rows
    share = x.shape[0] // count
    parts = lax.all_to_all(
        x.reshape(count, share, D), ("tile", "row"), split_axis=0, concat_axis=0, tiled=True
    )
    mine = jnp.sum(parts.astype(F32), axis=0).astype(x.dtype)
    spread = jnp.broadcast_to(mine[None], (count, share, D))
    return lax.all_to_all(
        spread, ("tile", "row"), split_axis=0, concat_axis=0, tiled=True
    ).reshape(x.shape)


def local(
    point_feats,
    point_tile,
    point_cell,
    point_valid,
    pillar_frame,
    cotangent,
    params,
    first_moment,
    second_moment,
):
    tile_count = lax.axis_size("tile")
    row_count = lax.axis_size("row")
    device_count = tile_count * row_count
    extent_x, extent_y = pillar_frame.shape
    cell_count = extent_x * extent_y
    quads_x, quads_y = extent_x // QS, extent_y // QS
    quads = quads_x * quads_y
    points = point_cell.shape[0]
    capacity = 2 * points // tile_count
    par = params.reshape(-1, D)

    cot = by_quads(cotangent, quads_x, quads_y)
    cot_halos = exchange(cot[0], cot[:, 0], cot[0, :1], -1)

    shape = (points // BLOCK, BLOCK)
    send = bin_points(
        point_feats,
        point_tile.reshape(shape),
        point_cell.reshape(shape),
        point_valid.reshape(shape),
        tile_count,
        capacity,
        extent_y,
        quads_y,
    )
    recv = lax.all_to_all(send, "tile", split_axis=0, concat_axis=0, tiled=True)
    held = jnp.sum(recv[:, 11].astype(jnp.int32), axis=1)

    frames = by_quads(pillar_frame, quads_x, quads_y)
    frames = jnp.pad(frames, ((0, 0), (0, 0), (0, QP - QC)), constant_values=-1).reshape(-1)
    lanes = jnp.arange(D, dtype=jnp.int32)
    base_rows = (frames[:, None] == lanes[None] - (H1 + 1)).astype(F32)
    pillars, tags = encode_points(recv, held, par, base_rows, quads)
    pillars = pillars.reshape(quads_x, quads_y, QP, D)
    tags = tags.reshape(quads_x, quads_y, QC, D)
    tag_halos = exchange(tags[0], tags[:, 0], tags[0, :1], -1)

    first = first_layer(pillars, par, quads_x, quads_y)
    field, saved, sums_one = first[0], first[1:8], first[8]
    halos = exchange(*first[9:], -1)
    flags = jnp.stack(
        [
            (lax.axis_index("tile") == tile_count - 1).astype(jnp.int32),
            (lax.axis_index("row") == row_count - 1).astype(jnp.int32),
        ]
    )
    grads, grad_two, g_row, g_col, g_cor, sums_two = second_layer(
        flags, field, halos, tags, tag_halos, cot, cot_halos, par, 1.0 / (cell_count * device_count)
    )
    grad_halos = exchange(g_row, g_col, g_cor, 1)
    cell_grads, grad_one, grad_pout = first_layer_back(grads, grad_halos, pillars, saved, par)
    grad_pin = points_back(recv, held, par, cell_grads.reshape(quads * QP, D))

    stats = jnp.concatenate(
        [
            jnp.sum(sums_one, axis=1)[:3],
            jnp.sum(sums_two, axis=1)[:3],
            jnp.sum(sums_one, axis=1)[3:] / D,
            jnp.zeros((1, D), F32),
        ],
        axis=0,
    )
    pieces = jnp.concatenate([grad_two, grad_one, grad_pout, grad_pin, stats], axis=0)
    step = device_count * 8
    pieces = jnp.pad(pieces, ((0, -pieces.shape[0] % step), (0, 0)))
    total = reduce_all(pieces)
    norm, new_params, new_first, new_second, low, rms = update(
        total, par, first_moment.reshape(-1, D), second_moment.reshape(-1, D)
    )
    return (
        norm[0, 0],
        new_params.reshape(-1),
        new_first.reshape(-1),
        new_second.reshape(-1),
        low.reshape(-1),
        rms[:6, 0],
    )


def solution(mesh):
    return jax.shard_map(
        local,
        mesh=mesh,
        in_specs=(
            P(None, ("tile", "row")),
            P(("tile", "row"), None),
            P(("tile", "row")),
            P(("tile", "row")),
            P("tile", "row"),
            P("tile", "row", None),
            P(),
            P(),
            P(),
        ),
        out_specs=(P(), P(), P(), P(), P(), P()),
        check_vma=False,
    )
```

```python
import jax
import jax.numpy as jnp
from jax import lax
from jax.experimental import pallas as pl
from jax.experimental.pallas import tpu as pltpu
from jax.sharding import PartitionSpec as P

D = 128
HEADS = 8
HD = 16
FF = 256
H1 = 64
WIN = 12
C_IN = 11
QS = 6
QC = 36
QP = 40
SLOTS = 144
KEYS = HEADS * SLOTS
LAYER_ROWS = 1034
POINT_ROWS = 71
GRAD_ROWS = 1040
BLOCK = 256
CHUNK = 512
LO = 512
NW = 2

clip_norm = 0.01
beta_one = 0.9
beta_two = 0.999
step_count = 10
learn_rate = 0.1
decay_rate = 0.05
adam_eps = 1e-08

F32 = jnp.float32
BF16 = jnp.bfloat16
GELU_C = 0.7978845608028654
GELU_A = 0.044715


def mm(a, b):
    return lax.dot_general(a, b, (((1,), (0,)), ((), ())), preferred_element_type=F32)


def mm_nt(a, b):
    return lax.dot_general(a, b, (((1,), (1,)), ((), ())), preferred_element_type=F32)


def mm_tn(a, b):
    return lax.dot_general(a, b, (((0,), (0,)), ((), ())), preferred_element_type=F32)


def lane_iota(rows=1):
    return lax.broadcasted_iota(jnp.int32, (rows, D), 1)


def part8(v):
    return jnp.sum(v.reshape(v.shape[0] // 8, 8, v.shape[1]), axis=0)


def gelu_parts(v):
    sq = v * v
    t = jnp.tanh(v * (GELU_C + (GELU_C * GELU_A) * sq))
    half = 0.5 + 0.5 * t
    slope = half + (0.5 * v) * (1.0 - t * t) * (GELU_C + (3.0 * GELU_C * GELU_A) * sq)
    return v * half, slope


def gelu_only(v):
    t = jnp.tanh(v * (GELU_C + (GELU_C * GELU_A) * (v * v)))
    return v * (0.5 + 0.5 * t)


def normalize(y):
    center = y - jnp.mean(y, axis=-1, keepdims=True)
    rs = lax.rsqrt(jnp.mean(center * center, axis=-1, keepdims=True) + 1e-05)
    return center * rs, rs


def norm_pull(gx, xhat, rs):
    return rs * (
        gx
        - jnp.mean(gx, axis=-1, keepdims=True)
        - xhat * jnp.mean(gx * xhat, axis=-1, keepdims=True)
    )


def load_layer(par, base, w):
    for part in range(3):
        m = par[pl.ds(base + part, D, stride=3), :]
        w["qkv"][:, part * D : (part + 1) * D] = m.astype(BF16)
        if "qkv_t" in w:
            w["qkv_t"][part * D : (part + 1) * D, :] = m.T.astype(BF16)
    m = par[pl.ds(base + 384, D), :]
    w["out"][...] = m.astype(BF16)
    if "out_t" in w:
        w["out_t"][...] = m.T.astype(BF16)
    for part in range(2):
        m = par[pl.ds(base + 512 + part, D, stride=2), :]
        w["fin"][:, part * D : (part + 1) * D] = m.astype(BF16)
        if "fin_t" in w:
            w["fin_t"][part * D : (part + 1) * D, :] = m.T.astype(BF16)
        m = par[pl.ds(base + 768 + part * D, D), :]
        w["fout"][part * D : (part + 1) * D, :] = m.astype(BF16)
        if "fout_t" in w:
            w["fout_t"][:, part * D : (part + 1) * D] = m.T.astype(BF16)


WEIGHT_SHAPES = {
    "qkv": (D, 3 * D),
    "qkv_t": (3 * D, D),
    "out": (D, D),
    "out_t": (D, D),
    "fin": (D, FF),
    "fin_t": (FF, D),
    "fout": (FF, D),
    "fout_t": (D, FF),
}


def vec(par, base, row):
    return par[base + 1024 + row : base + 1025 + row, :]


def vec2(par, base, row):
    return jnp.concatenate([vec(par, base, row), vec(par, base, row + 1)], axis=1)


def head_lanes():
    return lane_iota() // HD


def head_rows(m):
    lanes = head_lanes()
    keep = [jnp.where(lanes == h, 1.0, 0.0).astype(BF16) for h in range(HEADS)]
    top = m[:D]
    rest = m[D:]
    return jnp.concatenate([top * k for k in keep] + [rest * k for k in keep], axis=0)


def window_bias(groups):
    keys = jnp.concatenate(
        [groups[:D]] + [groups[D:]] * HEADS + [jnp.ones((D, D), BF16)], axis=0
    )
    same = mm_nt(groups, keys)
    rows = lax.broadcasted_iota(jnp.int32, (SLOTS, D), 0)
    lanes = lane_iota(SLOTS)
    first = (same[:, :D] > 0.5) | (rows == lanes)
    last = (same[:, D : 2 * D] > 0.5) | (rows == lanes % HD + D)
    return (
        jnp.where(first, 0.0, -1000000000.0),
        jnp.where(last, 0.0, -1000000000.0),
        same[:, 2 * D :],
    )


def attend(qs, key, val, bias_first, bias_last):
    scores = mm_nt(key, head_rows(qs))
    probs = []
    for h in range(HEADS + 1):
        part = scores[:, h * D : (h + 1) * D] + (bias_first if h < HEADS else bias_last)
        expo = jnp.exp(part - jnp.max(part, axis=0, keepdims=True))
        probs.append((expo * (1.0 / jnp.sum(expo, axis=0, keepdims=True))).astype(BF16))
    probs = jnp.concatenate(probs, axis=1)
    return probs, query_pull(val, probs)


def attend_pull(probs, qs, key, val, gmix):
    rows = head_rows(gmix)
    pulled = mm_nt(val, rows)
    gs = []
    for h in range(HEADS + 1):
        cols = slice(h * D, (h + 1) * D)
        p = probs[:, cols].astype(F32)
        both = p * pulled[:, cols]
        gs.append((both - p * jnp.sum(both, axis=0, keepdims=True)).astype(BF16))
    gs = jnp.concatenate(gs, axis=1)
    return query_pull(key * 0.25, gs), mm(gs, head_rows(qs)).astype(BF16), mm(probs, rows).astype(BF16)


def query_pull(rows, cols):
    full = mm_tn(rows, cols)
    top = jnp.concatenate(
        [full[h * HD : (h + 1) * HD, h * D : (h + 1) * D] for h in range(HEADS)], axis=0
    )
    chan = lax.broadcasted_iota(jnp.int32, (D, D), 0)
    lanes = lane_iota(D)
    rest = jnp.where(chan // HD == lanes // HD, full[:, HEADS * D :], 0.0).astype(BF16)
    fold = jnp.where(
        lax.broadcasted_iota(jnp.int32, (HD, D), 0) == lane_iota(HD) % HD, 1.0, 0.0
    ).astype(BF16)
    return jnp.concatenate([top.T.astype(BF16), mm_nt(fold, rest).astype(BF16)], axis=0)


def split_qkv(packed, w):
    rows = slice(w * SLOTS, (w + 1) * SLOTS)
    return packed[rows, :D] * 0.25, packed[rows, D : 2 * D], packed[rows, 2 * D :]


def layer_forward(x, groups, par, base, w, sums):
    count = x.shape[0] // SLOTS
    low = x.astype(BF16)
    qkv_bias = jnp.concatenate(
        [vec(par, base, 0), jnp.zeros((1, D), F32), vec(par, base, 1)], axis=1
    )
    packed = (mm(low, w["qkv"][...]) + qkv_bias).astype(BF16)
    probs, mixes, lives = [], [], []
    for i in range(count):
        bias_first, bias_last, live = window_bias(groups[i])
        qs, key, val = split_qkv(packed, i)
        prob, mix = attend(qs, key, val, bias_first, bias_last)
        probs.append(prob)
        mixes.append(mix)
        lives.append(live)
    mix = jnp.concatenate(mixes, axis=0)
    live = jnp.concatenate(lives, axis=0)
    attn_out = mm(mix, w["out"][...]) + vec(par, base, 2)
    first = x + attn_out
    xhat1, rs1 = normalize(first)
    normed = (xhat1 * vec(par, base, 3) + vec(par, base, 4)) * live
    normed_low = normed.astype(BF16)
    pre = mm(normed_low, w["fin"][...]) + vec2(par, base, 5)
    act, slope = gelu_parts(pre)
    hidden = act.astype(BF16)
    ffn = mm(hidden, w["fout"][...]) + vec(par, base, 7)
    second = normed + ffn
    xhat2, rs2 = normalize(second)
    result = (xhat2 * vec(par, base, 8) + vec(par, base, 9)) * live
    sums[0] += part8(attn_out * attn_out * live)
    sums[1] += part8(ffn * ffn * live)
    sums[2] += part8(result * result)
    sums[3] += part8(live)
    return dict(
        low=low,
        packed=packed,
        probs=probs,
        mix=mix,
        live=live,
        first=first,
        second=second,
        xhat1=xhat1,
        rs1=rs1,
        xhat2=xhat2,
        rs2=rs2,
        normed_low=normed_low,
        slope=slope,
        hidden=hidden,
        result=result,
    )


def layer_backward(grad, k, par, base, w, acc):
    live = k["live"]
    gl = grad * live
    acc["vec"][8] += part8(gl * k["xhat2"])
    acc["vec"][9] += part8(gl)
    g2 = norm_pull(gl * vec(par, base, 8), k["xhat2"], k["rs2"])
    g_ffn = g2.astype(BF16)
    acc["fout"][...] += mm_tn(k["hidden"], g_ffn)
    acc["vec"][7] += part8(g_ffn.astype(F32))
    g_pre = (mm(g_ffn, w["fout_t"][...]) * k["slope"]).astype(BF16)
    acc["fin"][...] += mm_tn(k["normed_low"], g_pre)
    for part in range(2):
        acc["vec"][5 + part] += part8(g_pre[:, part * D : (part + 1) * D].astype(F32))
    g_norm = (g2 + mm(g_pre, w["fin_t"][...])) * live
    acc["vec"][3] += part8(g_norm * k["xhat1"])
    acc["vec"][4] += part8(g_norm)
    g1 = norm_pull(g_norm * vec(par, base, 3), k["xhat1"], k["rs1"])
    g_attn = g1.astype(BF16)
    acc["out"][...] += mm_tn(k["mix"], g_attn)
    acc["vec"][2] += part8(g_attn.astype(F32))
    g_mix = mm(g_attn, w["out_t"][...]).astype(BF16)
    pieces = []
    for i in range(grad.shape[0] // SLOTS):
        rows = slice(i * SLOTS, (i + 1) * SLOTS)
        qs, key, val = split_qkv(k["packed"], i)
        pieces.append(
            jnp.concatenate(
                attend_pull(k["probs"][i], qs, key, val, g_mix[rows]), axis=1
            )
        )
    g_packed = jnp.concatenate(pieces, axis=0)
    acc["qkv"][...] += mm_tn(k["low"], g_packed)
    acc["vec"][0] += part8(g_packed[:, :D].astype(F32))
    acc["vec"][1] += part8(g_packed[:, 2 * D :].astype(F32))
    return g1 + mm(g_packed, w["qkv_t"][...])


ACC_SHAPES = {
    "qkv": (D, 3 * D),
    "out": (D, D),
    "fin": (D, FF),
    "fout": (FF, D),
    "vec": (10, 8, D),
}


def clear(acc):
    for ref in acc.values():
        ref[...] = jnp.zeros(ref.shape, ref.dtype)


def store_grads(acc, sums, out):
    for part in range(3):
        out[pl.ds(part, D, stride=3), :] = acc["qkv"][:, part * D : (part + 1) * D]
    out[pl.ds(384, D), :] = acc["out"][...]
    for part in range(2):
        out[pl.ds(512 + part, D, stride=2), :] = acc["fin"][:, part * D : (part + 1) * D]
    out[pl.ds(768, FF), :] = acc["fout"][...]
    out[pl.ds(1024, 16), :] = jnp.concatenate(
        [jnp.sum(acc["vec"][i], axis=0, keepdims=True) for i in range(10)]
        + [jnp.sum(sums[i], axis=0, keepdims=True) for i in range(4)]
        + [jnp.zeros((2, D), F32)],
        axis=0,
    )


def gather_windows(scratch, pick):
    for i in range(NW):
        for r in range(2):
            for c in range(2):
                at = i * SLOTS + (2 * r + c) * QC
                scratch[pl.ds(at, QC), :] = pick(r, 2 * i + c)
    return scratch[...]


def spread_windows(scratch, value, put):
    scratch[...] = value
    for i in range(NW):
        for r in range(2):
            for c in range(2):
                put(r, 2 * i + c, scratch[pl.ds(i * SLOTS + (2 * r + c) * QC, QC), :])


def whole(shape, space=pltpu.VMEM):
    return pl.BlockSpec(shape, lambda *_: (0,) * len(shape), memory_space=space)


def params_for(limit=56):
    return pltpu.CompilerParams(
        dimension_semantics=("arbitrary",), vmem_limit_bytes=limit * 1024 * 1024
    )


def cost_of(flops):
    return pl.CostEstimate(flops=flops, bytes_accessed=1 << 24, transcendentals=0)


def first_layer(pillars, par, quads_x, quads_y):
    across = quads_x // 2
    along = quads_y // (2 * NW)
    windows = quads_x * quads_y // 4
    base = POINT_ROWS

    def kernel(pil, par_ref, *refs):
        outs, scratch = refs[:12], refs[12:]
        (
            field,
            probs_out,
            packed_out,
            mix_out,
            first_out,
            second_out,
            low_out,
            live_out,
            sums_out,
            row_out,
            col_out,
            cor_out,
        ) = outs
        names = ["qkv", "out", "fin", "fout"]
        w = dict(zip(names, scratch[:4]))
        wide, pout, sums = scratch[4:]
        step = pl.program_id(0)
        a = step // along
        b = step % along

        @pl.when(step == 0)
        def _():
            load_layer(par_ref, base, w)
            m = par_ref[pl.ds(6, H1), :].astype(BF16)
            pout[...] = jnp.concatenate([m, m], axis=0)
            sums[...] = jnp.zeros(sums.shape, F32)

        cells = gather_windows(wide, lambda r, c: pil[r, c, :QC, :])
        lanes = lane_iota()
        total = jnp.where(lanes < H1, cells, 0.0)
        count = cells[:, H1 : H1 + 1]
        high = total.astype(BF16).astype(F32)
        both = (high + pltpu.roll(total - high, H1, axis=1)).astype(BF16)
        pillar = mm(both, pout[...]) + count * par_ref[70:71, :]
        x = pillar / jnp.maximum(count, 1.0)
        onehot = jnp.where((lanes > H1) & (lanes < H1 + 4) & (count > 0.0), cells, 0.0).astype(BF16)
        groups = [onehot[i * SLOTS : (i + 1) * SLOTS] for i in range(NW)]
        k = layer_forward(x, groups, par_ref, base, w, sums)
        for i in range(NW):
            rows = slice(i * SLOTS, (i + 1) * SLOTS)
            probs_out[i] = k["probs"][i]
            packed_out[i] = k["packed"][rows]
            mix_out[i] = k["mix"][rows]
            first_out[i] = k["first"][rows]
            second_out[i] = k["second"][rows]
            low_out[i] = k["low"][rows]
            live_out[i] = k["live"][rows]

        def put(r, c, v):
            field[r, c, :QC, :] = v

        spread_windows(wide, k["result"], put)

        @pl.when(a == 0)
        def _():
            for c in range(2 * NW):
                row_out[c] = field[0, c, :QC, :].astype(BF16)

        @pl.when(b == 0)
        def _():
            for r in range(2):
                col_out[r] = field[r, 0, :QC, :].astype(BF16)

        @pl.when(step == 0)
        def _():
            cor_out[0] = field[0, 0, :QC, :].astype(BF16)

        @pl.when(step == pl.num_programs(0) - 1)
        def _():
            sums_out[...] = sums[...]

    def win_spec(width):
        return pl.BlockSpec((NW, SLOTS, width), lambda s: (s, 0, 0))

    quad_spec = pl.BlockSpec((2, 2 * NW, QP, D), lambda s: (s // along, s % along, 0, 0))
    shape = jax.ShapeDtypeStruct
    return pl.pallas_call(
        kernel,
        grid=(across * along,),
        in_specs=[quad_spec, whole(par.shape)],
        out_specs=[
            quad_spec,
            win_spec(KEYS),
            win_spec(3 * D),
            win_spec(D),
            win_spec(D),
            win_spec(D),
            win_spec(D),
            win_spec(D),
            whole((4, 8, D)),
            pl.BlockSpec((2 * NW, QC, D), lambda s: (jnp.minimum(s, along - 1), 0, 0)),
            pl.BlockSpec((2, QC, D), lambda s: (s // along, 0, 0)),
            whole((1, QC, D)),
        ],
        out_shape=[
            shape((quads_x, quads_y, QP, D), F32),
            shape((windows, SLOTS, KEYS), BF16),
            shape((windows, SLOTS, 3 * D), BF16),
            shape((windows, SLOTS, D), BF16),
            shape((windows, SLOTS, D), F32),
            shape((windows, SLOTS, D), F32),
            shape((windows, SLOTS, D), BF16),
            shape((windows, SLOTS, D), F32),
            shape((4, 8, D), F32),
            shape((quads_y, QC, D), BF16),
            shape((quads_x, QC, D), BF16),
            shape((1, QC, D), BF16),
        ],
        scratch_shapes=[pltpu.VMEM(WEIGHT_SHAPES[n], BF16) for n in ["qkv", "out", "fin", "fout"]]
        + [
            pltpu.VMEM((NW * SLOTS, D), F32),
            pltpu.VMEM((D, D), BF16),
            pltpu.VMEM((4, 8, D), F32),
        ],
        compiler_params=params_for(),
        name="first_layer",
    )(pillars, par)


def second_layer(flags, field, halos, tags, tag_halos, cot, cot_halos, par, scale, grad_rows):
    quads_x, quads_y = field.shape[:2]
    across = quads_x // 2
    along = quads_y // (2 * NW)
    base = POINT_ROWS + LAYER_ROWS
    wnames = list(WEIGHT_SHAPES)
    anames = list(ACC_SHAPES)

    def kernel(flag, *refs):
        ins, refs = refs[:13], refs[13:]
        outs, scratch = refs[:5], refs[5:]
        fields, tagss, cots, par_ref = ins[:4], ins[4:8], ins[8:12], ins[12]
        grads, weights, row_out, col_out, cor_out = outs
        w = dict(zip(wnames, scratch))
        scratch = scratch[len(wnames) :]
        acc = dict(zip(anames, scratch))
        wide, sums, ext_x, ext_t, ext_g = scratch[len(anames) :]
        step = pl.program_id(0)
        a = step // along
        b = step % along

        @pl.when(step == 0)
        def _():
            load_layer(par_ref, base, w)
            sums[...] = jnp.zeros(sums.shape, F32)
            clear(acc)
            lanes = lane_iota()

            def moved(v, region):
                return pltpu.roll(v, 3 * region, axis=1)

            def fill(ext, srcs, turn_row, turn_col, turn_cor):
                main, row, col, cor = srcs

                def one(i, _):
                    ext[i // quads_y, i % quads_y, :QC, :] = main[
                        i // quads_y, i % quads_y, :QC, :
                    ].astype(F32)
                    return 0

                lax.fori_loop(0, quads_x * quads_y, one, 0, unroll=4)

                def one_row(i, _):
                    ext[quads_x, i, :QC, :] = turn_row(row[i].astype(F32))
                    return 0

                lax.fori_loop(1, quads_y, one_row, 0)
                for i in range(1, quads_x):
                    ext[i, quads_y, :QC, :] = turn_col(col[i].astype(F32))
                ext[quads_x, quads_y, :QC, :] = turn_cor(cor[0].astype(F32))

            def same(v):
                return v

            last_x = flag[0] > 0
            last_y = flag[1] > 0

            def tag_row(v):
                return jnp.where(last_x, moved(v, 2), v)

            def tag_col(v):
                return jnp.where(last_y, moved(v, 1), v)

            fill(ext_x, fields, same, same, same)
            fill(ext_t, tagss, tag_row, tag_col, lambda v: tag_row(tag_col(v)))
            fill(ext_g, cots, same, same, same)

        def picker(ext):
            return lambda r, c: ext[2 * a + 1 + r, 2 * NW * b + 1 + c, :QC, :]

        tag = gather_windows(wide, picker(ext_t)).astype(BF16)
        groups = [tag[i * SLOTS : (i + 1) * SLOTS] for i in range(NW)]
        x = gather_windows(wide, picker(ext_x))
        k = layer_forward(x, groups, par_ref, base, w, sums)
        grad = gather_windows(wide, picker(ext_g)) * scale
        gx = layer_backward(grad, k, par_ref, base, w, acc)

        def put(r, c, v):
            grads[r, c, :QC, :] = v

        spread_windows(wide, gx, put)

        @pl.when(a == across - 1)
        def _():
            for c in range(2 * NW):
                row_out[c] = grads[1, c, :QC, :].astype(BF16)

        @pl.when(b == along - 1)
        def _():
            for r in range(2):
                col_out[r] = grads[r, 2 * NW - 1, :QC, :].astype(BF16)

        @pl.when(step == pl.num_programs(0) - 1)
        def _():
            cor_out[0] = grads[1, 2 * NW - 1, :QC, :].astype(BF16)
            store_grads(acc, sums, weights)

    shape = jax.ShapeDtypeStruct
    quad_spec = pl.BlockSpec((2, 2 * NW, QP, D), lambda s: (s // along, s % along, 0, 0))
    ext = pltpu.VMEM((quads_x + 1, quads_y + 1, QP, D), F32)
    arrays = [field, *halos, tags, *tag_halos, cot, *cot_halos, par]
    return pl.pallas_call(
        kernel,
        grid=(across * along,),
        in_specs=[pl.BlockSpec(memory_space=pltpu.SMEM)] + [whole(v.shape) for v in arrays],
        out_specs=[
            quad_spec,
            whole((grad_rows, D)),
            pl.BlockSpec(
                (2 * NW, QC, D), lambda s: (jnp.maximum(s - (across - 1) * along, 0), 0, 0)
            ),
            pl.BlockSpec((2, QC, D), lambda s: (s // along, 0, 0)),
            whole((1, QC, D)),
        ],
        out_shape=[
            shape((quads_x, quads_y, QP, D), F32),
            shape((grad_rows, D), F32),
            shape((quads_y, QC, D), BF16),
            shape((quads_x, QC, D), BF16),
            shape((1, QC, D), BF16),
        ],
        scratch_shapes=[pltpu.VMEM(WEIGHT_SHAPES[n], BF16) for n in wnames]
        + [pltpu.VMEM(ACC_SHAPES[n], F32) for n in anames]
        + [
            pltpu.VMEM((NW * SLOTS, D), F32),
            pltpu.VMEM((4, 8, D), F32),
            ext,
            ext,
            ext,
        ],
        compiler_params=params_for(),
        name="second_layer",
    )(flags, *arrays)


def first_layer_back(grads, halos, pillars, saved, sums, par, grad_rows):
    quads_x, quads_y = grads.shape[:2]
    across = quads_x // 2
    along = quads_y // (2 * NW)
    base = POINT_ROWS
    wnames = list(WEIGHT_SHAPES)
    anames = list(ACC_SHAPES)

    def kernel(*refs):
        ins, refs = refs[:14], refs[14:]
        outs, scratch = refs[:2], refs[2:]
        main, row, col, cor, pil = ins[:5]
        probs, packed, mix, first, second, low, live = ins[5:12]
        sums_ref, par_ref = ins[12:]
        cell_out, weights = outs
        w = dict(zip(wnames, scratch))
        scratch = scratch[len(wnames) :]
        acc = dict(zip(anames, scratch))
        wide, ext, pout_t, pacc = scratch[len(anames) :]
        step = pl.program_id(0)
        a = step // along
        b = step % along

        @pl.when(step == 0)
        def _():
            load_layer(par_ref, base, w)
            clear(acc)
            pacc[...] = jnp.zeros(pacc.shape, F32)
            m = par_ref[pl.ds(6, H1), :]
            pout_t[...] = jnp.concatenate([m, m], axis=0).T.astype(BF16)
            for r in range(1, quads_x):

                def one(i, _):
                    ext[r, i, :QC, :] = main[r - 1, i - 1, :QC, :]
                    return 0

                lax.fori_loop(1, quads_y, one, 0)
                ext[r, 0, :QC, :] = col[r - 1].astype(F32)

            def one_row(i, _):
                ext[0, i, :QC, :] = row[i - 1].astype(F32)
                return 0

            lax.fori_loop(1, quads_y, one_row, 0)
            ext[0, 0, :QC, :] = cor[0].astype(F32)

        grad = gather_windows(wide, lambda r, c: ext[2 * a + r, 2 * NW * b + c, :QC, :])

        def rows_of(ref):
            return jnp.concatenate([ref[i] for i in range(NW)], axis=0)

        k = dict(
            low=rows_of(low),
            packed=rows_of(packed),
            probs=[probs[i] for i in range(NW)],
            mix=rows_of(mix),
            live=rows_of(live),
        )
        k["xhat1"], k["rs1"] = normalize(rows_of(first))
        k["xhat2"], k["rs2"] = normalize(rows_of(second))
        normed = (k["xhat1"] * vec(par_ref, base, 3) + vec(par_ref, base, 4)) * k["live"]
        k["normed_low"] = normed.astype(BF16)
        act, k["slope"] = gelu_parts(mm(k["normed_low"], w["fin"][...]) + vec2(par_ref, base, 5))
        k["hidden"] = act.astype(BF16)
        gx = layer_backward(grad, k, par_ref, base, w, acc)

        cells = gather_windows(wide, lambda r, c: pil[r, c, :QC, :])
        lanes = lane_iota()
        total = jnp.where(lanes <= H1, cells, 0.0)
        g_pillar = (gx / jnp.maximum(cells[:, H1 : H1 + 1], 1.0)).astype(BF16)
        high = total.astype(BF16)
        rest = (total - high.astype(F32)).astype(BF16)
        pacc[...] += mm_tn(high, g_pillar) + mm_tn(rest, g_pillar)

        def put(r, c, v):
            cell_out[r, c, :QC, :] = v
            cell_out[r, c, QC:, :] = jnp.zeros((QP - QC, D), F32)

        spread_windows(wide, mm(g_pillar, pout_t[...]), put)

        @pl.when(step == pl.num_programs(0) - 1)
        def _():
            store_grads(acc, sums_ref, weights)
            weights[GRAD_ROWS : GRAD_ROWS + 72, :] = pacc[:72, :]

    def win_spec(width):
        return pl.BlockSpec((NW, SLOTS, width), lambda s: (s, 0, 0))

    shape = jax.ShapeDtypeStruct
    quad_spec = pl.BlockSpec((2, 2 * NW, QP, D), lambda s: (s // along, s % along, 0, 0))
    return pl.pallas_call(
        kernel,
        grid=(across * along,),
        in_specs=[whole(grads.shape)]
        + [whole(v.shape) for v in halos]
        + [quad_spec]
        + [win_spec(v.shape[2]) for v in saved]
        + [whole(sums.shape), whole(par.shape)],
        out_specs=[quad_spec, whole((grad_rows, D))],
        out_shape=[shape((quads_x, quads_y, QP, D), F32), shape((grad_rows, D), F32)],
        scratch_shapes=[pltpu.VMEM(WEIGHT_SHAPES[n], BF16) for n in wnames]
        + [pltpu.VMEM(ACC_SHAPES[n], F32) for n in anames]
        + [
            pltpu.VMEM((NW * SLOTS, D), F32),
            pltpu.VMEM((quads_x, quads_y, QP, D), F32),
            pltpu.VMEM((D, D), BF16),
            pltpu.VMEM((D, D), F32),
        ],
        compiler_params=params_for(),
        cost_estimate=cost_of(grads.size * 12000),
        name="first_layer_back",
    )(grads, *halos, pillars, *saved, sums, par)


def one_hot(hit):
    return jnp.where(hit, 1.0, 0.0).astype(BF16)


def bin_points(feats, tiles, cells, valid, tile_count, capacity, extent_y, quads_y):
    blocks = tiles.shape[0]
    groups = tile_count * capacity // LO
    lots = 4
    wide = lots * BLOCK

    def kernel(feat_ref, tile_ref, cell_ref, valid_ref, out_ref, slot_ref, code_ref, acc):
        real = valid_ref[...] > 0
        t = jnp.where(real, tile_ref[...], tile_count)
        i0 = lax.broadcasted_iota(jnp.int32, (BLOCK, BLOCK), 0)
        i1 = lax.broadcasted_iota(jnp.int32, (BLOCK, BLOCK), 1)
        upto = one_hot(i0 <= i1)
        j0 = lax.broadcasted_iota(jnp.int32, (blocks, blocks), 0)
        j1 = lax.broadcasted_iota(jnp.int32, (blocks, blocks), 1)
        earlier = one_hot(j1 < j0)
        slot = jnp.full((blocks, BLOCK), -1.0, F32)
        for k in range(tile_count):
            hit = t == k
            run = mm(one_hot(hit), upto)
            total = jnp.broadcast_to(run[:, BLOCK - 1 :], (blocks, D)).astype(BF16)
            at = mm(earlier, total)[:, :1] + (k * capacity - 1.0)
            slot = jnp.where(hit, run + at, slot)
        slot_ref[...] = slot.astype(jnp.int32)

        def part(v, by):
            return ((v.astype(F32) + 0.5) * (1.0 / by)).astype(jnp.int32)

        cell = cell_ref[...]
        cx = part(cell, extent_y)
        cy = cell - cx * extent_y
        qx, qy = part(cx, QS), part(cy, QS)
        row = (qx * quads_y + qy) * QP + (cx - qx * QS) * QS + (cy - qy * QS)
        hi = row // LO
        lo = row - hi * LO
        low_part = lo % 256
        code_ref[0] = jnp.where(real, 1.0, 0.0)
        code_ref[1] = (hi + 1).astype(F32)
        code_ref[2] = (lo - low_part).astype(F32)
        code_ref[3] = low_part.astype(F32)
        acc[...] = jnp.zeros(acc.shape, F32)
        span = lax.broadcasted_iota(jnp.int32, (LO, wide), 0)

        def one(j, _):
            def line(ref, *lead):
                return jnp.concatenate(
                    [ref[(*lead, pl.ds(j * lots + u, 1), slice(None))] for u in range(lots)], axis=1
                )

            at = line(slot_ref)
            feat = feat_ref[:, pl.ds(pl.multiple_of(j * wide, wide), wide)].astype(F32)
            rows = jnp.concatenate(
                [feat] + [line(code_ref, i) for i in range(4)] + [jnp.zeros((1, wide), F32)], axis=0
            ).astype(BF16)
            group = at // LO
            place = one_hot(span == at % LO)
            spread = jnp.concatenate([rows * one_hot(group == g) for g in range(groups)], axis=0)
            acc[...] += mm_nt(spread, place)
            return 0

        lax.fori_loop(0, blocks // lots, one, 0)
        for k in range(tile_count):
            for at in range(0, capacity, LO):
                g, low = (k * capacity + at) // LO, (k * capacity + at) % LO
                size = min(LO, capacity)
                out_ref[k, :, at : at + size] = acc[g * 16 : g * 16 + 16, low : low + size].astype(
                    BF16
                )

    return pl.pallas_call(
        kernel,
        out_shape=jax.ShapeDtypeStruct((tile_count, 16, capacity), BF16),
        scratch_shapes=[
            pltpu.VMEM((blocks, BLOCK), jnp.int32),
            pltpu.VMEM((4, blocks, BLOCK), F32),
            pltpu.VMEM((groups * 16, LO), F32),
        ],
        compiler_params=pltpu.CompilerParams(vmem_limit_bytes=48 * 1024 * 1024),
        name="bin_points",
    )(feats, tiles, cells, valid)


def unpack_point_in(par_ref, win):
    lanes = lane_iota()
    flat = par_ref[0:6, :]
    turned = pltpu.roll(flat, H1, axis=1)
    even = jnp.where(lanes < H1, flat, turned)
    odd = jnp.where(lanes < H1, turned, flat)
    rows = []
    for k in range(C_IN):
        src = even if k % 2 == 0 else odd
        rows.append(src[k // 2 : k // 2 + 1])
    rows.append(jnp.zeros((5, D), F32))
    win[:, :D] = jnp.concatenate(rows, axis=0).astype(BF16)
    at = lax.broadcasted_iota(jnp.int32, (16, D), 0)
    win[:, D : 2 * D] = one_hot(at == 12)
    win[:, 2 * D :] = one_hot((at == 13) | (at == 14))
    return odd[5:6]


def encode_points(recv, held, par, base_rows, quads):
    sources, _, capacity = recv.shape
    chunk = min(CHUNK, capacity)
    groups = -(-quads * QP // LO)
    pairs = -(-groups // 2)

    def kernel(held_ref, recv_ref, par_ref, base_ref, out_ref, tag_ref, win, acc):
        bias = unpack_point_in(par_ref, win)
        acc[...] = jnp.zeros(acc.shape, F32)
        lanes = lane_iota()
        own = jnp.where(lanes < H1, 1.0, 2.0)
        count_of = (lanes + 1).astype(F32)
        span = lax.broadcasted_iota(jnp.int32, (LO, chunk), 0)

        def source(s, _):
            def piece(j, _):
                cols = recv_ref[s, :, pl.ds(pl.multiple_of(j * chunk, chunk), chunk)]
                wide = cols.astype(F32)
                place = one_hot(span == (wide[13:14] + wide[14:15]).astype(jnp.int32))
                both = mm_tn(cols, win[:, : 2 * D])
                act = gelu_only(both[:, :D] + bias)
                group = both[:, D:]
                spread = [
                    jnp.where(group == own + 2.0 * g, act, 0.0).astype(BF16) for g in range(pairs)
                ]
                spread.append(one_hot(group == count_of))
                acc[...] += mm(place, jnp.concatenate(spread, axis=1))
                return 0

            lax.fori_loop(0, (held_ref[s] + chunk - 1) // chunk, piece, 0)
            return 0

        lax.fori_loop(0, sources, source, 0)
        for g in range(groups):
            rows = min(LO, quads * QP - g * LO)
            v = acc[:rows, g // 2 * D : g // 2 * D + D]
            if g % 2 == 1:
                v = pltpu.roll(v, H1, axis=1)
            count = acc[:rows, pairs * D + g : pairs * D + g + 1]
            v = jnp.where(lanes < H1, v, jnp.where(lanes == H1, count, 0.0))
            out_ref[g * LO : g * LO + rows, :] = v + base_ref[g * LO : g * LO + rows, :]

        def finish(i, _):
            total = out_ref[pl.ds(pl.multiple_of(i * QP, 8), QP), :]
            count = total[:, H1 : H1 + 1]
            tag = jnp.where((lanes > H1) & (lanes < H1 + 4) & (count > 0.0), total, 0.0)
            tag_ref[i] = tag[:QC, :].astype(BF16)
            return 0

        lax.fori_loop(0, quads, finish, 0, unroll=4)

    shape = jax.ShapeDtypeStruct
    return pl.pallas_call(
        kernel,
        in_specs=[pl.BlockSpec(memory_space=pltpu.SMEM)]
        + [pl.BlockSpec(memory_space=pltpu.VMEM)] * 3,
        out_shape=[shape((quads * QP, D), F32), shape((quads, QC, D), BF16)],
        scratch_shapes=[pltpu.VMEM((16, 3 * D), BF16), pltpu.VMEM((LO, (pairs + 1) * D), F32)],
        compiler_params=pltpu.CompilerParams(vmem_limit_bytes=56 * 1024 * 1024),
        name="encode_points",
    )(held, recv, par, base_rows)


def points_back(recv, held, par, cell_grads):
    sources, _, capacity = recv.shape
    chunk = min(CHUNK, capacity)
    total_rows = cell_grads.shape[0]
    groups = -(-total_rows // LO)
    pairs = -(-groups // 2)

    def kernel(held_ref, recv_ref, par_ref, grad_ref, out_ref, win, table, acc):
        bias = unpack_point_in(par_ref, win)
        lanes = lane_iota()

        def rows_of(g):
            rows = max(0, min(LO, total_rows - g * LO))
            got = [grad_ref[g * LO : g * LO + rows, :]] if rows else []
            return jnp.concatenate(got + [jnp.zeros((LO - rows, D), F32)], axis=0) if rows < LO else got[0]

        for j in range(pairs):
            table[:, j * D : j * D + D] = jnp.where(
                lanes < H1, rows_of(2 * j), rows_of(2 * j + 1)
            ).astype(BF16)
        acc[...] = jnp.zeros((16, D), F32)
        own = jnp.where(lanes < H1, 1.0, 2.0)
        spot = lanes.astype(F32)

        def source(s, _):
            def piece(j, _):
                cols = recv_ref[s, :, pl.ds(pl.multiple_of(j * chunk, chunk), chunk)]
                made = mm_tn(cols, win[...])
                group = made[:, D : 2 * D]
                at = made[:, 2 * D :]
                place = jnp.concatenate([one_hot(at == spot + k * D) for k in range(LO // D)], axis=1)
                got = jnp.zeros((chunk, D), F32)
                for p in range(0, pairs, 2):
                    both = mm(place, table[:, p * D : min(p + 2, pairs) * D])
                    for u in range(both.shape[1] // D):
                        got = jnp.where(
                            group == own + 2.0 * (p + u), both[:, u * D : u * D + D], got
                        )
                slope = gelu_parts(made[:, :D] + bias)[1]
                acc[...] += mm(cols, (got * slope).astype(BF16))
                return 0

            lax.fori_loop(0, (held_ref[s] + chunk - 1) // chunk, piece, 0)
            return 0

        lax.fori_loop(0, sources, source, 0)
        both = acc[...] + pltpu.roll(acc[...], H1, axis=1)
        rows = [
            jnp.where(lanes < H1, both[2 * k : 2 * k + 1, :], both[2 * k + 1 : 2 * k + 2, :])
            for k in range(6)
        ]
        out_ref[...] = jnp.concatenate(rows + [jnp.zeros((2, D), F32)], axis=0)

    return pl.pallas_call(
        kernel,
        in_specs=[pl.BlockSpec(memory_space=pltpu.SMEM)]
        + [pl.BlockSpec(memory_space=pltpu.VMEM)] * 3,
        out_shape=jax.ShapeDtypeStruct((8, D), F32),
        scratch_shapes=[
            pltpu.VMEM((16, 3 * D), BF16),
            pltpu.VMEM((LO, pairs * D), BF16),
            pltpu.VMEM((16, D), F32),
        ],
        compiler_params=pltpu.CompilerParams(vmem_limit_bytes=48 * 1024 * 1024),
        cost_estimate=cost_of(recv.size * 100000),
        name="points_back",
    )(held, recv, par, cell_grads)


def update(shares, params, first_moment, second_moment):
    rows = params.shape[0]
    count = shares.shape[0]
    share = (shares.shape[1] - 16) // 2
    moves = [
        (1, GRAD_ROWS, 6, 65),
        (1, 0, POINT_ROWS, LAYER_ROWS),
        (0, 0, POINT_ROWS + LAYER_ROWS, LAYER_ROWS),
    ]

    def kernel(got, par, mom1, mom2, norm_ref, new_par, new1, new2, low, rms, two, one, grad):
        def unpack(s, point):
            v = got[s].astype(F32)
            at = pl.multiple_of(s * share, 8)
            two[pl.ds(at, share), :] = v[:share]
            one[pl.ds(at, share), :] = v[share : 2 * share]
            return point + v[2 * share : 2 * share + 8]

        grad[0:8, :] = lax.fori_loop(0, count, unpack, jnp.zeros((8, D), F32), unroll=4)
        for which, src, dst, length in moves:
            grad[pl.ds(dst, length), :] = (two, one)[which][pl.ds(src, length), :]
        g = grad[...]
        norm = jnp.sqrt(jnp.sum(g * g))
        norm_ref[0, 0] = norm
        factor = jnp.minimum(1.0, clip_norm / (norm + 1e-06))
        clipped = g * factor
        first = beta_one * mom1[...] + (1.0 - beta_one) * clipped
        second = beta_two * mom2[...] + (1.0 - beta_two) * clipped * clipped
        new1[...] = first
        new2[...] = second
        first_hat = first / (1.0 - beta_one**step_count)
        second_hat = second / (1.0 - beta_two**step_count)
        p = par[...]
        p = p - learn_rate * (first_hat / (jnp.sqrt(second_hat) + adam_eps) + decay_rate * p)
        new_par[...] = p
        low[...] = p.astype(BF16)
        stats = jnp.concatenate(
            [one[LAYER_ROWS : LAYER_ROWS + 3, :], two[LAYER_ROWS : LAYER_ROWS + 5, :]], axis=0
        )
        live = jnp.sum(one[LAYER_ROWS + 3 : LAYER_ROWS + 4, :], axis=1, keepdims=True)
        sums = jnp.sum(stats, axis=1, keepdims=True)
        rms[...] = jnp.broadcast_to(jnp.sqrt(sums / jnp.maximum(live, D)), (8, D))

    shape = jax.ShapeDtypeStruct
    flat = shape((rows, D), F32)
    return pl.pallas_call(
        kernel,
        out_specs=[pl.BlockSpec(memory_space=pltpu.SMEM)]
        + [pl.BlockSpec(memory_space=pltpu.VMEM)] * 5,
        out_shape=[shape((1, 1), F32), flat, flat, flat, shape((rows, D), BF16), shape((8, D), F32)],
        scratch_shapes=[pltpu.VMEM((count * share, D), F32)] * 2 + [pltpu.VMEM((rows, D), F32)],
        compiler_params=pltpu.CompilerParams(vmem_limit_bytes=48 * 1024 * 1024),
        name="update",
    )(shares, params, first_moment, second_moment)


def shifted(x, axes, by):
    if len(axes) == 1:
        count = lax.axis_size(axes[0])
        return lax.ppermute(x, axes[0], [(i, (i + by) % count) for i in range(count)])
    tiles, rows = lax.axis_size(axes[0]), lax.axis_size(axes[1])
    pairs = [
        (i * rows + j, (i + by) % tiles * rows + (j + by) % rows)
        for i in range(tiles)
        for j in range(rows)
    ]
    return lax.ppermute(x, axes, pairs)


def exchange(row, col, cor, by):
    return (
        shifted(row, ("tile",), by),
        shifted(col, ("row",), by),
        shifted(cor, ("tile", "row"), by),
    )


def by_quads(grid, quads_x, quads_y):
    trailing = grid.shape[2:]
    grid = grid.reshape((quads_x, QS, quads_y, QS) + trailing)
    return jnp.swapaxes(grid, 1, 2).reshape((quads_x, quads_y, QC) + trailing)


def all_to_all(x):
    return lax.all_to_all(x, ("tile", "row"), split_axis=0, concat_axis=0, tiled=True)


def scatter_sum(x, count):
    return jnp.sum(all_to_all(x.reshape(count, x.shape[0] // count, D)), axis=0)


def local(
    point_feats,
    point_tile,
    point_cell,
    point_valid,
    pillar_frame,
    cotangent,
    params,
    first_moment,
    second_moment,
):
    tile_count = lax.axis_size("tile")
    row_count = lax.axis_size("row")
    device_count = tile_count * row_count
    extent_x, extent_y = pillar_frame.shape
    cell_count = extent_x * extent_y
    quads_x, quads_y = extent_x // QS, extent_y // QS
    quads = quads_x * quads_y
    points = point_cell.shape[0]
    capacity = 2 * points // tile_count
    par = params.reshape(-1, D)

    cot = by_quads(cotangent, quads_x, quads_y)
    cot_halos = exchange(cot[0], cot[:, 0], cot[0, :1], -1)

    shape = (points // BLOCK, BLOCK)
    send = bin_points(
        point_feats,
        point_tile.reshape(shape),
        point_cell.reshape(shape),
        point_valid.reshape(shape),
        tile_count,
        capacity,
        extent_y,
        quads_y,
    )
    recv = lax.all_to_all(send, "tile", split_axis=0, concat_axis=0, tiled=True)
    held = jnp.sum(recv[:, 11].astype(jnp.int32), axis=1)

    frames = by_quads(pillar_frame, quads_x, quads_y)
    frames = jnp.pad(frames, ((0, 0), (0, 0), (0, QP - QC)), constant_values=-1).reshape(-1)
    lanes = jnp.arange(D, dtype=jnp.int32)
    base_rows = (frames[:, None] == lanes[None] - (H1 + 1)).astype(F32)
    pillars, tags = encode_points(recv, held, par, base_rows, quads)
    pillars = pillars.reshape(quads_x, quads_y, QP, D)
    tags = tags.reshape(quads_x, quads_y, QC, D)
    tag_halos = exchange(tags[0], tags[:, 0], tags[0, :1], -1)

    first = first_layer(pillars, par, quads_x, quads_y)
    field, saved, sums_one = first[0], first[1:8], first[8]
    halos = exchange(*first[9:], -1)
    flags = jnp.stack(
        [
            (lax.axis_index("tile") == tile_count - 1).astype(jnp.int32),
            (lax.axis_index("row") == row_count - 1).astype(jnp.int32),
        ]
    )
    step = device_count * 8
    grad_rows = -(-(GRAD_ROWS + 72) // step) * step
    grads, grad_two, g_row, g_col, g_cor = second_layer(
        flags,
        field,
        halos,
        tags,
        tag_halos,
        cot,
        cot_halos,
        par,
        1.0 / (cell_count * device_count),
        grad_rows,
    )
    grad_two, grad_halos = lax.optimization_barrier((grad_two, exchange(g_row, g_col, g_cor, 1)))
    sum_two = scatter_sum(grad_two, device_count)
    cell_grads, grad_one = first_layer_back(
        grads, grad_halos, pillars, saved, sums_one, par, grad_rows
    )
    grad_one, sum_two = lax.optimization_barrier((grad_one, sum_two))
    sum_one = scatter_sum(grad_one, device_count)
    grad_pin = points_back(recv, held, par, cell_grads.reshape(quads * QP, D))
    share = jnp.concatenate([sum_two, sum_one, grad_pin, jnp.zeros((8, D), F32)], axis=0)
    share = share.astype(BF16)
    total = all_to_all(jnp.broadcast_to(share[None], (device_count,) + share.shape))
    norm, new_params, new_first, new_second, low, rms = update(
        total, par, first_moment.reshape(-1, D), second_moment.reshape(-1, D)
    )
    return (
        norm[0, 0],
        new_params.reshape(-1),
        new_first.reshape(-1),
        new_second.reshape(-1),
        low.reshape(-1),
        rms[:6, 0],
    )


def solution(mesh):
    return jax.shard_map(
        local,
        mesh=mesh,
        in_specs=(
            P(None, ("tile", "row")),
            P(("tile", "row"), None),
            P(("tile", "row")),
            P(("tile", "row")),
            P("tile", "row"),
            P("tile", "row", None),
            P(),
            P(),
            P(),
        ),
        out_specs=(P(), P(), P(), P(), P(), P()),
        check_vma=False,
    )
```

```python
import jax
import jax.numpy as jnp
from jax import lax
from jax.experimental import pallas as pl
from jax.experimental.pallas import tpu as pltpu
from jax.sharding import PartitionSpec as P

D = 128
HEADS = 8
HD = 16
FF = 256
H1 = 64
WIN = 12
C_IN = 11
QS = 6
QC = 36
QP = 40
SLOTS = 144
KEYS = HEADS * SLOTS
LAYER_ROWS = 1034
POINT_ROWS = 71
GRAD_ROWS = 1040
BLOCK = 256
CHUNK = 512
LO = 512
NW = 8

clip_norm = 0.01
beta_one = 0.9
beta_two = 0.999
step_count = 10
learn_rate = 0.1
decay_rate = 0.05
adam_eps = 1e-08

F32 = jnp.float32
BF16 = jnp.bfloat16
GELU_C = 0.7978845608028654
GELU_A = 0.044715


def mm(a, b):
    return lax.dot_general(a, b, (((1,), (0,)), ((), ())), preferred_element_type=F32)


def mm_nt(a, b):
    return lax.dot_general(a, b, (((1,), (1,)), ((), ())), preferred_element_type=F32)


def mm_tn(a, b):
    return lax.dot_general(a, b, (((0,), (0,)), ((), ())), preferred_element_type=F32)


def lane_iota(rows=1):
    return lax.broadcasted_iota(jnp.int32, (rows, D), 1)


def part8(v):
    return jnp.sum(v.reshape(v.shape[0] // 8, 8, v.shape[1]), axis=0)


def gelu_parts(v):
    sq = v * v
    t = jnp.tanh(v * (GELU_C + (GELU_C * GELU_A) * sq))
    half = 0.5 + 0.5 * t
    slope = half + (0.5 * v) * (1.0 - t * t) * (GELU_C + (3.0 * GELU_C * GELU_A) * sq)
    return v * half, slope


def gelu_only(v):
    t = jnp.tanh(v * (GELU_C + (GELU_C * GELU_A) * (v * v)))
    return v * (0.5 + 0.5 * t)


def normalize(y):
    center = y - jnp.mean(y, axis=-1, keepdims=True)
    rs = lax.rsqrt(jnp.mean(center * center, axis=-1, keepdims=True) + 1e-05)
    return center * rs, rs


def norm_pull(gx, xhat, rs):
    return rs * (
        gx
        - jnp.mean(gx, axis=-1, keepdims=True)
        - xhat * jnp.mean(gx * xhat, axis=-1, keepdims=True)
    )


def load_layer(par, base, w):
    for part in range(3):
        m = par[pl.ds(base + part, D, stride=3), :]
        w["qkv"][:, part * D : (part + 1) * D] = m.astype(BF16)
        if "qkv_t" in w:
            w["qkv_t"][part * D : (part + 1) * D, :] = m.T.astype(BF16)
    m = par[pl.ds(base + 384, D), :]
    w["out"][...] = m.astype(BF16)
    if "out_t" in w:
        w["out_t"][...] = m.T.astype(BF16)
    for part in range(2):
        m = par[pl.ds(base + 512 + part, D, stride=2), :]
        w["fin"][:, part * D : (part + 1) * D] = m.astype(BF16)
        if "fin_t" in w:
            w["fin_t"][part * D : (part + 1) * D, :] = m.T.astype(BF16)
        m = par[pl.ds(base + 768 + part * D, D), :]
        w["fout"][part * D : (part + 1) * D, :] = m.astype(BF16)
        if "fout_t" in w:
            w["fout_t"][:, part * D : (part + 1) * D] = m.T.astype(BF16)


WEIGHT_SHAPES = {
    "qkv": (D, 3 * D),
    "qkv_t": (3 * D, D),
    "out": (D, D),
    "out_t": (D, D),
    "fin": (D, FF),
    "fin_t": (FF, D),
    "fout": (FF, D),
    "fout_t": (D, FF),
}


def vec(par, base, row):
    return par[base + 1024 + row : base + 1025 + row, :]


def vec2(par, base, row):
    return jnp.concatenate([vec(par, base, row), vec(par, base, row + 1)], axis=1)


def fold_rows():
    return one_hot(lax.broadcasted_iota(jnp.int32, (HD, D), 0) == lane_iota(HD) % HD)


def own_head():
    return lax.broadcasted_iota(jnp.int32, (D, D), 0) // HD == lane_iota(D) // HD


def turned(v):
    return v.astype(F32).T


def head_cols(v):
    top = turned(v[:D]).astype(BF16)
    none = jnp.zeros((HD, D), BF16)
    pairs = []
    for t in range(0, D, 2 * HD):
        left = jnp.concatenate([top[t : t + HD], none], axis=0)
        right = jnp.concatenate([none, top[t + HD : t + 2 * HD]], axis=0)
        pairs.append(jnp.concatenate([left, right], axis=1))
    return pairs, jnp.where(own_head(), mm_tn(v[D:], fold_rows()), 0.0).astype(BF16)


def by_head(rows, cols):
    pairs, rest = cols
    parts = []
    for t in range(HEADS // 2):
        both = mm(rows[:, 2 * HD * t : 2 * HD * (t + 1)], pairs[t])
        parts = parts + [both[:, :D], both[:, D:]]
    return parts + [mm(rows, rest)]


def head_sums(cols, parts):
    pairs, rest = cols
    sums = [
        mm_nt(pairs[t], jnp.concatenate(parts[2 * t : 2 * t + 2], axis=1)) for t in range(HEADS // 2)
    ]
    return (jnp.concatenate(sums, axis=0) + mm_nt(rest, parts[HEADS])).T.astype(BF16)


def window_bias(groups):
    keys = jnp.concatenate(
        [groups[:D]] + [groups[D:]] * HEADS + [jnp.ones((D, D), BF16)], axis=0
    )
    same = mm_nt(groups, keys)
    rows = lax.broadcasted_iota(jnp.int32, (SLOTS, D), 0)
    lanes = lane_iota(SLOTS)
    first = (same[:, :D] > 0.5) | (rows == lanes)
    last = (same[:, D : 2 * D] > 0.5) | (rows == lanes % HD + D)
    return (
        jnp.where(first, 0.0, -1000000000.0),
        jnp.where(last, 0.0, -1000000000.0),
        same[:, 2 * D :],
    )


def attend(qs, key, val, bias_first, bias_last):
    probs = []
    cols = head_cols(qs)
    yield
    parts = by_head(key, cols)
    yield
    for h, part in enumerate(parts):
        part = part + (bias_first if h < HEADS else bias_last)
        expo = jnp.exp(part - jnp.max(part, axis=0, keepdims=True))
        probs.append((expo * (1.0 / jnp.sum(expo, axis=0, keepdims=True))).astype(BF16))
    yield
    mix = yield from query_pull(val, probs)
    return probs, mix


def attend_pull(probs, qs, key, val, gmix):
    cols = head_cols(gmix)
    gs = []
    yield
    parts = by_head(val, cols)
    yield
    g_val = head_sums(cols, probs)
    yield
    for p_low, pulled in zip(probs, parts):
        p = p_low.astype(F32)
        both = p * pulled
        gs.append((both - p * jnp.sum(both, axis=0, keepdims=True)).astype(BF16))
    yield
    g_key = head_sums(head_cols(qs), gs)
    yield
    g_query = yield from query_pull(key * 0.25, gs)
    return g_query, g_key, g_val


def query_pull(rows, parts):
    flat = turned(rows).astype(BF16)
    tops = []
    for t in range(HEADS // 2):
        at = 2 * HD * t
        both = mm(flat[at : at + 2 * HD], jnp.concatenate(parts[2 * t : 2 * t + 2], axis=1))
        tops = tops + [both[:HD, :D], both[HD:, D:]]
    top = jnp.concatenate(tops, axis=0)
    rest = jnp.where(own_head(), mm(flat, parts[HEADS]), 0.0).astype(BF16)
    yield
    return jnp.concatenate([top.T.astype(BF16), mm_nt(fold_rows(), rest).astype(BF16)], axis=0)


def in_step(runs):
    results = [None] * len(runs)
    active = list(range(len(runs)))
    while active:
        for i in list(active):
            try:
                next(runs[i])
            except StopIteration as end:
                results[i] = end.value
                active.remove(i)
    return results


def split_qkv(packed, w):
    rows = slice(w * SLOTS, (w + 1) * SLOTS)
    return packed[rows, :D] * 0.25, packed[rows, D : 2 * D], packed[rows, 2 * D :]


def layer_forward(x, groups, par, base, w, sums):
    count = x.shape[0] // SLOTS
    low = x.astype(BF16)
    qkv_bias = jnp.concatenate(
        [vec(par, base, 0), jnp.zeros((1, D), F32), vec(par, base, 1)], axis=1
    )
    packed = (mm(low, w["qkv"][...]) + qkv_bias).astype(BF16)
    masks = [window_bias(group) for group in groups]
    done = in_step([attend(*split_qkv(packed, i), *masks[i][:2]) for i in range(count)])
    probs = [d[0] for d in done]
    mixes = [d[1] for d in done]
    lives = [m[2] for m in masks]
    mix = jnp.concatenate(mixes, axis=0)
    live = jnp.concatenate(lives, axis=0)
    attn_out = mm(mix, w["out"][...]) + vec(par, base, 2)
    first = x + attn_out
    xhat1, rs1 = normalize(first)
    normed = (xhat1 * vec(par, base, 3) + vec(par, base, 4)) * live
    normed_low = normed.astype(BF16)
    pre = mm(normed_low, w["fin"][...]) + vec2(par, base, 5)
    act, slope = gelu_parts(pre)
    hidden = act.astype(BF16)
    ffn = mm(hidden, w["fout"][...]) + vec(par, base, 7)
    second = normed + ffn
    xhat2, rs2 = normalize(second)
    result = (xhat2 * vec(par, base, 8) + vec(par, base, 9)) * live
    sums[0] += part8(attn_out * attn_out * live)
    sums[1] += part8(ffn * ffn * live)
    sums[2] += part8(result * result)
    sums[3] += part8(live)
    return dict(
        low=low,
        packed=packed,
        probs=probs,
        mix=mix,
        live=live,
        first=first,
        second=second,
        xhat1=xhat1,
        rs1=rs1,
        xhat2=xhat2,
        rs2=rs2,
        normed_low=normed_low,
        slope=slope,
        hidden=hidden,
        result=result,
    )


def layer_backward(grad, k, par, base, w, acc):
    live = k["live"]
    gl = grad * live
    acc["vec"][8] += part8(gl * k["xhat2"])
    acc["vec"][9] += part8(gl)
    g2 = norm_pull(gl * vec(par, base, 8), k["xhat2"], k["rs2"])
    g_ffn = g2.astype(BF16)
    acc["fout"][...] += mm_tn(k["hidden"], g_ffn)
    acc["vec"][7] += part8(g_ffn.astype(F32))
    g_pre = (mm(g_ffn, w["fout_t"][...]) * k["slope"]).astype(BF16)
    acc["fin"][...] += mm_tn(k["normed_low"], g_pre)
    for part in range(2):
        acc["vec"][5 + part] += part8(g_pre[:, part * D : (part + 1) * D].astype(F32))
    g_norm = (g2 + mm(g_pre, w["fin_t"][...])) * live
    acc["vec"][3] += part8(g_norm * k["xhat1"])
    acc["vec"][4] += part8(g_norm)
    g1 = norm_pull(g_norm * vec(par, base, 3), k["xhat1"], k["rs1"])
    g_attn = g1.astype(BF16)
    acc["out"][...] += mm_tn(k["mix"], g_attn)
    acc["vec"][2] += part8(g_attn.astype(F32))
    g_mix = mm(g_attn, w["out_t"][...]).astype(BF16)
    runs = []
    for i in range(grad.shape[0] // SLOTS):
        rows = slice(i * SLOTS, (i + 1) * SLOTS)
        runs.append(attend_pull(k["probs"][i], *split_qkv(k["packed"], i), g_mix[rows]))
    pieces = [jnp.concatenate(parts, axis=1) for parts in in_step(runs)]
    g_packed = jnp.concatenate(pieces, axis=0)
    acc["qkv"][...] += mm_tn(k["low"], g_packed)
    acc["vec"][0] += part8(g_packed[:, :D].astype(F32))
    acc["vec"][1] += part8(g_packed[:, 2 * D :].astype(F32))
    return g1 + mm(g_packed, w["qkv_t"][...])


ACC_SHAPES = {
    "qkv": (D, 3 * D),
    "out": (D, D),
    "fin": (D, FF),
    "fout": (FF, D),
    "vec": (10, 8, D),
}


def clear(acc):
    for ref in acc.values():
        ref[...] = jnp.zeros(ref.shape, ref.dtype)


def store_grads(acc, sums, out):
    for part in range(3):
        out[pl.ds(part, D, stride=3), :] = acc["qkv"][:, part * D : (part + 1) * D]
    out[pl.ds(384, D), :] = acc["out"][...]
    for part in range(2):
        out[pl.ds(512 + part, D, stride=2), :] = acc["fin"][:, part * D : (part + 1) * D]
    out[pl.ds(768, FF), :] = acc["fout"][...]
    out[pl.ds(1024, 16), :] = jnp.concatenate(
        [jnp.sum(acc["vec"][i], axis=0, keepdims=True) for i in range(10)]
        + [jnp.sum(sums[i], axis=0, keepdims=True) for i in range(4)]
        + [jnp.zeros((2, D), F32)],
        axis=0,
    )


def gather_windows(scratch, pick):
    for i in range(NW):
        for r in range(2):
            for c in range(2):
                at = i * SLOTS + (2 * r + c) * QC
                scratch[pl.ds(at, QC), :] = pick(r, 2 * i + c)
    return scratch[...]


def spread_windows(scratch, value, put):
    scratch[...] = value
    for i in range(NW):
        for r in range(2):
            for c in range(2):
                put(r, 2 * i + c, scratch[pl.ds(i * SLOTS + (2 * r + c) * QC, QC), :])


def whole(shape, space=pltpu.VMEM):
    return pl.BlockSpec(shape, lambda *_: (0,) * len(shape), memory_space=space)


def params_for(limit=56):
    return pltpu.CompilerParams(
        dimension_semantics=("arbitrary",), vmem_limit_bytes=limit * 1024 * 1024
    )


def cost_of(flops):
    return pl.CostEstimate(flops=flops, bytes_accessed=1 << 24, transcendentals=0)


def first_layer(pillars, par, quads_x, quads_y):
    across = quads_x // 2
    along = quads_y // (2 * NW)
    windows = quads_x * quads_y // 4
    base = POINT_ROWS

    def kernel(pil, par_ref, *refs):
        outs, scratch = refs[:12], refs[12:]
        (
            field,
            probs_out,
            packed_out,
            mix_out,
            first_out,
            second_out,
            low_out,
            live_out,
            sums_out,
            row_out,
            col_out,
            cor_out,
        ) = outs
        names = ["qkv", "out", "fin", "fout"]
        w = dict(zip(names, scratch[:4]))
        wide, pout, sums = scratch[4:]
        step = pl.program_id(0)
        a = step // along
        b = step % along

        @pl.when(step == 0)
        def _():
            load_layer(par_ref, base, w)
            m = par_ref[pl.ds(6, H1), :].astype(BF16)
            pout[...] = jnp.concatenate([m, m], axis=0)
            sums[...] = jnp.zeros(sums.shape, F32)

        cells = gather_windows(wide, lambda r, c: pil[r, c, :QC, :])
        lanes = lane_iota()
        total = jnp.where(lanes < H1, cells, 0.0)
        count = cells[:, H1 : H1 + 1]
        high = total.astype(BF16).astype(F32)
        both = (high + pltpu.roll(total - high, H1, axis=1)).astype(BF16)
        pillar = mm(both, pout[...]) + count * par_ref[70:71, :]
        x = pillar / jnp.maximum(count, 1.0)
        onehot = jnp.where((lanes > H1) & (lanes < H1 + 4) & (count > 0.0), cells, 0.0).astype(BF16)
        groups = [onehot[i * SLOTS : (i + 1) * SLOTS] for i in range(NW)]
        k = layer_forward(x, groups, par_ref, base, w, sums)
        for i in range(NW):
            rows = slice(i * SLOTS, (i + 1) * SLOTS)
            for h in range(HEADS + 1):
                probs_out[i, :, h * D : (h + 1) * D] = k["probs"][i][h]
            packed_out[i] = k["packed"][rows]
            mix_out[i] = k["mix"][rows]
            first_out[i] = k["first"][rows]
            second_out[i] = k["second"][rows]
            low_out[i] = k["low"][rows]
            live_out[i] = k["live"][rows]

        def put(r, c, v):
            field[r, c, :QC, :] = v

        spread_windows(wide, k["result"], put)

        @pl.when(a == 0)
        def _():
            for c in range(2 * NW):
                row_out[c] = field[0, c, :QC, :].astype(BF16)

        @pl.when(b == 0)
        def _():
            for r in range(2):
                col_out[r] = field[r, 0, :QC, :].astype(BF16)

        @pl.when(step == 0)
        def _():
            cor_out[0] = field[0, 0, :QC, :].astype(BF16)

        @pl.when(step == pl.num_programs(0) - 1)
        def _():
            sums_out[...] = sums[...]

    def win_spec(width):
        return pl.BlockSpec((NW, SLOTS, width), lambda s: (s, 0, 0))

    quad_spec = pl.BlockSpec((2, 2 * NW, QP, D), lambda s: (s // along, s % along, 0, 0))
    shape = jax.ShapeDtypeStruct
    return pl.pallas_call(
        kernel,
        grid=(across * along,),
        in_specs=[quad_spec, whole(par.shape)],
        out_specs=[
            quad_spec,
            win_spec(KEYS),
            win_spec(3 * D),
            win_spec(D),
            win_spec(D),
            win_spec(D),
            win_spec(D),
            win_spec(D),
            whole((4, 8, D)),
            pl.BlockSpec((2 * NW, QC, D), lambda s: (jnp.minimum(s, along - 1), 0, 0)),
            pl.BlockSpec((2, QC, D), lambda s: (s // along, 0, 0)),
            whole((1, QC, D)),
        ],
        out_shape=[
            shape((quads_x, quads_y, QP, D), F32),
            shape((windows, SLOTS, KEYS), BF16),
            shape((windows, SLOTS, 3 * D), BF16),
            shape((windows, SLOTS, D), BF16),
            shape((windows, SLOTS, D), F32),
            shape((windows, SLOTS, D), F32),
            shape((windows, SLOTS, D), BF16),
            shape((windows, SLOTS, D), F32),
            shape((4, 8, D), F32),
            shape((quads_y, QC, D), BF16),
            shape((quads_x, QC, D), BF16),
            shape((1, QC, D), BF16),
        ],
        scratch_shapes=[pltpu.VMEM(WEIGHT_SHAPES[n], BF16) for n in ["qkv", "out", "fin", "fout"]]
        + [
            pltpu.VMEM((NW * SLOTS, D), F32),
            pltpu.VMEM((D, D), BF16),
            pltpu.VMEM((4, 8, D), F32),
        ],
        compiler_params=params_for(),
        name="first_layer",
    )(pillars, par)


def second_layer(flags, field, halos, tags, tag_halos, cot, cot_halos, par, scale, grad_rows):
    quads_x, quads_y = field.shape[:2]
    across = quads_x // 2
    along = quads_y // (2 * NW)
    base = POINT_ROWS + LAYER_ROWS
    wnames = list(WEIGHT_SHAPES)
    anames = list(ACC_SHAPES)

    def kernel(flag, *refs):
        ins, refs = refs[:13], refs[13:]
        outs, scratch = refs[:5], refs[5:]
        fields, tagss, cots, par_ref = ins[:4], ins[4:8], ins[8:12], ins[12]
        grads, weights, row_out, col_out, cor_out = outs
        w = dict(zip(wnames, scratch))
        scratch = scratch[len(wnames) :]
        acc = dict(zip(anames, scratch))
        wide, sums, ext_x, ext_t, ext_g = scratch[len(anames) :]
        step = pl.program_id(0)
        a = step // along
        b = step % along

        @pl.when(step == 0)
        def _():
            load_layer(par_ref, base, w)
            sums[...] = jnp.zeros(sums.shape, F32)
            clear(acc)
            lanes = lane_iota()

            def moved(v, region):
                return pltpu.roll(v, 3 * region, axis=1)

            def fill(ext, srcs, turn_row, turn_col, turn_cor):
                main, row, col, cor = srcs

                def one(i, _):
                    ext[i // quads_y, i % quads_y, :QC, :] = main[
                        i // quads_y, i % quads_y, :QC, :
                    ].astype(F32)
                    return 0

                lax.fori_loop(0, quads_x * quads_y, one, 0, unroll=4)

                def one_row(i, _):
                    ext[quads_x, i, :QC, :] = turn_row(row[i].astype(F32))
                    return 0

                lax.fori_loop(1, quads_y, one_row, 0)
                for i in range(1, quads_x):
                    ext[i, quads_y, :QC, :] = turn_col(col[i].astype(F32))
                ext[quads_x, quads_y, :QC, :] = turn_cor(cor[0].astype(F32))

            def same(v):
                return v

            last_x = flag[0] > 0
            last_y = flag[1] > 0

            def tag_row(v):
                return jnp.where(last_x, moved(v, 2), v)

            def tag_col(v):
                return jnp.where(last_y, moved(v, 1), v)

            fill(ext_x, fields, same, same, same)
            fill(ext_t, tagss, tag_row, tag_col, lambda v: tag_row(tag_col(v)))
            fill(ext_g, cots, same, same, same)

        def picker(ext):
            return lambda r, c: ext[2 * a + 1 + r, 2 * NW * b + 1 + c, :QC, :]

        tag = gather_windows(wide, picker(ext_t)).astype(BF16)
        groups = [tag[i * SLOTS : (i + 1) * SLOTS] for i in range(NW)]
        x = gather_windows(wide, picker(ext_x))
        k = layer_forward(x, groups, par_ref, base, w, sums)
        grad = gather_windows(wide, picker(ext_g)) * scale
        gx = layer_backward(grad, k, par_ref, base, w, acc)

        def put(r, c, v):
            grads[r, c, :QC, :] = v

        spread_windows(wide, gx, put)

        @pl.when(a == across - 1)
        def _():
            for c in range(2 * NW):
                row_out[c] = grads[1, c, :QC, :].astype(BF16)

        @pl.when(b == along - 1)
        def _():
            for r in range(2):
                col_out[r] = grads[r, 2 * NW - 1, :QC, :].astype(BF16)

        @pl.when(step == pl.num_programs(0) - 1)
        def _():
            cor_out[0] = grads[1, 2 * NW - 1, :QC, :].astype(BF16)
            store_grads(acc, sums, weights)

    shape = jax.ShapeDtypeStruct
    quad_spec = pl.BlockSpec((2, 2 * NW, QP, D), lambda s: (s // along, s % along, 0, 0))
    ext = pltpu.VMEM((quads_x + 1, quads_y + 1, QP, D), F32)
    arrays = [field, *halos, tags, *tag_halos, cot, *cot_halos, par]
    return pl.pallas_call(
        kernel,
        grid=(across * along,),
        in_specs=[pl.BlockSpec(memory_space=pltpu.SMEM)] + [whole(v.shape) for v in arrays],
        out_specs=[
            quad_spec,
            whole((grad_rows, D)),
            pl.BlockSpec(
                (2 * NW, QC, D), lambda s: (jnp.maximum(s - (across - 1) * along, 0), 0, 0)
            ),
            pl.BlockSpec((2, QC, D), lambda s: (s // along, 0, 0)),
            whole((1, QC, D)),
        ],
        out_shape=[
            shape((quads_x, quads_y, QP, D), F32),
            shape((grad_rows, D), F32),
            shape((quads_y, QC, D), BF16),
            shape((quads_x, QC, D), BF16),
            shape((1, QC, D), BF16),
        ],
        scratch_shapes=[pltpu.VMEM(WEIGHT_SHAPES[n], BF16) for n in wnames]
        + [pltpu.VMEM(ACC_SHAPES[n], F32) for n in anames]
        + [
            pltpu.VMEM((NW * SLOTS, D), F32),
            pltpu.VMEM((4, 8, D), F32),
            ext,
            ext,
            ext,
        ],
        compiler_params=params_for(),
        name="second_layer",
    )(flags, *arrays)


def first_layer_back(grads, halos, pillars, saved, sums, par, grad_rows):
    quads_x, quads_y = grads.shape[:2]
    across = quads_x // 2
    along = quads_y // (2 * NW)
    base = POINT_ROWS
    wnames = list(WEIGHT_SHAPES)
    anames = list(ACC_SHAPES)

    def kernel(*refs):
        ins, refs = refs[:14], refs[14:]
        outs, scratch = refs[:2], refs[2:]
        main, row, col, cor, pil = ins[:5]
        probs, packed, mix, first, second, low, live = ins[5:12]
        sums_ref, par_ref = ins[12:]
        cell_out, weights = outs
        w = dict(zip(wnames, scratch))
        scratch = scratch[len(wnames) :]
        acc = dict(zip(anames, scratch))
        wide, ext, pout_t, pacc = scratch[len(anames) :]
        step = pl.program_id(0)
        a = step // along
        b = step % along

        @pl.when(step == 0)
        def _():
            load_layer(par_ref, base, w)
            clear(acc)
            pacc[...] = jnp.zeros(pacc.shape, F32)
            m = par_ref[pl.ds(6, H1), :]
            pout_t[...] = jnp.concatenate([m, m], axis=0).T.astype(BF16)
            for r in range(1, quads_x):

                def one(i, _):
                    ext[r, i, :QC, :] = main[r - 1, i - 1, :QC, :]
                    return 0

                lax.fori_loop(1, quads_y, one, 0)
                ext[r, 0, :QC, :] = col[r - 1].astype(F32)

            def one_row(i, _):
                ext[0, i, :QC, :] = row[i - 1].astype(F32)
                return 0

            lax.fori_loop(1, quads_y, one_row, 0)
            ext[0, 0, :QC, :] = cor[0].astype(F32)

        grad = gather_windows(wide, lambda r, c: ext[2 * a + r, 2 * NW * b + c, :QC, :])

        def rows_of(ref):
            return jnp.concatenate([ref[i] for i in range(NW)], axis=0)

        k = dict(
            low=rows_of(low),
            packed=rows_of(packed),
            probs=[
                [probs[i, :, h * D : (h + 1) * D] for h in range(HEADS + 1)] for i in range(NW)
            ],
            mix=rows_of(mix),
            live=rows_of(live),
        )
        k["xhat1"], k["rs1"] = normalize(rows_of(first))
        k["xhat2"], k["rs2"] = normalize(rows_of(second))
        normed = (k["xhat1"] * vec(par_ref, base, 3) + vec(par_ref, base, 4)) * k["live"]
        k["normed_low"] = normed.astype(BF16)
        act, k["slope"] = gelu_parts(mm(k["normed_low"], w["fin"][...]) + vec2(par_ref, base, 5))
        k["hidden"] = act.astype(BF16)
        gx = layer_backward(grad, k, par_ref, base, w, acc)

        cells = gather_windows(wide, lambda r, c: pil[r, c, :QC, :])
        lanes = lane_iota()
        total = jnp.where(lanes <= H1, cells, 0.0)
        g_pillar = (gx / jnp.maximum(cells[:, H1 : H1 + 1], 1.0)).astype(BF16)
        high = total.astype(BF16)
        rest = (total - high.astype(F32)).astype(BF16)
        pacc[...] += mm_tn(high, g_pillar) + mm_tn(rest, g_pillar)

        def put(r, c, v):
            cell_out[r, c, :QC, :] = v
            cell_out[r, c, QC:, :] = jnp.zeros((QP - QC, D), F32)

        spread_windows(wide, mm(g_pillar, pout_t[...]), put)

        @pl.when(step == pl.num_programs(0) - 1)
        def _():
            store_grads(acc, sums_ref, weights)
            weights[GRAD_ROWS : GRAD_ROWS + 72, :] = pacc[:72, :]

    def win_spec(width):
        return pl.BlockSpec((NW, SLOTS, width), lambda s: (s, 0, 0))

    shape = jax.ShapeDtypeStruct
    quad_spec = pl.BlockSpec((2, 2 * NW, QP, D), lambda s: (s // along, s % along, 0, 0))
    return pl.pallas_call(
        kernel,
        grid=(across * along,),
        in_specs=[whole(grads.shape)]
        + [whole(v.shape) for v in halos]
        + [quad_spec]
        + [win_spec(v.shape[2]) for v in saved]
        + [whole(sums.shape), whole(par.shape)],
        out_specs=[quad_spec, whole((grad_rows, D))],
        out_shape=[shape((quads_x, quads_y, QP, D), F32), shape((grad_rows, D), F32)],
        scratch_shapes=[pltpu.VMEM(WEIGHT_SHAPES[n], BF16) for n in wnames]
        + [pltpu.VMEM(ACC_SHAPES[n], F32) for n in anames]
        + [
            pltpu.VMEM((NW * SLOTS, D), F32),
            pltpu.VMEM((quads_x, quads_y, QP, D), F32),
            pltpu.VMEM((D, D), BF16),
            pltpu.VMEM((D, D), F32),
        ],
        compiler_params=params_for(),
        cost_estimate=cost_of(grads.size * 12000),
        name="first_layer_back",
    )(grads, *halos, pillars, *saved, sums, par)


def one_hot(hit):
    return jnp.where(hit, 1.0, 0.0).astype(BF16)


def bin_points(feats, tiles, cells, valid, tile_count, capacity, extent_y, quads_y):
    blocks = tiles.shape[0]
    groups = tile_count * capacity // LO
    lots = 4
    wide = lots * BLOCK

    def kernel(feat_ref, tile_ref, cell_ref, valid_ref, out_ref, slot_ref, code_ref, acc):
        real = valid_ref[...] > 0
        t = jnp.where(real, tile_ref[...], tile_count)
        i0 = lax.broadcasted_iota(jnp.int32, (BLOCK, BLOCK), 0)
        i1 = lax.broadcasted_iota(jnp.int32, (BLOCK, BLOCK), 1)
        upto = one_hot(i0 <= i1)
        j0 = lax.broadcasted_iota(jnp.int32, (blocks, blocks), 0)
        j1 = lax.broadcasted_iota(jnp.int32, (blocks, blocks), 1)
        earlier = one_hot(j1 < j0)
        slot = jnp.full((blocks, BLOCK), -1.0, F32)
        for k in range(tile_count):
            hit = t == k
            run = mm(one_hot(hit), upto)
            total = jnp.broadcast_to(run[:, BLOCK - 1 :], (blocks, D)).astype(BF16)
            at = mm(earlier, total)[:, :1] + (k * capacity - 1.0)
            slot = jnp.where(hit, run + at, slot)
        slot_ref[...] = slot.astype(jnp.int32)

        def part(v, by):
            return ((v.astype(F32) + 0.5) * (1.0 / by)).astype(jnp.int32)

        cell = cell_ref[...]
        cx = part(cell, extent_y)
        cy = cell - cx * extent_y
        qx, qy = part(cx, QS), part(cy, QS)
        row = (qx * quads_y + qy) * QP + (cx - qx * QS) * QS + (cy - qy * QS)
        hi = row // LO
        lo = row - hi * LO
        low_part = lo % 256
        code_ref[0] = jnp.where(real, 1.0, 0.0)
        code_ref[1] = (hi + 1).astype(F32)
        code_ref[2] = (lo - low_part).astype(F32)
        code_ref[3] = low_part.astype(F32)
        acc[...] = jnp.zeros(acc.shape, F32)
        span = lax.broadcasted_iota(jnp.int32, (LO, wide), 0)

        def one(j, _):
            def line(ref, *lead):
                return jnp.concatenate(
                    [ref[(*lead, pl.ds(j * lots + u, 1), slice(None))] for u in range(lots)], axis=1
                )

            at = line(slot_ref)
            feat = feat_ref[:, pl.ds(pl.multiple_of(j * wide, wide), wide)].astype(F32)
            rows = jnp.concatenate(
                [feat] + [line(code_ref, i) for i in range(4)] + [jnp.zeros((1, wide), F32)], axis=0
            ).astype(BF16)
            group = at // LO
            place = one_hot(span == at % LO)
            spread = jnp.concatenate([rows * one_hot(group == g) for g in range(groups)], axis=0)
            acc[...] += mm_nt(spread, place)
            return 0

        lax.fori_loop(0, blocks // lots, one, 0)
        for k in range(tile_count):
            for at in range(0, capacity, LO):
                g, low = (k * capacity + at) // LO, (k * capacity + at) % LO
                size = min(LO, capacity)
                out_ref[k, :, at : at + size] = acc[g * 16 : g * 16 + 16, low : low + size].astype(
                    BF16
                )

    return pl.pallas_call(
        kernel,
        out_shape=jax.ShapeDtypeStruct((tile_count, 16, capacity), BF16),
        scratch_shapes=[
            pltpu.VMEM((blocks, BLOCK), jnp.int32),
            pltpu.VMEM((4, blocks, BLOCK), F32),
            pltpu.VMEM((groups * 16, LO), F32),
        ],
        compiler_params=pltpu.CompilerParams(vmem_limit_bytes=48 * 1024 * 1024),
        name="bin_points",
    )(feats, tiles, cells, valid)


def unpack_point_in(par_ref, win):
    lanes = lane_iota()
    flat = par_ref[0:6, :]
    turned = pltpu.roll(flat, H1, axis=1)
    even = jnp.where(lanes < H1, flat, turned)
    odd = jnp.where(lanes < H1, turned, flat)
    rows = []
    for k in range(C_IN):
        src = even if k % 2 == 0 else odd
        rows.append(src[k // 2 : k // 2 + 1])
    rows.append(jnp.zeros((5, D), F32))
    win[:, :D] = jnp.concatenate(rows, axis=0).astype(BF16)
    at = lax.broadcasted_iota(jnp.int32, (16, D), 0)
    win[:, D : 2 * D] = one_hot(at == 12)
    win[:, 2 * D :] = one_hot((at == 13) | (at == 14))
    return odd[5:6]


def encode_points(recv, held, par, base_rows, quads):
    sources, _, capacity = recv.shape
    chunk = min(CHUNK, capacity)
    groups = -(-quads * QP // LO)
    pairs = -(-groups // 2)

    def kernel(held_ref, recv_ref, par_ref, base_ref, out_ref, tag_ref, win, acc):
        bias = unpack_point_in(par_ref, win)
        acc[...] = jnp.zeros(acc.shape, F32)
        lanes = lane_iota()
        own = jnp.where(lanes < H1, 1.0, 2.0)
        count_of = (lanes + 1).astype(F32)
        span = lax.broadcasted_iota(jnp.int32, (LO, chunk), 0)

        def source(s, _):
            def piece(j, _):
                cols = recv_ref[s, :, pl.ds(pl.multiple_of(j * chunk, chunk), chunk)]
                wide = cols.astype(F32)
                place = one_hot(span == (wide[13:14] + wide[14:15]).astype(jnp.int32))
                both = mm_tn(cols, win[:, : 2 * D])
                act = gelu_only(both[:, :D] + bias)
                group = both[:, D:]
                spread = [
                    jnp.where(group == own + 2.0 * g, act, 0.0).astype(BF16) for g in range(pairs)
                ]
                spread.append(one_hot(group == count_of))
                acc[...] += mm(place, jnp.concatenate(spread, axis=1))
                return 0

            lax.fori_loop(0, (held_ref[s] + chunk - 1) // chunk, piece, 0)
            return 0

        lax.fori_loop(0, sources, source, 0)
        for g in range(groups):
            rows = min(LO, quads * QP - g * LO)
            v = acc[:rows, g // 2 * D : g // 2 * D + D]
            if g % 2 == 1:
                v = pltpu.roll(v, H1, axis=1)
            count = acc[:rows, pairs * D + g : pairs * D + g + 1]
            v = jnp.where(lanes < H1, v, jnp.where(lanes == H1, count, 0.0))
            out_ref[g * LO : g * LO + rows, :] = v + base_ref[g * LO : g * LO + rows, :]

        def finish(i, _):
            total = out_ref[pl.ds(pl.multiple_of(i * QP, 8), QP), :]
            count = total[:, H1 : H1 + 1]
            tag = jnp.where((lanes > H1) & (lanes < H1 + 4) & (count > 0.0), total, 0.0)
            tag_ref[i] = tag[:QC, :].astype(BF16)
            return 0

        lax.fori_loop(0, quads, finish, 0, unroll=4)

    shape = jax.ShapeDtypeStruct
    return pl.pallas_call(
        kernel,
        in_specs=[pl.BlockSpec(memory_space=pltpu.SMEM)]
        + [pl.BlockSpec(memory_space=pltpu.VMEM)] * 3,
        out_shape=[shape((quads * QP, D), F32), shape((quads, QC, D), BF16)],
        scratch_shapes=[pltpu.VMEM((16, 3 * D), BF16), pltpu.VMEM((LO, (pairs + 1) * D), F32)],
        compiler_params=pltpu.CompilerParams(vmem_limit_bytes=56 * 1024 * 1024),
        name="encode_points",
    )(held, recv, par, base_rows)


def points_back(recv, held, par, cell_grads):
    sources, _, capacity = recv.shape
    chunk = min(CHUNK, capacity)
    total_rows = cell_grads.shape[0]
    groups = -(-total_rows // LO)
    pairs = -(-groups // 2)

    def kernel(held_ref, recv_ref, par_ref, grad_ref, out_ref, win, table, acc):
        bias = unpack_point_in(par_ref, win)
        lanes = lane_iota()

        def rows_of(g):
            rows = max(0, min(LO, total_rows - g * LO))
            got = [grad_ref[g * LO : g * LO + rows, :]] if rows else []
            return jnp.concatenate(got + [jnp.zeros((LO - rows, D), F32)], axis=0) if rows < LO else got[0]

        for j in range(pairs):
            table[:, j * D : j * D + D] = jnp.where(
                lanes < H1, rows_of(2 * j), rows_of(2 * j + 1)
            ).astype(BF16)
        acc[...] = jnp.zeros((16, D), F32)
        own = jnp.where(lanes < H1, 1.0, 2.0)
        spot = lanes.astype(F32)

        def source(s, _):
            def piece(j, _):
                cols = recv_ref[s, :, pl.ds(pl.multiple_of(j * chunk, chunk), chunk)]
                made = mm_tn(cols, win[...])
                group = made[:, D : 2 * D]
                at = made[:, 2 * D :]
                place = jnp.concatenate([one_hot(at == spot + k * D) for k in range(LO // D)], axis=1)
                got = jnp.zeros((chunk, D), F32)
                for p in range(0, pairs, 2):
                    both = mm(place, table[:, p * D : min(p + 2, pairs) * D])
                    for u in range(both.shape[1] // D):
                        got = jnp.where(
                            group == own + 2.0 * (p + u), both[:, u * D : u * D + D], got
                        )
                slope = gelu_parts(made[:, :D] + bias)[1]
                acc[...] += mm(cols, (got * slope).astype(BF16))
                return 0

            lax.fori_loop(0, (held_ref[s] + chunk - 1) // chunk, piece, 0)
            return 0

        lax.fori_loop(0, sources, source, 0)
        both = acc[...] + pltpu.roll(acc[...], H1, axis=1)
        rows = [
            jnp.where(lanes < H1, both[2 * k : 2 * k + 1, :], both[2 * k + 1 : 2 * k + 2, :])
            for k in range(6)
        ]
        out_ref[...] = jnp.concatenate(rows + [jnp.zeros((2, D), F32)], axis=0)

    return pl.pallas_call(
        kernel,
        in_specs=[pl.BlockSpec(memory_space=pltpu.SMEM)]
        + [pl.BlockSpec(memory_space=pltpu.VMEM)] * 3,
        out_shape=jax.ShapeDtypeStruct((8, D), F32),
        scratch_shapes=[
            pltpu.VMEM((16, 3 * D), BF16),
            pltpu.VMEM((LO, pairs * D), BF16),
            pltpu.VMEM((16, D), F32),
        ],
        compiler_params=pltpu.CompilerParams(vmem_limit_bytes=48 * 1024 * 1024),
        cost_estimate=cost_of(recv.size * 100000),
        name="points_back",
    )(held, recv, par, cell_grads)


def update(shares, params, first_moment, second_moment):
    rows = params.shape[0]
    count = shares.shape[0]
    share = (shares.shape[1] - 16) // 2
    moves = [
        (1, GRAD_ROWS, 6, 65),
        (1, 0, POINT_ROWS, LAYER_ROWS),
        (0, 0, POINT_ROWS + LAYER_ROWS, LAYER_ROWS),
    ]

    def kernel(got, par, mom1, mom2, norm_ref, new_par, new1, new2, low, rms, two, one, grad):
        def unpack(s, point):
            v = got[s].astype(F32)
            at = pl.multiple_of(s * share, 8)
            two[pl.ds(at, share), :] = v[:share]
            one[pl.ds(at, share), :] = v[share : 2 * share]
            return point + v[2 * share : 2 * share + 8]

        grad[0:8, :] = lax.fori_loop(0, count, unpack, jnp.zeros((8, D), F32), unroll=4)
        for which, src, dst, length in moves:
            grad[pl.ds(dst, length), :] = (two, one)[which][pl.ds(src, length), :]
        g = grad[...]
        norm = jnp.sqrt(jnp.sum(g * g))
        norm_ref[0, 0] = norm
        factor = jnp.minimum(1.0, clip_norm / (norm + 1e-06))
        clipped = g * factor
        first = beta_one * mom1[...] + (1.0 - beta_one) * clipped
        second = beta_two * mom2[...] + (1.0 - beta_two) * clipped * clipped
        new1[...] = first
        new2[...] = second
        first_hat = first / (1.0 - beta_one**step_count)
        second_hat = second / (1.0 - beta_two**step_count)
        p = par[...]
        p = p - learn_rate * (first_hat / (jnp.sqrt(second_hat) + adam_eps) + decay_rate * p)
        new_par[...] = p
        low[...] = p.astype(BF16)
        stats = jnp.concatenate(
            [one[LAYER_ROWS : LAYER_ROWS + 3, :], two[LAYER_ROWS : LAYER_ROWS + 5, :]], axis=0
        )
        live = jnp.sum(one[LAYER_ROWS + 3 : LAYER_ROWS + 4, :], axis=1, keepdims=True)
        sums = jnp.sum(stats, axis=1, keepdims=True)
        rms[...] = jnp.broadcast_to(jnp.sqrt(sums / jnp.maximum(live, D)), (8, D))

    shape = jax.ShapeDtypeStruct
    flat = shape((rows, D), F32)
    return pl.pallas_call(
        kernel,
        out_specs=[pl.BlockSpec(memory_space=pltpu.SMEM)]
        + [pl.BlockSpec(memory_space=pltpu.VMEM)] * 5,
        out_shape=[shape((1, 1), F32), flat, flat, flat, shape((rows, D), BF16), shape((8, D), F32)],
        scratch_shapes=[pltpu.VMEM((count * share, D), F32)] * 2 + [pltpu.VMEM((rows, D), F32)],
        compiler_params=pltpu.CompilerParams(vmem_limit_bytes=48 * 1024 * 1024),
        name="update",
    )(shares, params, first_moment, second_moment)


def shifted(x, axes, by):
    if len(axes) == 1:
        count = lax.axis_size(axes[0])
        return lax.ppermute(x, axes[0], [(i, (i + by) % count) for i in range(count)])
    tiles, rows = lax.axis_size(axes[0]), lax.axis_size(axes[1])
    pairs = [
        (i * rows + j, (i + by) % tiles * rows + (j + by) % rows)
        for i in range(tiles)
        for j in range(rows)
    ]
    return lax.ppermute(x, axes, pairs)


def exchange(row, col, cor, by):
    return (
        shifted(row, ("tile",), by),
        shifted(col, ("row",), by),
        shifted(cor, ("tile", "row"), by),
    )


def by_quads(grid, quads_x, quads_y):
    trailing = grid.shape[2:]
    grid = grid.reshape((quads_x, QS, quads_y, QS) + trailing)
    return jnp.swapaxes(grid, 1, 2).reshape((quads_x, quads_y, QC) + trailing)


def all_to_all(x):
    return lax.all_to_all(x, ("tile", "row"), split_axis=0, concat_axis=0, tiled=True)


def scatter_sum(x, count):
    return jnp.sum(all_to_all(x.reshape(count, x.shape[0] // count, D)), axis=0)


def local(
    point_feats,
    point_tile,
    point_cell,
    point_valid,
    pillar_frame,
    cotangent,
    params,
    first_moment,
    second_moment,
):
    tile_count = lax.axis_size("tile")
    row_count = lax.axis_size("row")
    device_count = tile_count * row_count
    extent_x, extent_y = pillar_frame.shape
    cell_count = extent_x * extent_y
    quads_x, quads_y = extent_x // QS, extent_y // QS
    quads = quads_x * quads_y
    points = point_cell.shape[0]
    capacity = 2 * points // tile_count
    par = params.reshape(-1, D)

    cot = by_quads(cotangent, quads_x, quads_y)
    cot_halos = exchange(cot[0], cot[:, 0], cot[0, :1], -1)

    shape = (points // BLOCK, BLOCK)
    send = bin_points(
        point_feats,
        point_tile.reshape(shape),
        point_cell.reshape(shape),
        point_valid.reshape(shape),
        tile_count,
        capacity,
        extent_y,
        quads_y,
    )
    recv = lax.all_to_all(send, "tile", split_axis=0, concat_axis=0, tiled=True)
    held = jnp.sum(recv[:, 11].astype(jnp.int32), axis=1)

    frames = by_quads(pillar_frame, quads_x, quads_y)
    frames = jnp.pad(frames, ((0, 0), (0, 0), (0, QP - QC)), constant_values=-1).reshape(-1)
    lanes = jnp.arange(D, dtype=jnp.int32)
    base_rows = (frames[:, None] == lanes[None] - (H1 + 1)).astype(F32)
    pillars, tags = encode_points(recv, held, par, base_rows, quads)
    pillars = pillars.reshape(quads_x, quads_y, QP, D)
    tags = tags.reshape(quads_x, quads_y, QC, D)
    tag_halos = exchange(tags[0], tags[:, 0], tags[0, :1], -1)

    first = first_layer(pillars, par, quads_x, quads_y)
    field, saved, sums_one = first[0], first[1:8], first[8]
    halos = exchange(*first[9:], -1)
    flags = jnp.stack(
        [
            (lax.axis_index("tile") == tile_count - 1).astype(jnp.int32),
            (lax.axis_index("row") == row_count - 1).astype(jnp.int32),
        ]
    )
    step = device_count * 8
    grad_rows = -(-(GRAD_ROWS + 72) // step) * step
    grads, grad_two, g_row, g_col, g_cor = second_layer(
        flags,
        field,
        halos,
        tags,
        tag_halos,
        cot,
        cot_halos,
        par,
        1.0 / (cell_count * device_count),
        grad_rows,
    )
    grad_two, grad_halos = lax.optimization_barrier((grad_two, exchange(g_row, g_col, g_cor, 1)))
    sum_two = scatter_sum(grad_two, device_count)
    cell_grads, grad_one = first_layer_back(
        grads, grad_halos, pillars, saved, sums_one, par, grad_rows
    )
    grad_one, sum_two = lax.optimization_barrier((grad_one, sum_two))
    sum_one = scatter_sum(grad_one, device_count)
    grad_pin = points_back(recv, held, par, cell_grads.reshape(quads * QP, D))
    share = jnp.concatenate([sum_two, sum_one, grad_pin, jnp.zeros((8, D), F32)], axis=0)
    share = share.astype(BF16)
    total = all_to_all(jnp.broadcast_to(share[None], (device_count,) + share.shape))
    norm, new_params, new_first, new_second, low, rms = update(
        total, par, first_moment.reshape(-1, D), second_moment.reshape(-1, D)
    )
    return (
        norm[0, 0],
        new_params.reshape(-1),
        new_first.reshape(-1),
        new_second.reshape(-1),
        low.reshape(-1),
        rms[:6, 0],
    )


def solution(mesh):
    return jax.shard_map(
        local,
        mesh=mesh,
        in_specs=(
            P(None, ("tile", "row")),
            P(("tile", "row"), None),
            P(("tile", "row")),
            P(("tile", "row")),
            P("tile", "row"),
            P("tile", "row", None),
            P(),
            P(),
            P(),
        ),
        out_specs=(P(), P(), P(), P(), P(), P()),
        check_vma=False,
    )
```

```python
import jax
import jax.numpy as jnp
from jax import lax
from jax.experimental import pallas as pl
from jax.experimental.pallas import tpu as pltpu
from jax.sharding import PartitionSpec as P

D = 128
HEADS = 8
HD = 16
FF = 256
H1 = 64
WIN = 12
C_IN = 11
QS = 6
QC = 36
QP = 40
SLOTS = 144
KEYS = HEADS * SLOTS
LAYER_ROWS = 1034
POINT_ROWS = 71
GRAD_ROWS = 1040
BLOCK = 128
CHUNK = 512
LO = 512
NW = 8

clip_norm = 0.01
beta_one = 0.9
beta_two = 0.999
step_count = 10
learn_rate = 0.1
decay_rate = 0.05
adam_eps = 1e-08

F32 = jnp.float32
BF16 = jnp.bfloat16
GELU_C = 0.7978845608028654
GELU_A = 0.044715


def mm(a, b):
    return lax.dot_general(a, b, (((1,), (0,)), ((), ())), preferred_element_type=F32)


def mm_nt(a, b):
    return lax.dot_general(a, b, (((1,), (1,)), ((), ())), preferred_element_type=F32)


def mm_tn(a, b):
    return lax.dot_general(a, b, (((0,), (0,)), ((), ())), preferred_element_type=F32)


def lane_iota(rows=1):
    return lax.broadcasted_iota(jnp.int32, (rows, D), 1)


def part8(v):
    return jnp.sum(v.reshape(v.shape[0] // 8, 8, v.shape[1]), axis=0)


def gelu_parts(v):
    sq = v * v
    t = jnp.tanh(v * (GELU_C + (GELU_C * GELU_A) * sq))
    half = 0.5 + 0.5 * t
    slope = half + (0.5 * v) * (1.0 - t * t) * (GELU_C + (3.0 * GELU_C * GELU_A) * sq)
    return v * half, slope


def gelu_only(v):
    t = jnp.tanh(v * (GELU_C + (GELU_C * GELU_A) * (v * v)))
    return v * (0.5 + 0.5 * t)


def normalize(y):
    center = y - jnp.mean(y, axis=-1, keepdims=True)
    rs = lax.rsqrt(jnp.mean(center * center, axis=-1, keepdims=True) + 1e-05)
    return center * rs, rs


def norm_pull(gx, xhat, rs):
    return rs * (
        gx
        - jnp.mean(gx, axis=-1, keepdims=True)
        - xhat * jnp.mean(gx * xhat, axis=-1, keepdims=True)
    )


def load_layer(par, base, w):
    for part in range(3):
        m = par[pl.ds(base + part, D, stride=3), :]
        w["qkv"][:, part * D : (part + 1) * D] = m.astype(BF16)
        if "qkv_t" in w:
            w["qkv_t"][part * D : (part + 1) * D, :] = m.T.astype(BF16)
    m = par[pl.ds(base + 384, D), :]
    w["out"][...] = m.astype(BF16)
    if "out_t" in w:
        w["out_t"][...] = m.T.astype(BF16)
    for part in range(2):
        m = par[pl.ds(base + 512 + part, D, stride=2), :]
        w["fin"][:, part * D : (part + 1) * D] = m.astype(BF16)
        if "fin_t" in w:
            w["fin_t"][part * D : (part + 1) * D, :] = m.T.astype(BF16)
        m = par[pl.ds(base + 768 + part * D, D), :]
        w["fout"][part * D : (part + 1) * D, :] = m.astype(BF16)
        if "fout_t" in w:
            w["fout_t"][:, part * D : (part + 1) * D] = m.T.astype(BF16)


WEIGHT_SHAPES = {
    "qkv": (D, 3 * D),
    "qkv_t": (3 * D, D),
    "out": (D, D),
    "out_t": (D, D),
    "fin": (D, FF),
    "fin_t": (FF, D),
    "fout": (FF, D),
    "fout_t": (D, FF),
}


def vec(par, base, row):
    return par[base + 1024 + row : base + 1025 + row, :]


def vec2(par, base, row):
    return jnp.concatenate([vec(par, base, row), vec(par, base, row + 1)], axis=1)


def fold_rows():
    return one_hot(lax.broadcasted_iota(jnp.int32, (HD, D), 0) == lane_iota(HD) % HD)


def own_head():
    return lax.broadcasted_iota(jnp.int32, (D, D), 0) // HD == lane_iota(D) // HD


def turned(v):
    return v.astype(F32).T


def head_cols(v):
    top = turned(v[:D]).astype(BF16)
    none = jnp.zeros((HD, D), BF16)
    pairs = []
    for t in range(0, D, 2 * HD):
        left = jnp.concatenate([top[t : t + HD], none], axis=0)
        right = jnp.concatenate([none, top[t + HD : t + 2 * HD]], axis=0)
        pairs.append(jnp.concatenate([left, right], axis=1))
    return pairs, jnp.where(own_head(), mm_tn(v[D:], fold_rows()), 0.0).astype(BF16)


def by_head(rows, cols):
    pairs, rest = cols
    parts = []
    for t in range(HEADS // 2):
        both = mm(rows[:, 2 * HD * t : 2 * HD * (t + 1)], pairs[t])
        parts = parts + [both[:, :D], both[:, D:]]
    return parts + [mm(rows, rest)]


def head_sums(cols, parts):
    pairs, rest = cols
    sums = [
        mm_nt(pairs[t], jnp.concatenate(parts[2 * t : 2 * t + 2], axis=1)) for t in range(HEADS // 2)
    ]
    return (jnp.concatenate(sums, axis=0) + mm_nt(rest, parts[HEADS])).T.astype(BF16)


def window_bias(groups):
    keys = jnp.concatenate(
        [groups[:D]] + [groups[D:]] * HEADS + [jnp.ones((D, D), BF16)], axis=0
    )
    same = mm_nt(groups, keys)
    rows = lax.broadcasted_iota(jnp.int32, (SLOTS, D), 0)
    lanes = lane_iota(SLOTS)
    first = (same[:, :D] > 0.5) | (rows == lanes)
    last = (same[:, D : 2 * D] > 0.5) | (rows == lanes % HD + D)
    return (
        jnp.where(first, 0.0, -1000000000.0),
        jnp.where(last, 0.0, -1000000000.0),
        same[:, 2 * D :],
    )


def attend(qs, key, val, bias_first, bias_last):
    probs = []
    cols = head_cols(qs)
    yield
    parts = by_head(key, cols)
    yield
    for h, part in enumerate(parts):
        part = part + (bias_first if h < HEADS else bias_last)
        expo = jnp.exp(part - jnp.max(part, axis=0, keepdims=True))
        probs.append((expo * (1.0 / jnp.sum(expo, axis=0, keepdims=True))).astype(BF16))
    yield
    mix = yield from query_pull(val, probs)
    return probs, mix


def attend_pull(probs, qs, key, val, gmix):
    cols = head_cols(gmix)
    gs = []
    yield
    parts = by_head(val, cols)
    yield
    g_val = head_sums(cols, probs)
    yield
    for p_low, pulled in zip(probs, parts):
        p = p_low.astype(F32)
        both = p * pulled
        gs.append((both - p * jnp.sum(both, axis=0, keepdims=True)).astype(BF16))
    yield
    g_key = head_sums(head_cols(qs), gs)
    yield
    g_query = yield from query_pull(key * 0.25, gs)
    return g_query, g_key, g_val


def query_pull(rows, parts):
    flat = turned(rows).astype(BF16)
    tops = []
    for t in range(HEADS // 2):
        at = 2 * HD * t
        both = mm(flat[at : at + 2 * HD], jnp.concatenate(parts[2 * t : 2 * t + 2], axis=1))
        tops = tops + [both[:HD, :D], both[HD:, D:]]
    top = jnp.concatenate(tops, axis=0)
    rest = jnp.where(own_head(), mm(flat, parts[HEADS]), 0.0).astype(BF16)
    yield
    return jnp.concatenate([top.T.astype(BF16), mm_nt(fold_rows(), rest).astype(BF16)], axis=0)


def in_step(runs):
    results = [None] * len(runs)
    active = list(range(len(runs)))
    while active:
        for i in list(active):
            try:
                next(runs[i])
            except StopIteration as end:
                results[i] = end.value
                active.remove(i)
    return results


def split_qkv(packed, w):
    rows = slice(w * SLOTS, (w + 1) * SLOTS)
    return packed[rows, :D] * 0.25, packed[rows, D : 2 * D], packed[rows, 2 * D :]


def layer_forward(x, groups, par, base, w, sums):
    count = x.shape[0] // SLOTS
    low = x.astype(BF16)
    qkv_bias = jnp.concatenate(
        [vec(par, base, 0), jnp.zeros((1, D), F32), vec(par, base, 1)], axis=1
    )
    packed = (mm(low, w["qkv"][...]) + qkv_bias).astype(BF16)
    masks = [window_bias(group) for group in groups]
    done = in_step([attend(*split_qkv(packed, i), *masks[i][:2]) for i in range(count)])
    probs = [d[0] for d in done]
    mixes = [d[1] for d in done]
    lives = [m[2] for m in masks]
    mix = jnp.concatenate(mixes, axis=0)
    live = jnp.concatenate(lives, axis=0)
    attn_out = mm(mix, w["out"][...]) + vec(par, base, 2)
    first = x + attn_out
    xhat1, rs1 = normalize(first)
    normed = (xhat1 * vec(par, base, 3) + vec(par, base, 4)) * live
    normed_low = normed.astype(BF16)
    pre = mm(normed_low, w["fin"][...]) + vec2(par, base, 5)
    act, slope = gelu_parts(pre)
    hidden = act.astype(BF16)
    ffn = mm(hidden, w["fout"][...]) + vec(par, base, 7)
    second = normed + ffn
    xhat2, rs2 = normalize(second)
    result = (xhat2 * vec(par, base, 8) + vec(par, base, 9)) * live
    sums[0] += part8(attn_out * attn_out * live)
    sums[1] += part8(ffn * ffn * live)
    sums[2] += part8(result * result)
    sums[3] += part8(live)
    return dict(
        low=low,
        packed=packed,
        probs=probs,
        mix=mix,
        live=live,
        first=first,
        second=second,
        xhat1=xhat1,
        rs1=rs1,
        xhat2=xhat2,
        rs2=rs2,
        normed_low=normed_low,
        slope=slope,
        hidden=hidden,
        result=result,
    )


def layer_backward(grad, k, par, base, w, acc):
    live = k["live"]
    gl = grad * live
    acc["vec"][8] += part8(gl * k["xhat2"])
    acc["vec"][9] += part8(gl)
    g2 = norm_pull(gl * vec(par, base, 8), k["xhat2"], k["rs2"])
    g_ffn = g2.astype(BF16)
    acc["fout"][...] += mm_tn(k["hidden"], g_ffn)
    acc["vec"][7] += part8(g_ffn.astype(F32))
    g_pre = (mm(g_ffn, w["fout_t"][...]) * k["slope"]).astype(BF16)
    acc["fin"][...] += mm_tn(k["normed_low"], g_pre)
    for part in range(2):
        acc["vec"][5 + part] += part8(g_pre[:, part * D : (part + 1) * D].astype(F32))
    g_norm = (g2 + mm(g_pre, w["fin_t"][...])) * live
    acc["vec"][3] += part8(g_norm * k["xhat1"])
    acc["vec"][4] += part8(g_norm)
    g1 = norm_pull(g_norm * vec(par, base, 3), k["xhat1"], k["rs1"])
    g_attn = g1.astype(BF16)
    acc["out"][...] += mm_tn(k["mix"], g_attn)
    acc["vec"][2] += part8(g_attn.astype(F32))
    g_mix = mm(g_attn, w["out_t"][...]).astype(BF16)
    runs = []
    for i in range(grad.shape[0] // SLOTS):
        rows = slice(i * SLOTS, (i + 1) * SLOTS)
        runs.append(attend_pull(k["probs"][i], *split_qkv(k["packed"], i), g_mix[rows]))
    pieces = [jnp.concatenate(parts, axis=1) for parts in in_step(runs)]
    g_packed = jnp.concatenate(pieces, axis=0)
    acc["qkv"][...] += mm_tn(k["low"], g_packed)
    acc["vec"][0] += part8(g_packed[:, :D].astype(F32))
    acc["vec"][1] += part8(g_packed[:, 2 * D :].astype(F32))
    return g1 + mm(g_packed, w["qkv_t"][...])


ACC_SHAPES = {
    "qkv": (D, 3 * D),
    "out": (D, D),
    "fin": (D, FF),
    "fout": (FF, D),
    "vec": (10, 8, D),
}


def clear(acc):
    for ref in acc.values():
        ref[...] = jnp.zeros(ref.shape, ref.dtype)


def store_grads(acc, sums, out):
    for part in range(3):
        out[pl.ds(part, D, stride=3), :] = acc["qkv"][:, part * D : (part + 1) * D]
    out[pl.ds(384, D), :] = acc["out"][...]
    for part in range(2):
        out[pl.ds(512 + part, D, stride=2), :] = acc["fin"][:, part * D : (part + 1) * D]
    out[pl.ds(768, FF), :] = acc["fout"][...]
    out[pl.ds(1024, 16), :] = jnp.concatenate(
        [jnp.sum(acc["vec"][i], axis=0, keepdims=True) for i in range(10)]
        + [jnp.sum(sums[i], axis=0, keepdims=True) for i in range(4)]
        + [jnp.zeros((2, D), F32)],
        axis=0,
    )


def gather_windows(scratch, pick):
    for i in range(NW):
        for r in range(2):
            for c in range(2):
                at = i * SLOTS + (2 * r + c) * QC
                scratch[pl.ds(at, QC), :] = pick(r, 2 * i + c)
    return scratch[...]


def spread_windows(scratch, value, put):
    scratch[...] = value
    for i in range(NW):
        for r in range(2):
            for c in range(2):
                put(r, 2 * i + c, scratch[pl.ds(i * SLOTS + (2 * r + c) * QC, QC), :])


def whole(shape, space=pltpu.VMEM):
    return pl.BlockSpec(shape, lambda *_: (0,) * len(shape), memory_space=space)


def params_for(limit=56):
    return pltpu.CompilerParams(
        dimension_semantics=("arbitrary",), vmem_limit_bytes=limit * 1024 * 1024
    )


def cost_of(flops):
    return pl.CostEstimate(flops=flops, bytes_accessed=1 << 24, transcendentals=0)


def first_layer(pillars, par, quads_x, quads_y):
    across = quads_x // 2
    along = quads_y // (2 * NW)
    windows = quads_x * quads_y // 4
    base = POINT_ROWS

    def kernel(pil, par_ref, *refs):
        outs, scratch = refs[:12], refs[12:]
        (
            field,
            probs_out,
            packed_out,
            mix_out,
            first_out,
            second_out,
            low_out,
            live_out,
            sums_out,
            row_out,
            col_out,
            cor_out,
        ) = outs
        names = ["qkv", "out", "fin", "fout"]
        w = dict(zip(names, scratch[:4]))
        wide, pout, sums = scratch[4:]
        step = pl.program_id(0)
        a = step // along
        b = step % along

        @pl.when(step == 0)
        def _():
            load_layer(par_ref, base, w)
            m = par_ref[pl.ds(6, H1), :].astype(BF16)
            pout[...] = jnp.concatenate([m, m], axis=0)
            sums[...] = jnp.zeros(sums.shape, F32)

        cells = gather_windows(wide, lambda r, c: pil[r, c, :QC, :])
        lanes = lane_iota()
        total = jnp.where(lanes < H1, cells, 0.0)
        count = cells[:, H1 : H1 + 1]
        high = total.astype(BF16).astype(F32)
        both = (high + pltpu.roll(total - high, H1, axis=1)).astype(BF16)
        pillar = mm(both, pout[...]) + count * par_ref[70:71, :]
        x = pillar / jnp.maximum(count, 1.0)
        onehot = jnp.where((lanes > H1) & (lanes < H1 + 4) & (count > 0.0), cells, 0.0).astype(BF16)
        groups = [onehot[i * SLOTS : (i + 1) * SLOTS] for i in range(NW)]
        k = layer_forward(x, groups, par_ref, base, w, sums)
        for i in range(NW):
            rows = slice(i * SLOTS, (i + 1) * SLOTS)
            for h in range(HEADS + 1):
                probs_out[i, :, h * D : (h + 1) * D] = k["probs"][i][h]
            packed_out[i] = k["packed"][rows]
            mix_out[i] = k["mix"][rows]
            first_out[i] = k["first"][rows]
            second_out[i] = k["second"][rows]
            low_out[i] = k["low"][rows]
            live_out[i] = k["live"][rows]

        def put(r, c, v):
            field[r, c, :QC, :] = v

        spread_windows(wide, k["result"], put)

        @pl.when(a == 0)
        def _():
            for c in range(2 * NW):
                row_out[c] = field[0, c, :QC, :].astype(BF16)

        @pl.when(b == 0)
        def _():
            for r in range(2):
                col_out[r] = field[r, 0, :QC, :].astype(BF16)

        @pl.when(step == 0)
        def _():
            cor_out[0] = field[0, 0, :QC, :].astype(BF16)

        @pl.when(step == pl.num_programs(0) - 1)
        def _():
            sums_out[...] = sums[...]

    def win_spec(width):
        return pl.BlockSpec((NW, SLOTS, width), lambda s: (s, 0, 0))

    quad_spec = pl.BlockSpec((2, 2 * NW, QP, D), lambda s: (s // along, s % along, 0, 0))
    shape = jax.ShapeDtypeStruct
    return pl.pallas_call(
        kernel,
        grid=(across * along,),
        in_specs=[quad_spec, whole(par.shape)],
        out_specs=[
            quad_spec,
            win_spec(KEYS),
            win_spec(3 * D),
            win_spec(D),
            win_spec(D),
            win_spec(D),
            win_spec(D),
            win_spec(D),
            whole((4, 8, D)),
            pl.BlockSpec((2 * NW, QC, D), lambda s: (jnp.minimum(s, along - 1), 0, 0)),
            pl.BlockSpec((2, QC, D), lambda s: (s // along, 0, 0)),
            whole((1, QC, D)),
        ],
        out_shape=[
            shape((quads_x, quads_y, QP, D), F32),
            shape((windows, SLOTS, KEYS), BF16),
            shape((windows, SLOTS, 3 * D), BF16),
            shape((windows, SLOTS, D), BF16),
            shape((windows, SLOTS, D), F32),
            shape((windows, SLOTS, D), F32),
            shape((windows, SLOTS, D), BF16),
            shape((windows, SLOTS, D), F32),
            shape((4, 8, D), F32),
            shape((quads_y, QC, D), BF16),
            shape((quads_x, QC, D), BF16),
            shape((1, QC, D), BF16),
        ],
        scratch_shapes=[pltpu.VMEM(WEIGHT_SHAPES[n], BF16) for n in ["qkv", "out", "fin", "fout"]]
        + [
            pltpu.VMEM((NW * SLOTS, D), F32),
            pltpu.VMEM((D, D), BF16),
            pltpu.VMEM((4, 8, D), F32),
        ],
        compiler_params=params_for(),
        name="first_layer",
    )(pillars, par)


def second_layer(flags, field, halos, tags, tag_halos, cot, cot_halos, par, scale, grad_rows):
    quads_x, quads_y = field.shape[:2]
    across = quads_x // 2
    along = quads_y // (2 * NW)
    base = POINT_ROWS + LAYER_ROWS
    wnames = list(WEIGHT_SHAPES)
    anames = list(ACC_SHAPES)

    def kernel(flag, *refs):
        ins, refs = refs[:13], refs[13:]
        outs, scratch = refs[:5], refs[5:]
        fields, tagss, cots, par_ref = ins[:4], ins[4:8], ins[8:12], ins[12]
        grads, weights, row_out, col_out, cor_out = outs
        w = dict(zip(wnames, scratch))
        scratch = scratch[len(wnames) :]
        acc = dict(zip(anames, scratch))
        wide, sums, ext_x, ext_t, ext_g = scratch[len(anames) :]
        step = pl.program_id(0)
        a = step // along
        b = step % along

        @pl.when(step == 0)
        def _():
            load_layer(par_ref, base, w)
            sums[...] = jnp.zeros(sums.shape, F32)
            clear(acc)
            lanes = lane_iota()

            def moved(v, region):
                return pltpu.roll(v, 3 * region, axis=1)

            def fill(ext, srcs, turn_row, turn_col, turn_cor):
                main, row, col, cor = srcs

                def one(i, _):
                    ext[i // quads_y, i % quads_y, :QC, :] = main[
                        i // quads_y, i % quads_y, :QC, :
                    ].astype(F32)
                    return 0

                lax.fori_loop(0, quads_x * quads_y, one, 0, unroll=4)

                def one_row(i, _):
                    ext[quads_x, i, :QC, :] = turn_row(row[i].astype(F32))
                    return 0

                lax.fori_loop(1, quads_y, one_row, 0)
                for i in range(1, quads_x):
                    ext[i, quads_y, :QC, :] = turn_col(col[i].astype(F32))
                ext[quads_x, quads_y, :QC, :] = turn_cor(cor[0].astype(F32))

            def same(v):
                return v

            last_x = flag[0] > 0
            last_y = flag[1] > 0

            def tag_row(v):
                return jnp.where(last_x, moved(v, 2), v)

            def tag_col(v):
                return jnp.where(last_y, moved(v, 1), v)

            fill(ext_x, fields, same, same, same)
            fill(ext_t, tagss, tag_row, tag_col, lambda v: tag_row(tag_col(v)))
            fill(ext_g, cots, same, same, same)

        def picker(ext):
            return lambda r, c: ext[2 * a + 1 + r, 2 * NW * b + 1 + c, :QC, :]

        tag = gather_windows(wide, picker(ext_t)).astype(BF16)
        groups = [tag[i * SLOTS : (i + 1) * SLOTS] for i in range(NW)]
        x = gather_windows(wide, picker(ext_x))
        k = layer_forward(x, groups, par_ref, base, w, sums)
        grad = gather_windows(wide, picker(ext_g)) * scale
        gx = layer_backward(grad, k, par_ref, base, w, acc)

        def put(r, c, v):
            grads[r, c, :QC, :] = v

        spread_windows(wide, gx, put)

        @pl.when(a == across - 1)
        def _():
            for c in range(2 * NW):
                row_out[c] = grads[1, c, :QC, :].astype(BF16)

        @pl.when(b == along - 1)
        def _():
            for r in range(2):
                col_out[r] = grads[r, 2 * NW - 1, :QC, :].astype(BF16)

        @pl.when(step == pl.num_programs(0) - 1)
        def _():
            cor_out[0] = grads[1, 2 * NW - 1, :QC, :].astype(BF16)
            store_grads(acc, sums, weights)

    shape = jax.ShapeDtypeStruct
    quad_spec = pl.BlockSpec((2, 2 * NW, QP, D), lambda s: (s // along, s % along, 0, 0))
    ext = pltpu.VMEM((quads_x + 1, quads_y + 1, QP, D), F32)
    arrays = [field, *halos, tags, *tag_halos, cot, *cot_halos, par]
    return pl.pallas_call(
        kernel,
        grid=(across * along,),
        in_specs=[pl.BlockSpec(memory_space=pltpu.SMEM)] + [whole(v.shape) for v in arrays],
        out_specs=[
            quad_spec,
            whole((grad_rows, D)),
            pl.BlockSpec(
                (2 * NW, QC, D), lambda s: (jnp.maximum(s - (across - 1) * along, 0), 0, 0)
            ),
            pl.BlockSpec((2, QC, D), lambda s: (s // along, 0, 0)),
            whole((1, QC, D)),
        ],
        out_shape=[
            shape((quads_x, quads_y, QP, D), F32),
            shape((grad_rows, D), F32),
            shape((quads_y, QC, D), BF16),
            shape((quads_x, QC, D), BF16),
            shape((1, QC, D), BF16),
        ],
        scratch_shapes=[pltpu.VMEM(WEIGHT_SHAPES[n], BF16) for n in wnames]
        + [pltpu.VMEM(ACC_SHAPES[n], F32) for n in anames]
        + [
            pltpu.VMEM((NW * SLOTS, D), F32),
            pltpu.VMEM((4, 8, D), F32),
            ext,
            ext,
            ext,
        ],
        compiler_params=params_for(),
        name="second_layer",
    )(flags, *arrays)


def first_layer_back(grads, halos, pillars, saved, sums, par, grad_rows):
    quads_x, quads_y = grads.shape[:2]
    across = quads_x // 2
    along = quads_y // (2 * NW)
    base = POINT_ROWS
    wnames = list(WEIGHT_SHAPES)
    anames = list(ACC_SHAPES)

    def kernel(*refs):
        ins, refs = refs[:14], refs[14:]
        outs, scratch = refs[:2], refs[2:]
        main, row, col, cor, pil = ins[:5]
        probs, packed, mix, first, second, low, live = ins[5:12]
        sums_ref, par_ref = ins[12:]
        cell_out, weights = outs
        w = dict(zip(wnames, scratch))
        scratch = scratch[len(wnames) :]
        acc = dict(zip(anames, scratch))
        wide, ext, pout_t, pacc = scratch[len(anames) :]
        step = pl.program_id(0)
        a = step // along
        b = step % along

        @pl.when(step == 0)
        def _():
            load_layer(par_ref, base, w)
            clear(acc)
            pacc[...] = jnp.zeros(pacc.shape, F32)
            m = par_ref[pl.ds(6, H1), :]
            pout_t[...] = jnp.concatenate([m, m], axis=0).T.astype(BF16)
            for r in range(1, quads_x):

                def one(i, _):
                    ext[r, i, :QC, :] = main[r - 1, i - 1, :QC, :]
                    return 0

                lax.fori_loop(1, quads_y, one, 0)
                ext[r, 0, :QC, :] = col[r - 1].astype(F32)

            def one_row(i, _):
                ext[0, i, :QC, :] = row[i - 1].astype(F32)
                return 0

            lax.fori_loop(1, quads_y, one_row, 0)
            ext[0, 0, :QC, :] = cor[0].astype(F32)

        grad = gather_windows(wide, lambda r, c: ext[2 * a + r, 2 * NW * b + c, :QC, :])

        def rows_of(ref):
            return jnp.concatenate([ref[i] for i in range(NW)], axis=0)

        k = dict(
            low=rows_of(low),
            packed=rows_of(packed),
            probs=[
                [probs[i, :, h * D : (h + 1) * D] for h in range(HEADS + 1)] for i in range(NW)
            ],
            mix=rows_of(mix),
            live=rows_of(live),
        )
        k["xhat1"], k["rs1"] = normalize(rows_of(first))
        k["xhat2"], k["rs2"] = normalize(rows_of(second))
        normed = (k["xhat1"] * vec(par_ref, base, 3) + vec(par_ref, base, 4)) * k["live"]
        k["normed_low"] = normed.astype(BF16)
        act, k["slope"] = gelu_parts(mm(k["normed_low"], w["fin"][...]) + vec2(par_ref, base, 5))
        k["hidden"] = act.astype(BF16)
        gx = layer_backward(grad, k, par_ref, base, w, acc)

        cells = gather_windows(wide, lambda r, c: pil[r, c, :QC, :])
        lanes = lane_iota()
        total = jnp.where(lanes <= H1, cells, 0.0)
        g_pillar = (gx / jnp.maximum(cells[:, H1 : H1 + 1], 1.0)).astype(BF16)
        high = total.astype(BF16)
        rest = (total - high.astype(F32)).astype(BF16)
        pacc[...] += mm_tn(high, g_pillar) + mm_tn(rest, g_pillar)

        def put(r, c, v):
            cell_out[r, c, :QC, :] = v
            cell_out[r, c, QC:, :] = jnp.zeros((QP - QC, D), F32)

        spread_windows(wide, mm(g_pillar, pout_t[...]), put)

        @pl.when(step == pl.num_programs(0) - 1)
        def _():
            store_grads(acc, sums_ref, weights)
            weights[GRAD_ROWS : GRAD_ROWS + 72, :] = pacc[:72, :]

    def win_spec(width):
        return pl.BlockSpec((NW, SLOTS, width), lambda s: (s, 0, 0))

    shape = jax.ShapeDtypeStruct
    quad_spec = pl.BlockSpec((2, 2 * NW, QP, D), lambda s: (s // along, s % along, 0, 0))
    return pl.pallas_call(
        kernel,
        grid=(across * along,),
        in_specs=[whole(grads.shape)]
        + [whole(v.shape) for v in halos]
        + [quad_spec]
        + [win_spec(v.shape[2]) for v in saved]
        + [whole(sums.shape), whole(par.shape)],
        out_specs=[quad_spec, whole((grad_rows, D))],
        out_shape=[shape((quads_x, quads_y, QP, D), F32), shape((grad_rows, D), F32)],
        scratch_shapes=[pltpu.VMEM(WEIGHT_SHAPES[n], BF16) for n in wnames]
        + [pltpu.VMEM(ACC_SHAPES[n], F32) for n in anames]
        + [
            pltpu.VMEM((NW * SLOTS, D), F32),
            pltpu.VMEM((quads_x, quads_y, QP, D), F32),
            pltpu.VMEM((D, D), BF16),
            pltpu.VMEM((D, D), F32),
        ],
        compiler_params=params_for(),
        cost_estimate=cost_of(grads.size * 12000),
        name="first_layer_back",
    )(grads, *halos, pillars, *saved, sums, par)


def one_hot(hit):
    return jnp.where(hit, 1.0, 0.0).astype(BF16)


def bin_points(feats, tiles, cells, valid, tile_count, capacity, extent_y, quads_y):
    blocks = tiles.shape[0]
    groups = tile_count * capacity // LO
    lots = 8
    wide = lots * BLOCK

    def kernel(feat_ref, tile_ref, cell_ref, valid_ref, out_ref, slot_ref, code_ref, acc):
        real = valid_ref[...] > 0
        t = jnp.where(real, tile_ref[...], tile_count)
        i0 = lax.broadcasted_iota(jnp.int32, (BLOCK, BLOCK), 0)
        i1 = lax.broadcasted_iota(jnp.int32, (BLOCK, BLOCK), 1)
        upto = one_hot(i0 <= i1)
        j0 = lax.broadcasted_iota(jnp.int32, (blocks, blocks), 0)
        j1 = lax.broadcasted_iota(jnp.int32, (blocks, blocks), 1)
        earlier = one_hot(j1 < j0)
        slot = jnp.full((blocks, BLOCK), -1.0, F32)
        for k in range(tile_count):
            hit = t == k
            run = mm(one_hot(hit), upto)
            total = jnp.broadcast_to(run[:, BLOCK - 1 :], (blocks, D)).astype(BF16)
            at = mm(earlier, total)[:, :1] + (k * capacity - 1.0)
            slot = jnp.where(hit, run + at, slot)
        slot_ref[...] = slot.astype(jnp.int32)

        def part(v, by):
            return ((v.astype(F32) + 0.5) * (1.0 / by)).astype(jnp.int32)

        cell = cell_ref[...]
        cx = part(cell, extent_y)
        cy = cell - cx * extent_y
        qx, qy = part(cx, QS), part(cy, QS)
        row = (qx * quads_y + qy) * QP + (cx - qx * QS) * QS + (cy - qy * QS)
        hi = row // LO
        lo = row - hi * LO
        low_part = lo % 256
        code_ref[0] = jnp.where(real, 1.0, 0.0)
        code_ref[1] = (hi + 1).astype(F32)
        code_ref[2] = (lo - low_part).astype(F32)
        code_ref[3] = low_part.astype(F32)
        acc[...] = jnp.zeros(acc.shape, F32)
        span = lax.broadcasted_iota(jnp.int32, (LO, wide), 0)

        def one(j, _):
            def line(ref, *lead):
                return jnp.concatenate(
                    [ref[(*lead, pl.ds(j * lots + u, 1), slice(None))] for u in range(lots)], axis=1
                )

            at = line(slot_ref)
            feat = feat_ref[:, pl.ds(pl.multiple_of(j * wide, wide), wide)].astype(F32)
            rows = jnp.concatenate(
                [feat] + [line(code_ref, i) for i in range(4)] + [jnp.zeros((1, wide), F32)], axis=0
            ).astype(BF16)
            group = at // LO
            place = one_hot(span == at % LO)
            spread = jnp.concatenate([rows * one_hot(group == g) for g in range(groups)], axis=0)
            acc[...] += mm_nt(spread, place)
            return 0

        lax.fori_loop(0, blocks // lots, one, 0)
        for k in range(tile_count):
            for at in range(0, capacity, LO):
                g, low = (k * capacity + at) // LO, (k * capacity + at) % LO
                size = min(LO, capacity)
                out_ref[k, :, at : at + size] = acc[g * 16 : g * 16 + 16, low : low + size].astype(
                    BF16
                )

    return pl.pallas_call(
        kernel,
        out_shape=jax.ShapeDtypeStruct((tile_count, 16, capacity), BF16),
        scratch_shapes=[
            pltpu.VMEM((blocks, BLOCK), jnp.int32),
            pltpu.VMEM((4, blocks, BLOCK), F32),
            pltpu.VMEM((groups * 16, LO), F32),
        ],
        compiler_params=pltpu.CompilerParams(vmem_limit_bytes=48 * 1024 * 1024),
        name="bin_points",
    )(feats, tiles, cells, valid)


def unpack_point_in(par_ref, win):
    lanes = lane_iota()
    flat = par_ref[0:6, :]
    turned = pltpu.roll(flat, H1, axis=1)
    even = jnp.where(lanes < H1, flat, turned)
    odd = jnp.where(lanes < H1, turned, flat)
    rows = []
    for k in range(C_IN):
        src = even if k % 2 == 0 else odd
        rows.append(src[k // 2 : k // 2 + 1])
    rows.append(jnp.zeros((5, D), F32))
    win[:, :D] = jnp.concatenate(rows, axis=0).astype(BF16)
    at = lax.broadcasted_iota(jnp.int32, (16, D), 0)
    win[:, D : 2 * D] = one_hot(at == 12)
    win[:, 2 * D :] = one_hot((at == 13) | (at == 14))
    return odd[5:6]


def list_chunks(held_ref, todo, sources, chunk, most):
    def source(s, n):
        def put(j, n):
            todo[n] = s * most + j
            return n + 1

        return lax.fori_loop(0, (held_ref[s] + chunk - 1) // chunk, put, n)

    todo[0] = 0
    return lax.fori_loop(0, sources, source, 0)


def two_stage(count, todo, most, prepare, finish, even, odd):
    def ready(i, buffers):
        item = todo[jnp.minimum(i, jnp.maximum(count - 1, 0))]
        prepare(item // most, item % most, jnp.where(i < count, 1.0, 0.0), buffers)

    def pair(k, _):
        ready(2 * k + 1, odd)
        finish(even)
        ready(2 * k + 2, even)
        finish(odd)
        return 0

    ready(0, even)
    lax.fori_loop(0, (count + 1) // 2, pair, 0)


def encode_points(recv, held, par, base_rows, quads):
    sources, _, capacity = recv.shape
    chunk = min(CHUNK, capacity)
    groups = -(-quads * QP // LO)
    pairs = -(-groups // 2)

    most = capacity // chunk

    def kernel(held_ref, recv_ref, par_ref, base_ref, out_ref, tag_ref, win, acc, todo, *buffers):
        bias = unpack_point_in(par_ref, win)
        acc[...] = jnp.zeros(acc.shape, F32)
        lanes = lane_iota()
        own = jnp.where(lanes < H1, 1.0, 2.0)
        count_of = (lanes + 1).astype(F32)
        span = lax.broadcasted_iota(jnp.int32, (LO, chunk), 0)

        def prepare(s, j, real, into):
            place, spread = into
            cols = recv_ref[s, :, pl.ds(pl.multiple_of(j * chunk, chunk), chunk)]
            wide = cols.astype(F32)
            place[...] = one_hot(span == (wide[13:14] + wide[14:15]).astype(jnp.int32))
            both = mm_tn(cols, win[:, : 2 * D])
            act = gelu_only(both[:, :D] + bias)
            group = both[:, D:] * real
            for g in range(pairs):
                spread[:, g * D : g * D + D] = jnp.where(group == own + 2.0 * g, act, 0.0).astype(
                    BF16
                )
            spread[:, pairs * D :] = one_hot(group == count_of)

        def finish_chunk(held):
            acc[...] += mm(held[0][...], held[1][...])

        count = list_chunks(held_ref, todo, sources, chunk, most)
        two_stage(count, todo, most, prepare, finish_chunk, buffers[:2], buffers[2:])
        for g in range(groups):
            rows = min(LO, quads * QP - g * LO)
            v = acc[:rows, g // 2 * D : g // 2 * D + D]
            if g % 2 == 1:
                v = pltpu.roll(v, H1, axis=1)
            count = acc[:rows, pairs * D + g : pairs * D + g + 1]
            v = jnp.where(lanes < H1, v, jnp.where(lanes == H1, count, 0.0))
            out_ref[g * LO : g * LO + rows, :] = v + base_ref[g * LO : g * LO + rows, :]

        def finish(i, _):
            total = out_ref[pl.ds(pl.multiple_of(i * QP, 8), QP), :]
            count = total[:, H1 : H1 + 1]
            tag = jnp.where((lanes > H1) & (lanes < H1 + 4) & (count > 0.0), total, 0.0)
            tag_ref[i] = tag[:QC, :].astype(BF16)
            return 0

        lax.fori_loop(0, quads, finish, 0, unroll=4)

    shape = jax.ShapeDtypeStruct
    return pl.pallas_call(
        kernel,
        in_specs=[pl.BlockSpec(memory_space=pltpu.SMEM)]
        + [pl.BlockSpec(memory_space=pltpu.VMEM)] * 3,
        out_shape=[shape((quads * QP, D), F32), shape((quads, QC, D), BF16)],
        scratch_shapes=[pltpu.VMEM((16, 3 * D), BF16), pltpu.VMEM((LO, (pairs + 1) * D), F32)]
        + [pltpu.SMEM((sources * most + 1,), jnp.int32)]
        + [pltpu.VMEM((LO, chunk), BF16), pltpu.VMEM((chunk, (pairs + 1) * D), BF16)] * 2,
        compiler_params=pltpu.CompilerParams(vmem_limit_bytes=56 * 1024 * 1024),
        name="encode_points",
    )(held, recv, par, base_rows)


def points_back(recv, held, par, cell_grads):
    sources, _, capacity = recv.shape
    chunk = min(CHUNK, capacity)
    total_rows = cell_grads.shape[0]
    groups = -(-total_rows // LO)
    pairs = -(-groups // 2)

    most = capacity // chunk

    def kernel(
        held_ref, recv_ref, par_ref, grad_ref, out_ref, win, table, acc, todo, *buffers
    ):
        bias = unpack_point_in(par_ref, win)
        lanes = lane_iota()

        def rows_of(g):
            rows = max(0, min(LO, total_rows - g * LO))
            got = [grad_ref[g * LO : g * LO + rows, :]] if rows else []
            return jnp.concatenate(got + [jnp.zeros((LO - rows, D), F32)], axis=0) if rows < LO else got[0]

        for j in range(pairs):
            table[:, j * D : j * D + D] = jnp.where(
                lanes < H1, rows_of(2 * j), rows_of(2 * j + 1)
            ).astype(BF16)
        acc[...] = jnp.zeros((16, D), F32)
        own = jnp.where(lanes < H1, 1.0, 2.0)
        spot = lanes.astype(F32)

        def prepare(s, j, real, into):
            place, group, slope, kept = into
            cols = recv_ref[s, :, pl.ds(pl.multiple_of(j * chunk, chunk), chunk)]
            made = mm_tn(cols, win[...])
            kept[...] = cols
            group[...] = made[:, D : 2 * D] * real
            for k in range(LO // D):
                place[:, k * D : k * D + D] = one_hot(made[:, 2 * D :] == spot + k * D)
            slope[...] = gelu_parts(made[:, :D] + bias)[1]

        def finish_chunk(held):
            place, group, slope, kept = held
            got = jnp.zeros((chunk, D), F32)
            for p in range(0, pairs, 2):
                both = mm(place[...], table[:, p * D : min(p + 2, pairs) * D])
                for u in range(both.shape[1] // D):
                    got = jnp.where(
                        group[...] == own + 2.0 * (p + u), both[:, u * D : u * D + D], got
                    )
            acc[...] += mm(kept[...], (got * slope[...]).astype(BF16))

        count = list_chunks(held_ref, todo, sources, chunk, most)
        two_stage(count, todo, most, prepare, finish_chunk, buffers[:4], buffers[4:])
        both = acc[...] + pltpu.roll(acc[...], H1, axis=1)
        rows = [
            jnp.where(lanes < H1, both[2 * k : 2 * k + 1, :], both[2 * k + 1 : 2 * k + 2, :])
            for k in range(6)
        ]
        out_ref[...] = jnp.concatenate(rows + [jnp.zeros((2, D), F32)], axis=0)

    return pl.pallas_call(
        kernel,
        in_specs=[pl.BlockSpec(memory_space=pltpu.SMEM)]
        + [pl.BlockSpec(memory_space=pltpu.VMEM)] * 3,
        out_shape=jax.ShapeDtypeStruct((8, D), F32),
        scratch_shapes=[
            pltpu.VMEM((16, 3 * D), BF16),
            pltpu.VMEM((LO, pairs * D), BF16),
            pltpu.VMEM((16, D), F32),
            pltpu.SMEM((sources * most + 1,), jnp.int32),
        ]
        + [
            pltpu.VMEM((chunk, LO), BF16),
            pltpu.VMEM((chunk, D), F32),
            pltpu.VMEM((chunk, D), F32),
            pltpu.VMEM((16, chunk), BF16),
        ]
        * 2,
        compiler_params=pltpu.CompilerParams(vmem_limit_bytes=48 * 1024 * 1024),
        cost_estimate=cost_of(recv.size * 100000),
        name="points_back",
    )(held, recv, par, cell_grads)


def update(shares, params, first_moment, second_moment):
    rows = params.shape[0]
    count = shares.shape[0]
    share = (shares.shape[1] - 16) // 2
    moves = [
        (1, GRAD_ROWS, 6, 65),
        (1, 0, POINT_ROWS, LAYER_ROWS),
        (0, 0, POINT_ROWS + LAYER_ROWS, LAYER_ROWS),
    ]

    def kernel(got, par, mom1, mom2, norm_ref, new_par, new1, new2, low, rms, two, one, grad):
        def unpack(s, point):
            v = got[s].astype(F32)
            at = pl.multiple_of(s * share, 8)
            two[pl.ds(at, share), :] = v[:share]
            one[pl.ds(at, share), :] = v[share : 2 * share]
            return point + v[2 * share : 2 * share + 8]

        grad[0:8, :] = lax.fori_loop(0, count, unpack, jnp.zeros((8, D), F32), unroll=4)
        for which, src, dst, length in moves:
            grad[pl.ds(dst, length), :] = (two, one)[which][pl.ds(src, length), :]
        g = grad[...]
        norm = jnp.sqrt(jnp.sum(g * g))
        norm_ref[0, 0] = norm
        factor = jnp.minimum(1.0, clip_norm / (norm + 1e-06))
        clipped = g * factor
        first = beta_one * mom1[...] + (1.0 - beta_one) * clipped
        second = beta_two * mom2[...] + (1.0 - beta_two) * clipped * clipped
        new1[...] = first
        new2[...] = second
        first_hat = first / (1.0 - beta_one**step_count)
        second_hat = second / (1.0 - beta_two**step_count)
        p = par[...]
        p = p - learn_rate * (first_hat / (jnp.sqrt(second_hat) + adam_eps) + decay_rate * p)
        new_par[...] = p
        low[...] = p.astype(BF16)
        stats = jnp.concatenate(
            [one[LAYER_ROWS : LAYER_ROWS + 3, :], two[LAYER_ROWS : LAYER_ROWS + 5, :]], axis=0
        )
        live = jnp.sum(one[LAYER_ROWS + 3 : LAYER_ROWS + 4, :], axis=1, keepdims=True)
        sums = jnp.sum(stats, axis=1, keepdims=True)
        rms[...] = jnp.broadcast_to(jnp.sqrt(sums / jnp.maximum(live, D)), (8, D))

    shape = jax.ShapeDtypeStruct
    flat = shape((rows, D), F32)
    return pl.pallas_call(
        kernel,
        out_specs=[pl.BlockSpec(memory_space=pltpu.SMEM)]
        + [pl.BlockSpec(memory_space=pltpu.VMEM)] * 5,
        out_shape=[shape((1, 1), F32), flat, flat, flat, shape((rows, D), BF16), shape((8, D), F32)],
        scratch_shapes=[pltpu.VMEM((count * share, D), F32)] * 2 + [pltpu.VMEM((rows, D), F32)],
        compiler_params=pltpu.CompilerParams(vmem_limit_bytes=48 * 1024 * 1024),
        name="update",
    )(shares, params, first_moment, second_moment)


def shifted(x, axes, by):
    if len(axes) == 1:
        count = lax.axis_size(axes[0])
        return lax.ppermute(x, axes[0], [(i, (i + by) % count) for i in range(count)])
    tiles, rows = lax.axis_size(axes[0]), lax.axis_size(axes[1])
    pairs = [
        (i * rows + j, (i + by) % tiles * rows + (j + by) % rows)
        for i in range(tiles)
        for j in range(rows)
    ]
    return lax.ppermute(x, axes, pairs)


def exchange(row, col, cor, by):
    return (
        shifted(row, ("tile",), by),
        shifted(col, ("row",), by),
        shifted(cor, ("tile", "row"), by),
    )


def by_quads(grid, quads_x, quads_y):
    trailing = grid.shape[2:]
    grid = grid.reshape((quads_x, QS, quads_y, QS) + trailing)
    return jnp.swapaxes(grid, 1, 2).reshape((quads_x, quads_y, QC) + trailing)


def all_to_all(x):
    return lax.all_to_all(x, ("tile", "row"), split_axis=0, concat_axis=0, tiled=True)


def scatter_sum(x, count):
    return jnp.sum(all_to_all(x.reshape(count, x.shape[0] // count, D)), axis=0)


def local(
    point_feats,
    point_tile,
    point_cell,
    point_valid,
    pillar_frame,
    cotangent,
    params,
    first_moment,
    second_moment,
):
    tile_count = lax.axis_size("tile")
    row_count = lax.axis_size("row")
    device_count = tile_count * row_count
    extent_x, extent_y = pillar_frame.shape
    cell_count = extent_x * extent_y
    quads_x, quads_y = extent_x // QS, extent_y // QS
    quads = quads_x * quads_y
    points = point_cell.shape[0]
    capacity = 2 * points // tile_count
    par = params.reshape(-1, D)

    cot = by_quads(cotangent, quads_x, quads_y)
    cot_halos = exchange(cot[0], cot[:, 0], cot[0, :1], -1)

    shape = (points // BLOCK, BLOCK)
    send = bin_points(
        point_feats,
        point_tile.reshape(shape),
        point_cell.reshape(shape),
        point_valid.reshape(shape),
        tile_count,
        capacity,
        extent_y,
        quads_y,
    )
    recv = lax.all_to_all(send, "tile", split_axis=0, concat_axis=0, tiled=True)
    held = jnp.sum(recv[:, 11].astype(jnp.int32), axis=1)

    frames = by_quads(pillar_frame, quads_x, quads_y)
    frames = jnp.pad(frames, ((0, 0), (0, 0), (0, QP - QC)), constant_values=-1).reshape(-1)
    lanes = jnp.arange(D, dtype=jnp.int32)
    base_rows = (frames[:, None] == lanes[None] - (H1 + 1)).astype(F32)
    pillars, tags = encode_points(recv, held, par, base_rows, quads)
    pillars = pillars.reshape(quads_x, quads_y, QP, D)
    tags = tags.reshape(quads_x, quads_y, QC, D)
    tag_halos = exchange(tags[0], tags[:, 0], tags[0, :1], -1)

    first = first_layer(pillars, par, quads_x, quads_y)
    field, saved, sums_one = first[0], first[1:8], first[8]
    halos = exchange(*first[9:], -1)
    flags = jnp.stack(
        [
            (lax.axis_index("tile") == tile_count - 1).astype(jnp.int32),
            (lax.axis_index("row") == row_count - 1).astype(jnp.int32),
        ]
    )
    step = device_count * 8
    grad_rows = -(-(GRAD_ROWS + 72) // step) * step
    grads, grad_two, g_row, g_col, g_cor = second_layer(
        flags,
        field,
        halos,
        tags,
        tag_halos,
        cot,
        cot_halos,
        par,
        1.0 / (cell_count * device_count),
        grad_rows,
    )
    grad_two, grad_halos = lax.optimization_barrier((grad_two, exchange(g_row, g_col, g_cor, 1)))
    sum_two = scatter_sum(grad_two, device_count)
    cell_grads, grad_one = first_layer_back(
        grads, grad_halos, pillars, saved, sums_one, par, grad_rows
    )
    grad_one, sum_two = lax.optimization_barrier((grad_one, sum_two))
    sum_one = scatter_sum(grad_one, device_count)
    grad_pin = points_back(recv, held, par, cell_grads.reshape(quads * QP, D))
    share = jnp.concatenate([sum_two, sum_one, grad_pin, jnp.zeros((8, D), F32)], axis=0)
    share = share.astype(BF16)
    total = all_to_all(jnp.broadcast_to(share[None], (device_count,) + share.shape))
    norm, new_params, new_first, new_second, low, rms = update(
        total, par, first_moment.reshape(-1, D), second_moment.reshape(-1, D)
    )
    return (
        norm[0, 0],
        new_params.reshape(-1),
        new_first.reshape(-1),
        new_second.reshape(-1),
        low.reshape(-1),
        rms[:6, 0],
    )


def solution(mesh):
    return jax.shard_map(
        local,
        mesh=mesh,
        in_specs=(
            P(None, ("tile", "row")),
            P(("tile", "row"), None),
            P(("tile", "row")),
            P(("tile", "row")),
            P("tile", "row"),
            P("tile", "row", None),
            P(),
            P(),
            P(),
        ),
        out_specs=(P(), P(), P(), P(), P(), P()),
        check_vma=False,
    )
```

```python
import jax
import jax.numpy as jnp
from jax import lax
from jax.experimental import pallas as pl
from jax.experimental.pallas import tpu as pltpu
from jax.sharding import PartitionSpec as P

D = 128
HEADS = 8
HD = 16
FF = 256
H1 = 64
WIN = 12
C_IN = 11
QS = 6
QC = 36
QP = 40
SLOTS = 144
KEYS = HEADS * SLOTS
LAYER_ROWS = 1034
POINT_ROWS = 71
GRAD_ROWS = 1040
BLOCK = 128
CHUNK = 512
LO = 512
NW = 8
NF = 4

clip_norm = 0.01
beta_one = 0.9
beta_two = 0.999
step_count = 10
learn_rate = 0.1
decay_rate = 0.05
adam_eps = 1e-08

F32 = jnp.float32
BF16 = jnp.bfloat16
GELU_C = 0.7978845608028654
GELU_A = 0.044715


def mm(a, b):
    return lax.dot_general(a, b, (((1,), (0,)), ((), ())), preferred_element_type=F32)


def mm_nt(a, b):
    return lax.dot_general(a, b, (((1,), (1,)), ((), ())), preferred_element_type=F32)


def mm_tn(a, b):
    return lax.dot_general(a, b, (((0,), (0,)), ((), ())), preferred_element_type=F32)


def lane_iota(rows=1):
    return lax.broadcasted_iota(jnp.int32, (rows, D), 1)


def part8(v):
    return jnp.sum(v.reshape(v.shape[0] // 8, 8, v.shape[1]), axis=0)


def gelu_parts(v):
    sq = v * v
    t = jnp.tanh(v * (GELU_C + (GELU_C * GELU_A) * sq))
    half = 0.5 + 0.5 * t
    slope = half + (0.5 * v) * (1.0 - t * t) * (GELU_C + (3.0 * GELU_C * GELU_A) * sq)
    return v * half, slope


def gelu_only(v):
    t = jnp.tanh(v * (GELU_C + (GELU_C * GELU_A) * (v * v)))
    return v * (0.5 + 0.5 * t)


def normalize(y):
    center = y - jnp.mean(y, axis=-1, keepdims=True)
    rs = lax.rsqrt(jnp.mean(center * center, axis=-1, keepdims=True) + 1e-05)
    return center * rs, rs


def norm_pull(gx, xhat, rs):
    return rs * (
        gx
        - jnp.mean(gx, axis=-1, keepdims=True)
        - xhat * jnp.mean(gx * xhat, axis=-1, keepdims=True)
    )


def load_layer(par, base, w):
    for part in range(3):
        m = par[pl.ds(base + part, D, stride=3), :]
        w["qkv"][:, part * D : (part + 1) * D] = m.astype(BF16)
        if "qkv_t" in w:
            w["qkv_t"][part * D : (part + 1) * D, :] = m.T.astype(BF16)
    m = par[pl.ds(base + 384, D), :]
    w["out"][...] = m.astype(BF16)
    if "out_t" in w:
        w["out_t"][...] = m.T.astype(BF16)
    for part in range(2):
        m = par[pl.ds(base + 512 + part, D, stride=2), :]
        w["fin"][:, part * D : (part + 1) * D] = m.astype(BF16)
        if "fin_t" in w:
            w["fin_t"][part * D : (part + 1) * D, :] = m.T.astype(BF16)
        m = par[pl.ds(base + 768 + part * D, D), :]
        w["fout"][part * D : (part + 1) * D, :] = m.astype(BF16)
        if "fout_t" in w:
            w["fout_t"][:, part * D : (part + 1) * D] = m.T.astype(BF16)


WEIGHT_SHAPES = {
    "qkv": (D, 3 * D),
    "qkv_t": (3 * D, D),
    "out": (D, D),
    "out_t": (D, D),
    "fin": (D, FF),
    "fin_t": (FF, D),
    "fout": (FF, D),
    "fout_t": (D, FF),
}


def vec(par, base, row):
    return par[base + 1024 + row : base + 1025 + row, :]


def vec2(par, base, row):
    return jnp.concatenate([vec(par, base, row), vec(par, base, row + 1)], axis=1)


def fold_rows():
    return one_hot(lax.broadcasted_iota(jnp.int32, (HD, D), 0) == lane_iota(HD) % HD)


def own_head():
    return lax.broadcasted_iota(jnp.int32, (D, D), 0) // HD == lane_iota(D) // HD


def turned(v):
    return v.astype(F32).T


def head_cols(v):
    top = turned(v[:D]).astype(BF16)
    none = jnp.zeros((HD, D), BF16)
    pairs = []
    for t in range(0, D, 2 * HD):
        left = jnp.concatenate([top[t : t + HD], none], axis=0)
        right = jnp.concatenate([none, top[t + HD : t + 2 * HD]], axis=0)
        pairs.append(jnp.concatenate([left, right], axis=1))
    return pairs, jnp.where(own_head(), mm_tn(v[D:], fold_rows()), 0.0).astype(BF16)


def by_head(rows, cols):
    pairs, rest = cols
    parts = []
    for t in range(HEADS // 2):
        both = mm(rows[:, 2 * HD * t : 2 * HD * (t + 1)], pairs[t])
        parts = parts + [both[:, :D], both[:, D:]]
    return parts + [mm(rows, rest)]


def head_sums(cols, parts):
    pairs, rest = cols
    sums = [
        mm_nt(pairs[t], jnp.concatenate(parts[2 * t : 2 * t + 2], axis=1)) for t in range(HEADS // 2)
    ]
    return (jnp.concatenate(sums, axis=0) + mm_nt(rest, parts[HEADS])).T.astype(BF16)


def window_bias(groups):
    keys = jnp.concatenate(
        [groups[:D]] + [groups[D:]] * HEADS + [jnp.ones((D, D), BF16)], axis=0
    )
    same = mm_nt(groups, keys)
    rows = lax.broadcasted_iota(jnp.int32, (SLOTS, D), 0)
    lanes = lane_iota(SLOTS)
    first = (same[:, :D] > 0.5) | (rows == lanes)
    last = (same[:, D : 2 * D] > 0.5) | (rows == lanes % HD + D)
    return (
        jnp.where(first, 0.0, -1000000000.0),
        jnp.where(last, 0.0, -1000000000.0),
        same[:, 2 * D :],
    )


def attend(qs, key, val, bias_first, bias_last):
    probs = []
    cols = head_cols(qs)
    yield
    parts = by_head(key, cols)
    yield
    for h, part in enumerate(parts):
        part = part + (bias_first if h < HEADS else bias_last)
        expo = jnp.exp(part - jnp.max(part, axis=0, keepdims=True))
        probs.append((expo * (1.0 / jnp.sum(expo, axis=0, keepdims=True))).astype(BF16))
    yield
    mix = yield from query_pull(val, probs)
    return probs, mix


def attend_pull(probs, qs, key, val, gmix):
    cols = head_cols(gmix)
    gs = []
    yield
    parts = by_head(val, cols)
    yield
    g_val = head_sums(cols, probs)
    yield
    for p_low, pulled in zip(probs, parts):
        p = p_low.astype(F32)
        both = p * pulled
        gs.append((both - p * jnp.sum(both, axis=0, keepdims=True)).astype(BF16))
    yield
    g_key = head_sums(head_cols(qs), gs)
    yield
    g_query = yield from query_pull(key * 0.25, gs)
    return g_query, g_key, g_val


def query_pull(rows, parts):
    flat = turned(rows).astype(BF16)
    tops = []
    for t in range(HEADS // 2):
        at = 2 * HD * t
        both = mm(flat[at : at + 2 * HD], jnp.concatenate(parts[2 * t : 2 * t + 2], axis=1))
        tops = tops + [both[:HD, :D], both[HD:, D:]]
    top = jnp.concatenate(tops, axis=0)
    rest = jnp.where(own_head(), mm(flat, parts[HEADS]), 0.0).astype(BF16)
    yield
    return jnp.concatenate([top.T.astype(BF16), mm_nt(fold_rows(), rest).astype(BF16)], axis=0)


def in_step(runs):
    results = [None] * len(runs)
    active = list(range(len(runs)))
    while active:
        for i in list(active):
            try:
                next(runs[i])
            except StopIteration as end:
                results[i] = end.value
                active.remove(i)
    return results


def split_qkv(packed, w):
    rows = slice(w * SLOTS, (w + 1) * SLOTS)
    return packed[rows, :D] * 0.25, packed[rows, D : 2 * D], packed[rows, 2 * D :]


def layer_forward(x, groups, par, base, w, sums):
    count = x.shape[0] // SLOTS
    low = x.astype(BF16)
    qkv_bias = jnp.concatenate(
        [vec(par, base, 0), jnp.zeros((1, D), F32), vec(par, base, 1)], axis=1
    )
    packed = (mm(low, w["qkv"][...]) + qkv_bias).astype(BF16)
    masks = [window_bias(group) for group in groups]
    done = in_step([attend(*split_qkv(packed, i), *masks[i][:2]) for i in range(count)])
    probs = [d[0] for d in done]
    mixes = [d[1] for d in done]
    lives = [m[2] for m in masks]
    mix = jnp.concatenate(mixes, axis=0)
    live = jnp.concatenate(lives, axis=0)
    attn_out = mm(mix, w["out"][...]) + vec(par, base, 2)
    first = x + attn_out
    xhat1, rs1 = normalize(first)
    normed = (xhat1 * vec(par, base, 3) + vec(par, base, 4)) * live
    normed_low = normed.astype(BF16)
    pre = mm(normed_low, w["fin"][...]) + vec2(par, base, 5)
    act, slope = gelu_parts(pre)
    hidden = act.astype(BF16)
    ffn = mm(hidden, w["fout"][...]) + vec(par, base, 7)
    second = normed + ffn
    xhat2, rs2 = normalize(second)
    result = (xhat2 * vec(par, base, 8) + vec(par, base, 9)) * live
    sums[0] += part8(attn_out * attn_out * live)
    sums[1] += part8(ffn * ffn * live)
    sums[2] += part8(result * result)
    sums[3] += part8(live)
    return dict(
        low=low,
        packed=packed,
        probs=probs,
        mix=mix,
        live=live,
        first=first,
        second=second,
        xhat1=xhat1,
        rs1=rs1,
        xhat2=xhat2,
        rs2=rs2,
        normed_low=normed_low,
        slope=slope,
        hidden=hidden,
        result=result,
    )


def layer_backward(grad, k, par, base, w, acc):
    live = k["live"]
    gl = grad * live
    acc["vec"][8] += part8(gl * k["xhat2"])
    acc["vec"][9] += part8(gl)
    g2 = norm_pull(gl * vec(par, base, 8), k["xhat2"], k["rs2"])
    g_ffn = g2.astype(BF16)
    acc["fout"][...] += mm_tn(k["hidden"], g_ffn)
    acc["vec"][7] += part8(g_ffn.astype(F32))
    g_pre = (mm(g_ffn, w["fout_t"][...]) * k["slope"]).astype(BF16)
    acc["fin"][...] += mm_tn(k["normed_low"], g_pre)
    for part in range(2):
        acc["vec"][5 + part] += part8(g_pre[:, part * D : (part + 1) * D].astype(F32))
    g_norm = (g2 + mm(g_pre, w["fin_t"][...])) * live
    acc["vec"][3] += part8(g_norm * k["xhat1"])
    acc["vec"][4] += part8(g_norm)
    g1 = norm_pull(g_norm * vec(par, base, 3), k["xhat1"], k["rs1"])
    g_attn = g1.astype(BF16)
    acc["out"][...] += mm_tn(k["mix"], g_attn)
    acc["vec"][2] += part8(g_attn.astype(F32))
    g_mix = mm(g_attn, w["out_t"][...]).astype(BF16)
    runs = []
    for i in range(grad.shape[0] // SLOTS):
        rows = slice(i * SLOTS, (i + 1) * SLOTS)
        runs.append(attend_pull(k["probs"][i], *split_qkv(k["packed"], i), g_mix[rows]))
    pieces = [jnp.concatenate(parts, axis=1) for parts in in_step(runs)]
    g_packed = jnp.concatenate(pieces, axis=0)
    acc["qkv"][...] += mm_tn(k["low"], g_packed)
    acc["vec"][0] += part8(g_packed[:, :D].astype(F32))
    acc["vec"][1] += part8(g_packed[:, 2 * D :].astype(F32))
    return g1 + mm(g_packed, w["qkv_t"][...])


ACC_SHAPES = {
    "qkv": (D, 3 * D),
    "out": (D, D),
    "fin": (D, FF),
    "fout": (FF, D),
    "vec": (10, 8, D),
}


def clear(acc):
    for ref in acc.values():
        ref[...] = jnp.zeros(ref.shape, ref.dtype)


def store_grads(acc, sums, out):
    for part in range(3):
        out[pl.ds(part, D, stride=3), :] = acc["qkv"][:, part * D : (part + 1) * D]
    out[pl.ds(384, D), :] = acc["out"][...]
    for part in range(2):
        out[pl.ds(512 + part, D, stride=2), :] = acc["fin"][:, part * D : (part + 1) * D]
    out[pl.ds(768, FF), :] = acc["fout"][...]
    out[pl.ds(1024, 16), :] = jnp.concatenate(
        [jnp.sum(acc["vec"][i], axis=0, keepdims=True) for i in range(10)]
        + [jnp.sum(sums[i], axis=0, keepdims=True) for i in range(4)]
        + [jnp.zeros((2, D), F32)],
        axis=0,
    )


def gather_windows(scratch, pick):
    for i in range(scratch.shape[0] // SLOTS):
        for r in range(2):
            for c in range(2):
                at = i * SLOTS + (2 * r + c) * QC
                scratch[pl.ds(at, QC), :] = pick(r, 2 * i + c)
    return scratch[...]


def spread_windows(scratch, value, put):
    scratch[...] = value
    for i in range(scratch.shape[0] // SLOTS):
        for r in range(2):
            for c in range(2):
                put(r, 2 * i + c, scratch[pl.ds(i * SLOTS + (2 * r + c) * QC, QC), :])


def whole(shape, space=pltpu.VMEM):
    return pl.BlockSpec(shape, lambda *_: (0,) * len(shape), memory_space=space)


def params_for(limit=56):
    return pltpu.CompilerParams(
        dimension_semantics=("arbitrary",), vmem_limit_bytes=limit * 1024 * 1024
    )


def cost_of(flops):
    return pl.CostEstimate(flops=flops, bytes_accessed=1 << 24, transcendentals=0)


def first_layer(pillars, par, quads_x, quads_y):
    across = quads_x // 2
    along = quads_y // (2 * NF)
    windows = quads_x * quads_y // 4
    base = POINT_ROWS

    def kernel(pil, par_ref, *refs):
        outs, scratch = refs[:12], refs[12:]
        (
            field,
            probs_out,
            packed_out,
            mix_out,
            first_out,
            second_out,
            low_out,
            live_out,
            sums_out,
            row_out,
            col_out,
            cor_out,
        ) = outs
        names = ["qkv", "out", "fin", "fout"]
        w = dict(zip(names, scratch[:4]))
        wide, pout, sums = scratch[4:]
        step = pl.program_id(0)
        a = step // along
        b = step % along

        @pl.when(step == 0)
        def _():
            load_layer(par_ref, base, w)
            m = par_ref[pl.ds(6, H1), :].astype(BF16)
            pout[...] = jnp.concatenate([m, m], axis=0)
            sums[...] = jnp.zeros(sums.shape, F32)

        cells = gather_windows(wide, lambda r, c: pil[r, c, :QC, :])
        lanes = lane_iota()
        total = jnp.where(lanes < H1, cells, 0.0)
        count = cells[:, H1 : H1 + 1]
        high = total.astype(BF16).astype(F32)
        both = (high + pltpu.roll(total - high, H1, axis=1)).astype(BF16)
        pillar = mm(both, pout[...]) + count * par_ref[70:71, :]
        x = pillar / jnp.maximum(count, 1.0)
        onehot = jnp.where((lanes > H1) & (lanes < H1 + 4) & (count > 0.0), cells, 0.0).astype(BF16)
        groups = [onehot[i * SLOTS : (i + 1) * SLOTS] for i in range(NF)]
        k = layer_forward(x, groups, par_ref, base, w, sums)
        for i in range(NF):
            rows = slice(i * SLOTS, (i + 1) * SLOTS)
            for h in range(HEADS + 1):
                probs_out[i, :, h * D : (h + 1) * D] = k["probs"][i][h]
            packed_out[i] = k["packed"][rows]
            mix_out[i] = k["mix"][rows]
            first_out[i] = k["first"][rows]
            second_out[i] = k["second"][rows]
            low_out[i] = k["low"][rows]
            live_out[i] = k["live"][rows]

        def put(r, c, v):
            field[r, c, :QC, :] = v

        spread_windows(wide, k["result"], put)

        @pl.when(a == 0)
        def _():
            for c in range(2 * NF):
                row_out[c] = field[0, c, :QC, :].astype(BF16)

        @pl.when(b == 0)
        def _():
            for r in range(2):
                col_out[r] = field[r, 0, :QC, :].astype(BF16)

        @pl.when(step == 0)
        def _():
            cor_out[0] = field[0, 0, :QC, :].astype(BF16)

        @pl.when(step == pl.num_programs(0) - 1)
        def _():
            sums_out[...] = sums[...]

    def win_spec(width):
        return pl.BlockSpec((NF, SLOTS, width), lambda s: (s, 0, 0))

    quad_spec = pl.BlockSpec((2, 2 * NF, QP, D), lambda s: (s // along, s % along, 0, 0))
    shape = jax.ShapeDtypeStruct
    return pl.pallas_call(
        kernel,
        grid=(across * along,),
        in_specs=[quad_spec, whole(par.shape)],
        out_specs=[
            quad_spec,
            win_spec(KEYS),
            win_spec(3 * D),
            win_spec(D),
            win_spec(D),
            win_spec(D),
            win_spec(D),
            win_spec(D),
            whole((4, 8, D)),
            pl.BlockSpec((2 * NF, QC, D), lambda s: (jnp.minimum(s, along - 1), 0, 0)),
            pl.BlockSpec((2, QC, D), lambda s: (s // along, 0, 0)),
            whole((1, QC, D)),
        ],
        out_shape=[
            shape((quads_x, quads_y, QP, D), F32),
            shape((windows, SLOTS, KEYS), BF16),
            shape((windows, SLOTS, 3 * D), BF16),
            shape((windows, SLOTS, D), BF16),
            shape((windows, SLOTS, D), F32),
            shape((windows, SLOTS, D), F32),
            shape((windows, SLOTS, D), BF16),
            shape((windows, SLOTS, D), F32),
            shape((4, 8, D), F32),
            shape((quads_y, QC, D), BF16),
            shape((quads_x, QC, D), BF16),
            shape((1, QC, D), BF16),
        ],
        scratch_shapes=[pltpu.VMEM(WEIGHT_SHAPES[n], BF16) for n in ["qkv", "out", "fin", "fout"]]
        + [
            pltpu.VMEM((NF * SLOTS, D), F32),
            pltpu.VMEM((D, D), BF16),
            pltpu.VMEM((4, 8, D), F32),
        ],
        compiler_params=params_for(),
        cost_estimate=cost_of(pillars.size * 12000),
        name="first_layer",
    )(pillars, par)


def second_layer(flags, field, halos, tags, cot, early_halos, par, scale, grad_rows):
    quads_x, quads_y = field.shape[:2]
    across = quads_x // 2
    along = quads_y // (2 * NW)
    base = POINT_ROWS + LAYER_ROWS
    wnames = list(WEIGHT_SHAPES)
    anames = list(ACC_SHAPES)

    def kernel(flag, *refs):
        ins, refs = refs[:10], refs[10:]
        outs, scratch = refs[:5], refs[5:]
        fields, (tag_ref, cot_ref), early, par_ref = ins[:4], ins[4:6], ins[6:9], ins[9]
        grads, weights, row_out, col_out, cor_out = outs
        w = dict(zip(wnames, scratch))
        scratch = scratch[len(wnames) :]
        acc = dict(zip(anames, scratch))
        wide, sums, ext_x, ext_t, ext_g = scratch[len(anames) :]
        step = pl.program_id(0)
        a = step // along
        b = step % along

        @pl.when(step == 0)
        def _():
            load_layer(par_ref, base, w)
            sums[...] = jnp.zeros(sums.shape, F32)
            clear(acc)
            lanes = lane_iota()

            def moved(v, region):
                return pltpu.roll(v, 3 * region, axis=1)

            def fill(ext, srcs, first, turn_row, turn_col, turn_cor):
                main, row, col, cor = srcs
                rows = slice(first, first + QC)

                def one(i, _):
                    ext[i // quads_y, i % quads_y, :QC, :] = main[
                        i // quads_y, i % quads_y, :QC, :
                    ].astype(F32)
                    return 0

                lax.fori_loop(0, quads_x * quads_y, one, 0, unroll=4)

                def one_row(i, _):
                    ext[quads_x, i, :QC, :] = turn_row(row[i, rows, :].astype(F32))
                    return 0

                lax.fori_loop(1, quads_y, one_row, 0)
                for i in range(1, quads_x):
                    ext[i, quads_y, :QC, :] = turn_col(col[i, rows, :].astype(F32))
                ext[quads_x, quads_y, :QC, :] = turn_cor(cor[0, rows, :].astype(F32))

            def same(v):
                return v

            last_x = flag[0] > 0
            last_y = flag[1] > 0

            def tag_row(v):
                return jnp.where(last_x, moved(v, 2), v)

            def tag_col(v):
                return jnp.where(last_y, moved(v, 1), v)

            fill(ext_x, fields, 0, same, same, same)
            fill(ext_g, [cot_ref, *early], 0, same, same, same)
            fill(ext_t, [tag_ref, *early], QP, tag_row, tag_col, lambda v: tag_row(tag_col(v)))

        def picker(ext):
            return lambda r, c: ext[2 * a + 1 + r, 2 * NW * b + 1 + c, :QC, :]

        tag = gather_windows(wide, picker(ext_t)).astype(BF16)
        groups = [tag[i * SLOTS : (i + 1) * SLOTS] for i in range(NW)]
        x = gather_windows(wide, picker(ext_x))
        k = layer_forward(x, groups, par_ref, base, w, sums)
        grad = gather_windows(wide, picker(ext_g)) * scale
        gx = layer_backward(grad, k, par_ref, base, w, acc)

        def put(r, c, v):
            grads[r, c, :QC, :] = v

        spread_windows(wide, gx, put)

        @pl.when(a == across - 1)
        def _():
            for c in range(2 * NW):
                row_out[c] = grads[1, c, :QC, :].astype(BF16)

        @pl.when(b == along - 1)
        def _():
            for r in range(2):
                col_out[r] = grads[r, 2 * NW - 1, :QC, :].astype(BF16)

        @pl.when(step == pl.num_programs(0) - 1)
        def _():
            cor_out[0] = grads[1, 2 * NW - 1, :QC, :].astype(BF16)
            store_grads(acc, sums, weights)

    shape = jax.ShapeDtypeStruct
    quad_spec = pl.BlockSpec((2, 2 * NW, QP, D), lambda s: (s // along, s % along, 0, 0))
    ext = pltpu.VMEM((quads_x + 1, quads_y + 1, QP, D), F32)
    arrays = [field, *halos, tags, cot, *early_halos, par]
    return pl.pallas_call(
        kernel,
        grid=(across * along,),
        in_specs=[pl.BlockSpec(memory_space=pltpu.SMEM)] + [whole(v.shape) for v in arrays],
        out_specs=[
            quad_spec,
            whole((grad_rows, D)),
            pl.BlockSpec(
                (2 * NW, QC, D), lambda s: (jnp.maximum(s - (across - 1) * along, 0), 0, 0)
            ),
            pl.BlockSpec((2, QC, D), lambda s: (s // along, 0, 0)),
            whole((1, QC, D)),
        ],
        out_shape=[
            shape((quads_x, quads_y, QP, D), F32),
            shape((grad_rows, D), F32),
            shape((quads_y, QC, D), BF16),
            shape((quads_x, QC, D), BF16),
            shape((1, QC, D), BF16),
        ],
        scratch_shapes=[pltpu.VMEM(WEIGHT_SHAPES[n], BF16) for n in wnames]
        + [pltpu.VMEM(ACC_SHAPES[n], F32) for n in anames]
        + [
            pltpu.VMEM((NW * SLOTS, D), F32),
            pltpu.VMEM((4, 8, D), F32),
            ext,
            ext,
            ext,
        ],
        compiler_params=params_for(),
        name="second_layer",
    )(flags, *arrays)


def first_layer_back(grads, halos, pillars, saved, sums, par, grad_rows):
    quads_x, quads_y = grads.shape[:2]
    across = quads_x // 2
    along = quads_y // (2 * NW)
    base = POINT_ROWS
    wnames = list(WEIGHT_SHAPES)
    anames = list(ACC_SHAPES)

    def kernel(*refs):
        ins, refs = refs[:14], refs[14:]
        outs, scratch = refs[:2], refs[2:]
        main, row, col, cor, pil = ins[:5]
        probs, packed, mix, first, second, low, live = ins[5:12]
        sums_ref, par_ref = ins[12:]
        cell_out, weights = outs
        w = dict(zip(wnames, scratch))
        scratch = scratch[len(wnames) :]
        acc = dict(zip(anames, scratch))
        wide, ext, pout_t, pacc = scratch[len(anames) :]
        step = pl.program_id(0)
        a = step // along
        b = step % along

        @pl.when(step == 0)
        def _():
            load_layer(par_ref, base, w)
            clear(acc)
            pacc[...] = jnp.zeros(pacc.shape, F32)
            m = par_ref[pl.ds(6, H1), :]
            pout_t[...] = jnp.concatenate([m, m], axis=0).T.astype(BF16)
            for r in range(1, quads_x):

                def one(i, _):
                    ext[r, i, :QC, :] = main[r - 1, i - 1, :QC, :]
                    return 0

                lax.fori_loop(1, quads_y, one, 0)
                ext[r, 0, :QC, :] = col[r - 1].astype(F32)

            def one_row(i, _):
                ext[0, i, :QC, :] = row[i - 1].astype(F32)
                return 0

            lax.fori_loop(1, quads_y, one_row, 0)
            ext[0, 0, :QC, :] = cor[0].astype(F32)

        grad = gather_windows(wide, lambda r, c: ext[2 * a + r, 2 * NW * b + c, :QC, :])

        def rows_of(ref):
            return jnp.concatenate([ref[i] for i in range(NW)], axis=0)

        k = dict(
            low=rows_of(low),
            packed=rows_of(packed),
            probs=[
                [probs[i, :, h * D : (h + 1) * D] for h in range(HEADS + 1)] for i in range(NW)
            ],
            mix=rows_of(mix),
            live=rows_of(live),
        )
        k["xhat1"], k["rs1"] = normalize(rows_of(first))
        k["xhat2"], k["rs2"] = normalize(rows_of(second))
        normed = (k["xhat1"] * vec(par_ref, base, 3) + vec(par_ref, base, 4)) * k["live"]
        k["normed_low"] = normed.astype(BF16)
        act, k["slope"] = gelu_parts(mm(k["normed_low"], w["fin"][...]) + vec2(par_ref, base, 5))
        k["hidden"] = act.astype(BF16)
        gx = layer_backward(grad, k, par_ref, base, w, acc)

        cells = gather_windows(wide, lambda r, c: pil[r, c, :QC, :])
        lanes = lane_iota()
        total = jnp.where(lanes <= H1, cells, 0.0)
        g_pillar = (gx / jnp.maximum(cells[:, H1 : H1 + 1], 1.0)).astype(BF16)
        high = total.astype(BF16)
        rest = (total - high.astype(F32)).astype(BF16)
        pacc[...] += mm_tn(high, g_pillar) + mm_tn(rest, g_pillar)

        def put(r, c, v):
            cell_out[r, c, :QC, :] = v
            cell_out[r, c, QC:, :] = jnp.zeros((QP - QC, D), F32)

        spread_windows(wide, mm(g_pillar, pout_t[...]), put)

        @pl.when(step == pl.num_programs(0) - 1)
        def _():
            store_grads(acc, sums_ref, weights)
            weights[GRAD_ROWS : GRAD_ROWS + 72, :] = pacc[:72, :]

    def win_spec(width):
        return pl.BlockSpec((NW, SLOTS, width), lambda s: (s, 0, 0))

    shape = jax.ShapeDtypeStruct
    quad_spec = pl.BlockSpec((2, 2 * NW, QP, D), lambda s: (s // along, s % along, 0, 0))
    return pl.pallas_call(
        kernel,
        grid=(across * along,),
        in_specs=[whole(grads.shape)]
        + [whole(v.shape) for v in halos]
        + [quad_spec]
        + [win_spec(v.shape[2]) for v in saved]
        + [whole(sums.shape), whole(par.shape)],
        out_specs=[quad_spec, whole((grad_rows, D))],
        out_shape=[shape((quads_x, quads_y, QP, D), F32), shape((grad_rows, D), F32)],
        scratch_shapes=[pltpu.VMEM(WEIGHT_SHAPES[n], BF16) for n in wnames]
        + [pltpu.VMEM(ACC_SHAPES[n], F32) for n in anames]
        + [
            pltpu.VMEM((NW * SLOTS, D), F32),
            pltpu.VMEM((quads_x, quads_y, QP, D), F32),
            pltpu.VMEM((D, D), BF16),
            pltpu.VMEM((D, D), F32),
        ],
        compiler_params=params_for(),
        cost_estimate=cost_of(grads.size * 12000),
        name="first_layer_back",
    )(grads, *halos, pillars, *saved, sums, par)


def one_hot(hit):
    return jnp.where(hit, 1.0, 0.0).astype(BF16)


def bin_points(feats, tiles, cells, valid, tile_count, capacity, extent_y, quads_y):
    blocks = tiles.shape[0]
    groups = tile_count * capacity // LO
    lots = 8
    wide = lots * BLOCK

    def kernel(feat_ref, tile_ref, cell_ref, valid_ref, out_ref, slot_ref, code_ref, acc):
        real = valid_ref[...] > 0
        t = jnp.where(real, tile_ref[...], tile_count)
        i0 = lax.broadcasted_iota(jnp.int32, (BLOCK, BLOCK), 0)
        i1 = lax.broadcasted_iota(jnp.int32, (BLOCK, BLOCK), 1)
        upto = one_hot(i0 <= i1)
        j0 = lax.broadcasted_iota(jnp.int32, (blocks, blocks), 0)
        j1 = lax.broadcasted_iota(jnp.int32, (blocks, blocks), 1)
        earlier = one_hot(j1 < j0)
        slot = jnp.full((blocks, BLOCK), -1.0, F32)
        for k in range(tile_count):
            hit = t == k
            run = mm(one_hot(hit), upto)
            total = jnp.broadcast_to(run[:, BLOCK - 1 :], (blocks, D)).astype(BF16)
            at = mm(earlier, total)[:, :1] + (k * capacity - 1.0)
            slot = jnp.where(hit, run + at, slot)
        slot_ref[...] = slot.astype(jnp.int32)

        def part(v, by):
            return ((v.astype(F32) + 0.5) * (1.0 / by)).astype(jnp.int32)

        cell = cell_ref[...]
        cx = part(cell, extent_y)
        cy = cell - cx * extent_y
        qx, qy = part(cx, QS), part(cy, QS)
        row = (qx * quads_y + qy) * QP + (cx - qx * QS) * QS + (cy - qy * QS)
        hi = row // LO
        lo = row - hi * LO
        low_part = lo % 256
        code_ref[0] = jnp.where(real, 1.0, 0.0)
        code_ref[1] = (hi + 1).astype(F32)
        code_ref[2] = (lo - low_part).astype(F32)
        code_ref[3] = low_part.astype(F32)
        acc[...] = jnp.zeros(acc.shape, F32)
        span = lax.broadcasted_iota(jnp.int32, (LO, wide), 0)

        def one(j, _):
            def line(ref, *lead):
                return jnp.concatenate(
                    [ref[(*lead, pl.ds(j * lots + u, 1), slice(None))] for u in range(lots)], axis=1
                )

            at = line(slot_ref)
            feat = feat_ref[:, pl.ds(pl.multiple_of(j * wide, wide), wide)].astype(F32)
            rows = jnp.concatenate(
                [feat] + [line(code_ref, i) for i in range(4)] + [jnp.zeros((1, wide), F32)], axis=0
            ).astype(BF16)
            group = at // LO
            place = one_hot(span == at % LO)
            spread = jnp.concatenate([rows * one_hot(group == g) for g in range(groups)], axis=0)
            acc[...] += mm_nt(spread, place)
            return 0

        lax.fori_loop(0, blocks // lots, one, 0)
        for k in range(tile_count):
            for at in range(0, capacity, LO):
                g, low = (k * capacity + at) // LO, (k * capacity + at) % LO
                size = min(LO, capacity)
                out_ref[k, :, at : at + size] = acc[g * 16 : g * 16 + 16, low : low + size].astype(
                    BF16
                )

    return pl.pallas_call(
        kernel,
        out_shape=jax.ShapeDtypeStruct((tile_count, 16, capacity), BF16),
        scratch_shapes=[
            pltpu.VMEM((blocks, BLOCK), jnp.int32),
            pltpu.VMEM((4, blocks, BLOCK), F32),
            pltpu.VMEM((groups * 16, LO), F32),
        ],
        compiler_params=pltpu.CompilerParams(vmem_limit_bytes=48 * 1024 * 1024),
        name="bin_points",
    )(feats, tiles, cells, valid)


def unpack_point_in(par_ref, win):
    lanes = lane_iota()
    flat = par_ref[0:6, :]
    turned = pltpu.roll(flat, H1, axis=1)
    even = jnp.where(lanes < H1, flat, turned)
    odd = jnp.where(lanes < H1, turned, flat)
    rows = []
    for k in range(C_IN):
        src = even if k % 2 == 0 else odd
        rows.append(src[k // 2 : k // 2 + 1])
    rows.append(jnp.zeros((5, D), F32))
    win[:, :D] = jnp.concatenate(rows, axis=0).astype(BF16)
    at = lax.broadcasted_iota(jnp.int32, (16, D), 0)
    win[:, D : 2 * D] = one_hot(at == 12)
    win[:, 2 * D :] = one_hot((at == 13) | (at == 14))
    return odd[5:6]


def list_chunks(held_ref, todo, sources, chunk, most):
    def source(s, n):
        def put(j, n):
            todo[n] = s * most + j
            return n + 1

        return lax.fori_loop(0, (held_ref[s] + chunk - 1) // chunk, put, n)

    todo[0] = 0
    return lax.fori_loop(0, sources, source, 0)


def two_stage(count, todo, most, prepare, finish, even, odd):
    def ready(i, buffers):
        item = todo[jnp.minimum(i, jnp.maximum(count - 1, 0))]
        prepare(item // most, item % most, jnp.where(i < count, 1.0, 0.0), buffers)

    def pair(k, _):
        ready(2 * k + 1, odd)
        finish(even)
        ready(2 * k + 2, even)
        finish(odd)
        return 0

    ready(0, even)
    lax.fori_loop(0, (count + 1) // 2, pair, 0)


def encode_points(recv, held, par, base_rows, quads_x, quads_y):
    sources, _, capacity = recv.shape
    chunk = min(CHUNK, capacity)
    quads = quads_x * quads_y
    groups = -(-quads * QP // LO)
    pairs = -(-groups // 2)

    most = capacity // chunk

    def kernel(held_ref, recv_ref, par_ref, base_ref, out_ref, tag_ref, col_ref, *refs):
        win, acc, todo, *buffers = refs
        bias = unpack_point_in(par_ref, win)
        acc[...] = jnp.zeros(acc.shape, F32)
        lanes = lane_iota()
        own = jnp.where(lanes < H1, 1.0, 2.0)
        count_of = (lanes + 1).astype(F32)
        span = lax.broadcasted_iota(jnp.int32, (LO, chunk), 0)

        def prepare(s, j, real, into):
            place, spread = into
            cols = recv_ref[s, :, pl.ds(pl.multiple_of(j * chunk, chunk), chunk)]
            wide = cols.astype(F32)
            place[...] = one_hot(span == (wide[13:14] + wide[14:15]).astype(jnp.int32))
            both = mm_tn(cols, win[:, : 2 * D])
            act = gelu_only(both[:, :D] + bias)
            group = both[:, D:] * real
            for g in range(pairs):
                spread[:, g * D : g * D + D] = jnp.where(group == own + 2.0 * g, act, 0.0).astype(
                    BF16
                )
            spread[:, pairs * D :] = one_hot(group == count_of)

        def finish_chunk(held):
            acc[...] += mm(held[0][...], held[1][...])

        count = list_chunks(held_ref, todo, sources, chunk, most)
        two_stage(count, todo, most, prepare, finish_chunk, buffers[:2], buffers[2:])
        for g in range(groups):
            rows = min(LO, quads * QP - g * LO)
            v = acc[:rows, g // 2 * D : g // 2 * D + D]
            if g % 2 == 1:
                v = pltpu.roll(v, H1, axis=1)
            count = acc[:rows, pairs * D + g : pairs * D + g + 1]
            v = jnp.where(lanes < H1, v, jnp.where(lanes == H1, count, 0.0))
            out_ref[g * LO : g * LO + rows, :] = v + base_ref[g * LO : g * LO + rows, :]

        def finish(i, _):
            total = out_ref[pl.ds(pl.multiple_of(i * QP, 8), QP), :]
            count = total[:, H1 : H1 + 1]
            tag = jnp.where((lanes > H1) & (lanes < H1 + 4) & (count > 0.0), total, 0.0)
            tag_ref[i] = tag[:QC, :].astype(BF16)
            return 0

        lax.fori_loop(0, quads, finish, 0, unroll=4)
        for i in range(quads_x):
            col_ref[i] = tag_ref[i * quads_y]

    shape = jax.ShapeDtypeStruct
    return pl.pallas_call(
        kernel,
        in_specs=[pl.BlockSpec(memory_space=pltpu.SMEM)]
        + [pl.BlockSpec(memory_space=pltpu.VMEM)] * 3,
        out_shape=[
            shape((quads * QP, D), F32),
            shape((quads, QC, D), BF16),
            shape((quads_x, QC, D), BF16),
        ],
        scratch_shapes=[pltpu.VMEM((16, 3 * D), BF16), pltpu.VMEM((LO, (pairs + 1) * D), F32)]
        + [pltpu.SMEM((sources * most + 1,), jnp.int32)]
        + [pltpu.VMEM((LO, chunk), BF16), pltpu.VMEM((chunk, (pairs + 1) * D), BF16)] * 2,
        compiler_params=pltpu.CompilerParams(vmem_limit_bytes=56 * 1024 * 1024),
        name="encode_points",
    )(held, recv, par, base_rows)


def points_back(recv, held, par, cell_grads):
    sources, _, capacity = recv.shape
    chunk = min(CHUNK, capacity)
    total_rows = cell_grads.shape[0]
    groups = -(-total_rows // LO)
    pairs = -(-groups // 2)

    most = capacity // chunk

    def kernel(
        held_ref, recv_ref, par_ref, grad_ref, out_ref, win, table, acc, todo, *buffers
    ):
        bias = unpack_point_in(par_ref, win)
        lanes = lane_iota()

        def rows_of(g):
            rows = max(0, min(LO, total_rows - g * LO))
            got = [grad_ref[g * LO : g * LO + rows, :]] if rows else []
            return jnp.concatenate(got + [jnp.zeros((LO - rows, D), F32)], axis=0) if rows < LO else got[0]

        for j in range(pairs):
            table[:, j * D : j * D + D] = jnp.where(
                lanes < H1, rows_of(2 * j), rows_of(2 * j + 1)
            ).astype(BF16)
        acc[...] = jnp.zeros((16, D), F32)
        own = jnp.where(lanes < H1, 1.0, 2.0)
        spot = lanes.astype(F32)

        def prepare(s, j, real, into):
            place, group, slope, kept = into
            cols = recv_ref[s, :, pl.ds(pl.multiple_of(j * chunk, chunk), chunk)]
            made = mm_tn(cols, win[...])
            kept[...] = cols
            group[...] = made[:, D : 2 * D] * real
            for k in range(LO // D):
                place[:, k * D : k * D + D] = one_hot(made[:, 2 * D :] == spot + k * D)
            slope[...] = gelu_parts(made[:, :D] + bias)[1]

        def finish_chunk(held):
            place, group, slope, kept = held
            got = jnp.zeros((chunk, D), F32)
            for p in range(0, pairs, 2):
                both = mm(place[...], table[:, p * D : min(p + 2, pairs) * D])
                for u in range(both.shape[1] // D):
                    got = jnp.where(
                        group[...] == own + 2.0 * (p + u), both[:, u * D : u * D + D], got
                    )
            acc[...] += mm(kept[...], (got * slope[...]).astype(BF16))

        count = list_chunks(held_ref, todo, sources, chunk, most)
        two_stage(count, todo, most, prepare, finish_chunk, buffers[:4], buffers[4:])
        both = acc[...] + pltpu.roll(acc[...], H1, axis=1)
        rows = [
            jnp.where(lanes < H1, both[2 * k : 2 * k + 1, :], both[2 * k + 1 : 2 * k + 2, :])
            for k in range(6)
        ]
        out_ref[...] = jnp.concatenate(rows + [jnp.zeros((2, D), F32)], axis=0)

    return pl.pallas_call(
        kernel,
        in_specs=[pl.BlockSpec(memory_space=pltpu.SMEM)]
        + [pl.BlockSpec(memory_space=pltpu.VMEM)] * 3,
        out_shape=jax.ShapeDtypeStruct((8, D), F32),
        scratch_shapes=[
            pltpu.VMEM((16, 3 * D), BF16),
            pltpu.VMEM((LO, pairs * D), BF16),
            pltpu.VMEM((16, D), F32),
            pltpu.SMEM((sources * most + 1,), jnp.int32),
        ]
        + [
            pltpu.VMEM((chunk, LO), BF16),
            pltpu.VMEM((chunk, D), F32),
            pltpu.VMEM((chunk, D), F32),
            pltpu.VMEM((16, chunk), BF16),
        ]
        * 2,
        compiler_params=pltpu.CompilerParams(vmem_limit_bytes=48 * 1024 * 1024),
        cost_estimate=cost_of(recv.size * 100000),
        name="points_back",
    )(held, recv, par, cell_grads)


def update(shares, params, first_moment, second_moment):
    rows = params.shape[0]
    count = shares.shape[0]
    share = (shares.shape[1] - 16) // 2
    moves = [
        (1, GRAD_ROWS, 6, 65),
        (1, 0, POINT_ROWS, LAYER_ROWS),
        (0, 0, POINT_ROWS + LAYER_ROWS, LAYER_ROWS),
    ]

    def kernel(got, par, mom1, mom2, norm_ref, new_par, new1, new2, low, rms, two, one, grad):
        def unpack(s, point):
            v = got[s].astype(F32)
            at = pl.multiple_of(s * share, 8)
            two[pl.ds(at, share), :] = v[:share]
            one[pl.ds(at, share), :] = v[share : 2 * share]
            return point + v[2 * share : 2 * share + 8]

        grad[0:8, :] = lax.fori_loop(0, count, unpack, jnp.zeros((8, D), F32), unroll=4)
        for which, src, dst, length in moves:
            grad[pl.ds(dst, length), :] = (two, one)[which][pl.ds(src, length), :]
        g = grad[...]
        norm = jnp.sqrt(jnp.sum(g * g))
        norm_ref[0, 0] = norm
        factor = jnp.minimum(1.0, clip_norm / (norm + 1e-06))
        clipped = g * factor
        first = beta_one * mom1[...] + (1.0 - beta_one) * clipped
        second = beta_two * mom2[...] + (1.0 - beta_two) * clipped * clipped
        new1[...] = first
        new2[...] = second
        first_hat = first / (1.0 - beta_one**step_count)
        second_hat = second / (1.0 - beta_two**step_count)
        p = par[...]
        p = p - learn_rate * (first_hat / (jnp.sqrt(second_hat) + adam_eps) + decay_rate * p)
        new_par[...] = p
        low[...] = p.astype(BF16)
        stats = jnp.concatenate(
            [one[LAYER_ROWS : LAYER_ROWS + 3, :], two[LAYER_ROWS : LAYER_ROWS + 5, :]], axis=0
        )
        live = jnp.sum(one[LAYER_ROWS + 3 : LAYER_ROWS + 4, :], axis=1, keepdims=True)
        sums = jnp.sum(stats, axis=1, keepdims=True)
        rms[...] = jnp.broadcast_to(jnp.sqrt(sums / jnp.maximum(live, D)), (8, D))

    shape = jax.ShapeDtypeStruct
    flat = shape((rows, D), F32)
    return pl.pallas_call(
        kernel,
        out_specs=[pl.BlockSpec(memory_space=pltpu.SMEM)]
        + [pl.BlockSpec(memory_space=pltpu.VMEM)] * 5,
        out_shape=[shape((1, 1), F32), flat, flat, flat, shape((rows, D), BF16), shape((8, D), F32)],
        scratch_shapes=[pltpu.VMEM((count * share, D), F32)] * 2 + [pltpu.VMEM((rows, D), F32)],
        compiler_params=pltpu.CompilerParams(vmem_limit_bytes=48 * 1024 * 1024),
        name="update",
    )(shares, params, first_moment, second_moment)


def shifted(x, axes, by):
    if len(axes) == 1:
        count = lax.axis_size(axes[0])
        return lax.ppermute(x, axes[0], [(i, (i + by) % count) for i in range(count)])
    tiles, rows = lax.axis_size(axes[0]), lax.axis_size(axes[1])
    pairs = [
        (i * rows + j, (i + by) % tiles * rows + (j + by) % rows)
        for i in range(tiles)
        for j in range(rows)
    ]
    return lax.ppermute(x, axes, pairs)


def exchange(row, col, cor, by):
    return (
        shifted(row, ("tile",), by),
        shifted(col, ("row",), by),
        shifted(cor, ("tile", "row"), by),
    )


def by_quads(grid, quads_x, quads_y):
    trailing = grid.shape[2:]
    grid = grid.reshape((quads_x, QS, quads_y, QS) + trailing)
    return jnp.swapaxes(grid, 1, 2).reshape((quads_x, quads_y, QC) + trailing)


def all_to_all(x):
    return lax.all_to_all(x, ("tile", "row"), split_axis=0, concat_axis=0, tiled=True)


def scatter_sum(x, count):
    return jnp.sum(all_to_all(x.reshape(count, x.shape[0] // count, D)), axis=0)


def local(
    point_feats,
    point_tile,
    point_cell,
    point_valid,
    pillar_frame,
    cotangent,
    params,
    first_moment,
    second_moment,
):
    tile_count = lax.axis_size("tile")
    row_count = lax.axis_size("row")
    device_count = tile_count * row_count
    extent_x, extent_y = pillar_frame.shape
    cell_count = extent_x * extent_y
    quads_x, quads_y = extent_x // QS, extent_y // QS
    quads = quads_x * quads_y
    points = point_cell.shape[0]
    capacity = 2 * points // tile_count
    par = params.reshape(-1, D)

    cot = by_quads(cotangent, quads_x, quads_y)

    shape = (points // BLOCK, BLOCK)
    send = bin_points(
        point_feats,
        point_tile.reshape(shape),
        point_cell.reshape(shape),
        point_valid.reshape(shape),
        tile_count,
        capacity,
        extent_y,
        quads_y,
    )
    recv = lax.all_to_all(send, "tile", split_axis=0, concat_axis=0, tiled=True)
    held = jnp.sum(recv[:, 11].astype(jnp.int32), axis=1)

    frames = by_quads(pillar_frame, quads_x, quads_y)
    frames = jnp.pad(frames, ((0, 0), (0, 0), (0, QP - QC)), constant_values=-1).reshape(-1)
    lanes = jnp.arange(D, dtype=jnp.int32)
    base_rows = (frames[:, None] == lanes[None] - (H1 + 1)).astype(F32)
    pillars, tags, tag_col = encode_points(recv, held, par[:72], base_rows, quads_x, quads_y)
    pillars = pillars.reshape(quads_x, quads_y, QP, D)
    tags = tags.reshape(quads_x, quads_y, QC, D)

    def edges(cells, groups):
        gap = jnp.zeros(cells.shape[:-2] + (QP - QC, D), BF16)
        return jnp.concatenate([cells, gap, groups], axis=1)

    early_halos = exchange(
        edges(cot[0], tags[0]), edges(cot[:, 0], tag_col), edges(cot[0, :1], tags[0, :1]), -1
    )

    first = first_layer(pillars, par, quads_x, quads_y)
    field, saved, sums_one = first[0], first[1:8], first[8]
    early_halos, sides = lax.optimization_barrier((early_halos, first[9:]))
    halos = exchange(*sides, -1)
    flags = jnp.stack(
        [
            (lax.axis_index("tile") == tile_count - 1).astype(jnp.int32),
            (lax.axis_index("row") == row_count - 1).astype(jnp.int32),
        ]
    )
    step = device_count * 8
    grad_rows = -(-(GRAD_ROWS + 72) // step) * step
    grads, grad_two, g_row, g_col, g_cor = second_layer(
        flags,
        field,
        halos,
        tags,
        cot,
        early_halos,
        par,
        1.0 / (cell_count * device_count),
        grad_rows,
    )
    grad_two, grad_halos = lax.optimization_barrier((grad_two, exchange(g_row, g_col, g_cor, 1)))
    sum_two = scatter_sum(grad_two, device_count)
    cell_grads, grad_one = first_layer_back(
        grads, grad_halos, pillars, saved, sums_one, par, grad_rows
    )
    grad_one, sum_two = lax.optimization_barrier((grad_one, sum_two))
    sum_one = scatter_sum(grad_one, device_count)
    grad_pin = points_back(recv, held, par[:72], cell_grads.reshape(quads * QP, D))
    share = jnp.concatenate([sum_two, sum_one, grad_pin, jnp.zeros((8, D), F32)], axis=0)
    share = share.astype(BF16)
    total = all_to_all(jnp.broadcast_to(share[None], (device_count,) + share.shape))
    norm, new_params, new_first, new_second, low, rms = update(
        total, par, first_moment.reshape(-1, D), second_moment.reshape(-1, D)
    )
    return (
        norm[0, 0],
        new_params.reshape(-1),
        new_first.reshape(-1),
        new_second.reshape(-1),
        low.reshape(-1),
        rms[:6, 0],
    )


def solution(mesh):
    return jax.shard_map(
        local,
        mesh=mesh,
        in_specs=(
            P(None, ("tile", "row")),
            P(("tile", "row"), None),
            P(("tile", "row")),
            P(("tile", "row")),
            P("tile", "row"),
            P("tile", "row", None),
            P(),
            P(),
            P(),
        ),
        out_specs=(P(), P(), P(), P(), P(), P()),
        check_vma=False,
    )
```
